32 devices in a mesh: grp: 4 (over y, x), tile: 8 (over z, core).
Axes of the slice: x: 2, y: 2, z: 4, core: 2. Of those that a mesh axis runs over, the one named last changes fastest.
Arguments:
- observed: bfloat16 [512, 32, 2048], P('tile', 'grp'), as said below
- visible: int32 [32, 2048], P('grp', 'tile'), may hold values from 0 to 65535
- params_start: float32 [8, 32, 2048], P(None, 'grp', 'tile'), may hold values from -1.5 to 1.5, as said below
- light_directions: float32 [3, 32], replicated, may hold values from -1 to 1
- view_dirs: float32 [3, 16], replicated, may hold values from -1 to 1
- gains_start: float32 [32], replicated, may hold values from 0.5 to 1.5
Outputs:
- params_out: float32 [8, 32, 2048], P(None, 'grp', 'tile')
- gains_out: float32 [32], replicated
The draws below stay inside these ranges and needn't reach their ends.
Inputs may be any that keep to these rules, and one draw needn't show every extreme that they name: `observed`: luminance is positive. `params_start`: tilts within -0.3 to 0.3, diffuse 0.3 to 1.2, specular 0.1 to 0.8, sharpness logit -1.5 to 1.5, ambient -0.2 to 0.3, rim 0 to 0.5, retro -0.3 to 0.3.
All inputs are finite; a program needn't handle non-finite values.
Results may differ from the reference program's by a relative error of at most 0.0003.
Values may be sent and summed in bfloat16 or wider, within the bound.
No kernel may reach another device: no remote copies, remote signals or barrier semaphores. Data moves between devices by JAX's collectives and lax.ppermute only.
A program may use at most 64 MiB of HBM per device.

```python
import jax
import jax.numpy as jnp
from jax import lax

CAMS = 16
LIGHTS = 32
ITERS = 2
TEXEL_SAMPLES = 512
TEXEL_ROWS = 32
TEXEL_COLUMNS = 2048


def draw_observed(key, part):
    first_entry = jax.random.fold_in(key, 11)
    rows = jnp.arange(TEXEL_ROWS, dtype=jnp.float32)[None, :, None] / max(TEXEL_ROWS - 1, 1)
    cols = jnp.arange(TEXEL_COLUMNS, dtype=jnp.float32)[None, None, :] / max(TEXEL_COLUMNS - 1, 1)
    base_value = jax.random.uniform(first_entry, (TEXEL_SAMPLES, TEXEL_ROWS, TEXEL_COLUMNS), jnp.float32, 0.2, 1.4)
    ramp = jnp.exp(jnp.log(3.0) * (cols + rows))
    return (0.5 * base_value * ramp).astype(jnp.bfloat16)


def draw_params_start(key, part):
    lows = [-0.3, -0.3, 0.3, 0.1, -1.5, -0.2, 0.0, -0.3]
    highs = [0.3, 0.3, 1.2, 0.8, 1.5, 0.3, 0.5, 0.3]
    fields = []
    for i in range(8):
        sub = jax.random.fold_in(key, 100 + i)
        fields.append(jax.random.uniform(sub, (TEXEL_ROWS, TEXEL_COLUMNS), jnp.float32, lows[i], highs[i]))
    return jnp.stack(fields)


def place_ends(values, rng, least, high):
    shape = values.shape
    index_at = [jax.random.randint(jax.random.fold_in(rng, axis), (), 0, shape[axis]) for axis in range(len(shape))]
    values = values.at[tuple(index_at)].set(least)
    longest = shape.index(max(shape))
    index_at[longest] = (index_at[longest] + 1) % shape[longest]
    return values.at[tuple(index_at)].set(high)


def setup_inputs(seed: int = 0) -> dict:
    streams_of = jax.random.split(jax.random.key(seed), 7)
    return {
        "observed": draw_observed(jax.random.fold_in(streams_of[6], 71), 0),
        "visible": place_ends(jax.random.randint(streams_of[1], (TEXEL_ROWS, TEXEL_COLUMNS), 0, 2 ** CAMS), jax.random.fold_in(streams_of[1], 1), 0, (2 ** CAMS) - 1).astype(jnp.int32),
        "params_start": draw_params_start(jax.random.fold_in(streams_of[6], 71), 0),
        "light_directions": jnp.clip(jax.random.uniform(streams_of[3], (3, LIGHTS), jnp.float32, -1.0, 1.0), -1.0, 1.0),
        "view_dirs": jnp.clip(jax.random.uniform(streams_of[4], (3, CAMS), jnp.float32, -1.0, 1.0), -1.0, 1.0),
        "gains_start": jnp.clip(1.0 + 0.1 * jax.random.normal(streams_of[5], (LIGHTS,), jnp.float32), 0.5, 1.5),
    }


damping = 4.0
lift_z = 1.6

def unit_columns(raw):
    lifted = raw + jnp.array([0.0, 0.0, lift_z], jnp.float32)[:, None]
    return lifted / jnp.sqrt(lax.optimization_barrier(jnp.sum(lifted * lifted, axis=0, keepdims=True)))

def geometry(light_directions, view_dirs):
    lights = unit_columns(light_directions)
    views = unit_columns(view_dirs)
    raw_half = views.T[:, :, None] + lights[None]
    halves = raw_half / jnp.sqrt(lax.optimization_barrier(jnp.sum(raw_half * raw_half, axis=1, keepdims=True)))
    echoes = lax.optimization_barrier(jnp.sum(views.T[:, :, None] * lights[None], axis=1))
    return (lights, halves, views.T, echoes)

def facing(dir_x, dir_y, dir_z, tilt_u, tilt_v, scale_q):
    facing_dot = (dir_x * tilt_u + dir_y * tilt_v + dir_z) * scale_q
    by_u = (dir_x - facing_dot * tilt_u * scale_q) * scale_q
    by_v = (dir_y - facing_dot * tilt_v * scale_q) * scale_q
    return (facing_dot, by_u, by_v)

def camera_terms(observed_c, weight_c, params, gains, lights, half_c, view_c, echo_c):
    tilt_u, tilt_v, diffuse, specular, sharp_raw, ambient, rim_gain, retro_gain = [params[i] for i in range(8)]
    scale_q = 1.0 / jnp.sqrt(1.0 + tilt_u * tilt_u + tilt_v * tilt_v)
    light_dot, light_u, light_v = facing(lights[0][:, None], lights[1][:, None], lights[2][:, None], tilt_u, tilt_v, scale_q)
    half_dot, half_u, half_v = facing(half_c[0][:, None], half_c[1][:, None], half_c[2][:, None], tilt_u, tilt_v, scale_q)
    view_dot, view_u, view_v = facing(view_c[0], view_c[1], view_c[2], tilt_u, tilt_v, scale_q)
    sigma = jax.nn.sigmoid(sharp_raw)
    sharp = 1.0 + 20.0 * sigma
    lobe = jnp.exp(sharp * (half_dot - 1.0))
    back = 1.0 - view_dot
    rim_shape = back * back
    shaped = diffuse * light_dot + specular * lobe + ambient + rim_gain * rim_shape + retro_gain * echo_c[:, None]
    full = light_dot.shape
    jacob = [diffuse * light_u + specular * sharp * lobe * half_u - 2.0 * rim_gain * back * view_u, diffuse * light_v + specular * sharp * lobe * half_v - 2.0 * rim_gain * back * view_v, light_dot, lobe, specular * lobe * (half_dot - 1.0) * 20.0 * sigma * (1.0 - sigma), jnp.ones(full, jnp.float32), jnp.broadcast_to(rim_shape, full), jnp.broadcast_to(echo_c[:, None], full)]
    column = gains[:, None]
    resid = observed_c.astype(jnp.float32) - column * shaped
    scaled = [column * piece for piece in jacob]
    surface_normal = []
    for i in range(8):
        for j in range(i, 8):
            surface_normal.append(weight_c * lax.optimization_barrier(jnp.sum(scaled[i] * scaled[j], axis=0)))
    right_side = [weight_c * lax.optimization_barrier(jnp.sum(piece * resid, axis=0)) for piece in scaled]
    lifted = lax.optimization_barrier(jnp.sum(weight_c * shaped * resid, axis=1))
    energy = lax.optimization_barrier(jnp.sum(weight_c * shaped * shaped, axis=1))
    return (jnp.stack(surface_normal), jnp.stack(right_side), lifted, energy)

def assemble(observed, weights, params, gains, lights, halves, views, echoes):
    texels = params.shape[1]

    def one_camera(carry, inputs):
        observed_c, weight_c, half_c, view_c, echo_c = inputs
        terms = camera_terms(observed_c, weight_c, params, gains, lights, half_c, view_c, echo_c)
        return (tuple((a + b for a, b in zip(carry, terms))), None)
    start = (jnp.zeros((36, texels), jnp.float32), jnp.zeros((8, texels), jnp.float32), jnp.zeros((LIGHTS,), jnp.float32), jnp.zeros((LIGHTS,), jnp.float32))
    result, unused = lax.scan(one_camera, start, (observed, weights, halves, views, echoes))
    return result

def solve_eight(surface_normal, right_side):
    entries = {}
    where = 0
    for i in range(8):
        for j in range(i, 8):
            entries[i, j] = surface_normal[where]
            where += 1
    lower = {}
    for j in range(8):
        accum = entries[j, j] + damping
        for k in range(j):
            accum = accum - lower[j, k] * lower[j, k]
        root = jnp.sqrt(accum)
        lower[j, j] = root
        for i in range(j + 1, 8):
            accum = entries[j, i]
            for k in range(j):
                accum = accum - lower[i, k] * lower[j, k]
            lower[i, j] = accum / root
    forward = []
    for i in range(8):
        accum = right_side[i]
        for k in range(i):
            accum = accum - lower[i, k] * forward[k]
        forward.append(accum / lower[i, i])
    answer = [None] * 8
    for i in range(7, -1, -1):
        accum = forward[i]
        for k in range(i + 1, 8):
            accum = accum - lower[k, i] * answer[k]
        answer[i] = accum / lower[i, i]
    return jnp.stack(answer)

def smooth_tilts(tilt):
    padded = jnp.pad(tilt, ((0, 0), (1, 1), (1, 1)))
    rows = tilt.shape[1]
    cols = tilt.shape[2]
    boxed = jnp.zeros(tilt.shape, jnp.float32)
    for i in range(3):
        for j in range(3):
            boxed = boxed + padded[:, i:i + rows, j:j + cols]
    return 0.5 * tilt + boxed * (0.5 / 9.0)

def reference(observed, visible, params_start, light_directions, view_dirs, gains_start):
    lights, halves, views, echoes = geometry(light_directions, view_dirs)
    rows = visible.shape[0]
    cols = visible.shape[1]
    flat_obs = observed.reshape(CAMS, LIGHTS, rows * cols)
    shifts = jnp.arange(CAMS, dtype=jnp.int32)
    weights = jnp.bitwise_and(jnp.right_shift(visible.reshape(1, -1), shifts[:, None]), 1).astype(jnp.float32)
    params = params_start.reshape(8, -1)
    gains = gains_start
    for iteration in range(ITERS):
        surface_normal, right_side, lifted, energy = assemble(flat_obs, weights, params, gains, lights, halves, views, echoes)
        params = params + solve_eight(surface_normal, right_side)
        gains = gains + lifted / (energy + 1.0)
        grid = params.reshape(8, rows, cols)
        params = jnp.concatenate([smooth_tilts(grid[:2]), grid[2:]], axis=0).reshape(8, -1)
    return (params.reshape(8, rows, cols), gains)
```

```python
import functools

import jax
import jax.numpy as jnp
from jax import lax
from jax.experimental import pallas as pl
from jax.experimental.pallas import tpu as pltpu
from jax.sharding import PartitionSpec as P

CAMS = 16
LIGHTS = 32
ITERS = 2

damping = 4.0
lift_z = 1.6
hidden = 1024.0
f32 = jnp.float32
bf16 = jnp.bfloat16
LANES = 128
VMEM_BYTES = 40 * 1024 * 1024
LINEAR = (2, 3, 5, 6, 7)
ENTRIES = [(i, j) for i in range(8) for j in range(i, 8)]


def unit_columns(raw):
    lifted = raw + jnp.array([0.0, 0.0, lift_z], f32)[:, None]
    return lifted / jnp.sqrt(jnp.sum(lifted * lifted, axis=0, keepdims=True))


def geometry(light_directions, view_dirs):
    lights = unit_columns(light_directions)
    views = unit_columns(view_dirs)
    raw_half = views[:, :, None] + lights[:, None, :]
    halves = raw_half / jnp.sqrt(jnp.sum(raw_half * raw_half, axis=0, keepdims=True))
    echoes = jnp.sum(views[:, :, None] * lights[:, None, :], axis=0)
    return lights, views, halves.reshape(3, -1), echoes.reshape(1, -1)


def thirds(x):
    first = lax.reduce_precision(x, 8, 7)
    rest = x - first
    second = lax.reduce_precision(rest, 8, 7)
    return first, second, rest - second


def split_value(x, count):
    pieces = []
    for _ in range(count - 1):
        head = x.astype(bf16).astype(f32)
        pieces.append(head)
        x = x - head
    pieces.append(x)
    return pieces


def split_pair(x):
    head = x.astype(bf16)
    return head, (x - head.astype(f32)).astype(bf16)


def dot(a, b):
    return jnp.dot(a, b, preferred_element_type=f32)


def total(terms):
    terms = list(terms)
    out = terms[0]
    for t in terms[1:]:
        out = out + t
    return out


def inner(a, b):
    return total(x * y for x, y in zip(a, b))


def texel_forms(p):
    tu, tv, diffuse, spec, raw, ambient, rim, retro = p
    q = 1.0 / jnp.sqrt(1.0 + tu * tu + tv * tv)
    nx, ny, nz = tu * q, tv * q, q
    side = -(nx * ny) * q
    by_u = ((1.0 - nx * nx) * q, side, -(nz * nx) * q)
    by_v = (side, (1.0 - ny * ny) * q, -(nz * ny) * q)
    sigma = 1.0 / (1.0 + jnp.exp(-raw))
    sharp = 1.0 + 20.0 * sigma
    slope = 20.0 * sigma * (1.0 - sigma)
    return (nx, ny, nz), by_u, by_v, sharp, slope


def seen(mask, c):
    return jnp.bitwise_and(jnp.right_shift(mask, c), 1).astype(f32)


def put_slab(ref, k, value):
    rows, cols = value.shape
    for h in range(cols // LANES):
        ref[h, k * rows : (k + 1) * rows, :] = value[:, h * LANES : (h + 1) * LANES]


def get_slab(ref, k, rows):
    return jnp.concatenate([ref[h, k * rows : (k + 1) * rows, :] for h in range(ref.shape[0])], axis=1)


def get_rows(ref, start, count, stride):
    return jnp.concatenate([ref[h, pl.ds(start, count, stride=stride), :] for h in range(ref.shape[0])], axis=1)


def put_rows(ref, start, stride, value):
    count, cols = value.shape
    for h in range(cols // LANES):
        ref[h, pl.ds(start, count, stride=stride), :] = value[:, h * LANES : (h + 1) * LANES]


def put_lobe_rows(slab, normal, sharp):
    base = [sharp * normal[0], sharp * normal[1], sharp * normal[2], -sharp]
    parts = [split_value(x, 3) for x in base]
    row = 0
    for which in (0, 1, 0, 2, 1, 0):
        for part in parts:
            slab(row, part[which])
            row += 1
    return row


def normal_kernel(
    cam_ref, par_ref, vis_ref, gain_ref, lobe_ref, mixed_ref, square_ref, out_ref,
    rows_ref, sums_ref, mixed_scr, square_scr,
):
    rows, cols = par_ref.shape[1], par_ref.shape[2]
    depth = lobe_ref.shape[1]
    chunk = 4 * LIGHTS
    chunks = CAMS // 4

    gain2 = gain_ref[...] * gain_ref[...]
    for src, dst in ((mixed_ref, mixed_scr), (square_ref, square_scr)):
        head, tail = split_pair(src[...] * gain2)
        count = src.shape[0]
        dst[0:count, :] = head
        dst[count : 2 * count, :] = tail

    def slab(k, value):
        put_slab(rows_ref, k, value)

    p = [par_ref[i] for i in range(8)]
    normal, _, _, sharp, _ = texel_forms(p)
    used = put_lobe_rows(slab, normal, sharp)
    mask = vis_ref[...]
    for c in range(CAMS):
        slab(used + c, (seen(mask, c) - 1.0) * hidden)
    for k in range(used + CAMS, depth):
        slab(k, jnp.zeros((rows, cols), f32))

    def one_row(r, carry):
        texel = get_rows(rows_ref, r, depth, rows).astype(bf16)
        mixed = jnp.zeros((16, cols), f32)
        square = jnp.zeros((16, cols), f32)
        for ch in range(chunks):
            at = slice(ch * chunk, (ch + 1) * chunk)
            lobe = jnp.exp(dot(lobe_ref[at, :], texel))
            head, tail = split_pair(lobe)
            both = dot(mixed_scr[:, at], head)
            got = both[0:32] + both[32:64] + dot(mixed_scr[0:32, at], tail)
            mixed = mixed + got[0:16]
            put_rows(sums_ref, (32 + 16 * ch) * rows + r, rows, got[16:32])
            head, tail = split_pair(lobe * lobe)
            both = dot(square_scr[:, at], head)
            square = square + both[0:16] + both[16:32] + dot(square_scr[0:16, at], tail)
        put_rows(sums_ref, r, rows, mixed)
        put_rows(sums_ref, 16 * rows + r, rows, square)
        return carry

    lax.fori_loop(0, rows, one_row, 0)

    def one_part(h, carry):
        at = pl.ds(pl.multiple_of(h * LANES, LANES), LANES)

        def sums(k):
            return sums_ref[h, k * rows : (k + 1) * rows, :]

        p = [par_ref[i, :, at] for i in range(8)]
        mask = vis_ref[:, at]
        normal, by_u, by_v, sharp, slope = texel_forms(p)
        diffuse, spec, rim = p[2], p[3], p[6]
        zero = jnp.zeros((rows, LANES), f32)
        gam = {i: zero for i in (0, 1, 5, 6)}
        own = {(i, j): zero for i in (0, 1, 5, 6) for j in (0, 1, 5, 6) if i <= j and j != 5 and i != 5}
        lit = {i: zero for i in (0, 1, 5, 6)}
        grid = {(i, k): zero for i in (0, 1, 5, 6) for k in range(4)}
        echo_sq = zero
        view_sum = [zero, zero, zero]
        for c in range(CAMS):
            w = seen(mask, c)
            v = [cam_ref[i, c] for i in range(3)]
            back = 1.0 - inner(v, normal)
            turn = (-2.0 * rim) * back
            shape = {0: turn * inner(v, by_u), 1: turn * inner(v, by_v), 6: back * back}
            weighted = {i: w * shape[i] for i in shape}
            weighted[5] = w
            for i in gam:
                gam[i] = gam[i] + weighted[i]
                lit[i] = lit[i] + weighted[i] * cam_ref[4, c]
            for i, j in own:
                own[i, j] = own[i, j] + weighted[i] * shape[j]
            echo_sq = echo_sq + w * cam_ref[3, c]
            view_sum = [s + w * x for s, x in zip(view_sum, v)]
            for k in range(4):
                peak = sums(32 + 4 * c + k)
                for i in (0, 1, 6):
                    grid[i, k] = grid[i, k] + shape[i] * peak
                grid[5, k] = grid[5, k] + peak
        own[5, 5] = gam[5]
        for i in (0, 1):
            own[i, 5] = gam[i]
        own[5, 6] = gam[6]

        def gram(i, j):
            return cam_ref[5, 4 * i + j]

        entries = {ij: None for ij in ENTRIES}

        def add(i, j, value):
            ij = (min(i, j), max(i, j))
            entries[ij] = value if entries[ij] is None else entries[ij] + value

        def cross(i, j, value):
            add(i, j, value + value if i == j else value)

        flat = {0: [diffuse * x for x in by_u], 1: [diffuse * x for x in by_v], 2: list(normal)}
        edge = spec * sharp
        tilt = spec * slope
        glow = {
            0: {1 + k: edge * by_u[k] for k in range(3)},
            1: {1 + k: edge * by_v[k] for k in range(3)},
            3: {0: None},
            4: {0: -tilt, 1: tilt * normal[0], 2: tilt * normal[1], 3: tilt * normal[2]},
        }

        def combine(coefs, values):
            return total(values[k] if x is None else x * values[k] for k, x in coefs.items())

        count = gam[5]
        spread = {i: [total(gram(r, k) * flat[i][k] for k in range(3)) for r in range(3)] for i in flat}
        reach = {i: total(gram(3, k) * flat[i][k] for k in range(3)) for i in flat}
        view_spread = [total(gram(r, k) * view_sum[k] for k in range(3)) for r in range(3)]
        for i in flat:
            for j in flat:
                if i <= j:
                    add(i, j, count * inner(flat[j], spread[i]))
            for j in gam:
                cross(i, j, reach[i] * gam[j])
            cross(i, 7, inner(flat[i], view_spread))
        for i, j in own:
            add(i, j, gram(3, 3) * own[i, j])
        for i in lit:
            cross(i, 7, lit[i])
        add(7, 7, echo_sq)
        for j in glow:
            for i in flat:
                cross(i, j, total(flat[i][x] * combine(glow[j], {k: sums(4 * k + x) for k in glow[j]}) for x in range(3)))
            for i in gam:
                cross(i, j, combine(glow[j], {k: grid[i, k] for k in glow[j]}))
            cross(j, 7, combine(glow[j], {k: sums(4 * k + 3) for k in glow[j]}))
        packed = {}
        where = 0
        for i in range(4):
            for j in range(i, 4):
                packed[i, j] = packed[j, i] = where
                where += 1
        for i in glow:
            for j in glow:
                if i <= j:
                    half = {k: combine(glow[j], {x: sums(16 + packed[k, x]) for x in glow[j]}) for k in glow[i]}
                    add(i, j, combine(glow[i], half))

        def entry(i, j):
            return entries[min(i, j), max(i, j)]

        for i in range(8):
            out_ref[36 + i, :, at] = total(entry(i, j) * p[j] for j in LINEAR)
        lower = {}
        for j in range(8):
            accum = entries[j, j] + damping
            for k in range(j):
                accum = accum - lower[j, k] * lower[j, k]
            inverse = lax.rsqrt(accum)
            lower[j, j] = inverse
            for i in range(j + 1, 8):
                accum = entries[j, i]
                for k in range(j):
                    accum = accum - lower[i, k] * lower[j, k]
                lower[i, j] = accum * inverse
        for where, (i, j) in enumerate(ENTRIES):
            out_ref[where, :, at] = lower[j, i]
        return carry

    lax.fori_loop(0, cols // LANES, one_part, 0)


def sample_kernel(
    place_ref, cam_ref, own_ref, got_ref, gain_ref, lobe_ref, shade_ref, plain_ref, peak_ref, *refs, parts
):
    par_refs, vis_refs = refs[:parts], refs[parts : 2 * parts]
    out_refs = refs[2 * parts : 3 * parts]
    light_ref = refs[3 * parts]
    par_scr, vis_scr, obs_scr, rows_ref, sums_ref, light_scr = refs[3 * parts + 1 :]
    step = pl.program_id(0)
    samples, rows, cols = own_ref.shape
    held = 2 * samples
    cams = held // LIGHTS
    for s in range(parts):

        @pl.when(step == s)
        def _():
            par_scr[...] = par_refs[s][0:8]
            vis_scr[...] = vis_refs[s][...]

    core = place_ref[parts]
    mine = pl.multiple_of(core * (samples * rows), rows)
    theirs = pl.multiple_of((1 - core) * (samples * rows), rows)
    for h in range(cols // LANES):
        lanes = slice(h * LANES, (h + 1) * LANES)
        for src, at in ((own_ref, mine), (got_ref, theirs)):
            obs_scr[h, pl.ds(at, samples * rows), :] = src[:, :, lanes].astype(f32).reshape(samples * rows, LANES)

    def slab(k, value):
        put_slab(rows_ref, k, value)

    p = [par_scr[i] for i in range(8)]
    mask = vis_scr[...]
    normal, by_u, by_v, sharp, slope = texel_forms(p)
    base = cam_ref[3, 0].astype(jnp.int32)
    used = put_lobe_rows(slab, normal, sharp)
    weights = [seen(mask, base + c) for c in range(cams)]
    for c in range(cams):
        slab(used + c, (weights[c] - 1.0) * hidden)
        slab(65 + c, weights[c])
    for k in range(used + cams, 32):
        slab(k, jnp.zeros((rows, cols), f32))
    shade = [p[2] * normal[0], p[2] * normal[1], p[2] * normal[2], p[5], p[7]]
    pieces = [split_value(x, 2) for x in shade]
    at = 32
    for which in (0, 1, 0):
        for piece in pieces:
            slab(at, piece[which])
            at += 1
    for c in range(cams):
        back = 1.0 - inner([cam_ref[i, c] for i in range(3)], normal)
        head, tail = split_value(p[6] * (back * back), 2)
        slab(at + c, head)
        slab(at + cams + c, tail)
    for k in range(at + 2 * cams, 64):
        slab(k, jnp.zeros((rows, cols), f32))
    slab(64, p[3])

    gains = gain_ref[...]
    plain = jnp.concatenate(split_value(plain_ref[...] * gains, 2), axis=0).astype(bf16)
    peak = jnp.concatenate(split_value(peak_ref[...] * gains, 2), axis=0).astype(bf16)
    count = plain_ref.shape[0]

    def fold(x):
        return total(x[:, k * LANES : (k + 1) * LANES] for k in range(cols // LANES))

    def one_row(r, carry):
        lift, energy = carry
        lobe = jnp.exp(dot(lobe_ref[...], get_rows(rows_ref, r, 32, rows).astype(bf16)))
        shade = dot(shade_ref[...], get_rows(rows_ref, 32 * rows + r, 32, rows).astype(bf16))
        misc = get_rows(rows_ref, 64 * rows + r, 8, rows)
        obs = get_rows(obs_scr, r, held, rows)
        for c in range(cams):
            part = slice(c * LIGHTS, (c + 1) * LIGHTS)
            full = shade[part] + misc[0:1] * lobe[part]
            kept = full * misc[1 + c : 2 + c]
            lift = lift + fold(kept * obs[part])
            energy = energy + fold(kept * full)
        head, tail = split_pair(obs * lobe)
        both = dot(plain, obs.astype(bf16))
        put_rows(sums_ref, r, rows, both[0:count] + both[count : 2 * count])
        both = dot(peak, head)
        put_rows(sums_ref, count * rows + r, rows, both[0:8] + both[8:16] + dot(peak[0:8], tail))
        return lift, energy

    zero = jnp.zeros((LIGHTS, LANES), f32)
    lift, energy = lax.fori_loop(0, rows, one_row, (zero, zero))

    @pl.when(step == 0)
    def _():
        light_scr[0:LIGHTS, :] = lift
        light_scr[LIGHTS : 2 * LIGHTS, :] = energy

    @pl.when(step != 0)
    def _():
        light_scr[0:LIGHTS, :] = light_scr[0:LIGHTS, :] + lift
        light_scr[LIGHTS : 2 * LIGHTS, :] = light_scr[LIGHTS : 2 * LIGHTS, :] + energy

    @pl.when(step == parts - 1)
    def _():
        light_ref[...] = lax.dot_general(
            jnp.ones((8, LANES), f32),
            light_scr[...],
            (((1,), (1,)), ((), ())),
            precision=lax.Precision.HIGHEST,
            preferred_element_type=f32,
        )

    def sums(k):
        return get_slab(sums_ref, k, rows)

    flat = [None, None, None]
    lone, rim_sum, echo_sum, turn_u, turn_v = None, None, None, None, None

    def grow(old, new):
        return new if old is None else old + new

    for c in range(cams):
        v = [cam_ref[i, c] for i in range(3)]
        w = weights[c]
        one = w * sums(4 * c)
        lit = [w * sums(4 * c + 1 + x) for x in range(3)]
        back = 1.0 - inner(v, normal)
        bent = back * one
        lone = grow(lone, one)
        rim_sum = grow(rim_sum, back * bent)
        turn_u = grow(turn_u, bent * inner(v, by_u))
        turn_v = grow(turn_v, bent * inner(v, by_v))
        echo_sum = grow(echo_sum, inner(v, lit))
        flat = [grow(f, x) for f, x in zip(flat, lit)]
    spot = sums(count)
    spots = [sums(count + 1 + x) for x in range(3)]
    edge = p[3] * sharp
    twice = -2.0 * p[6]
    right = [
        p[2] * inner(by_u, flat) + edge * inner(by_u, spots) + twice * turn_u,
        p[2] * inner(by_v, flat) + edge * inner(by_v, spots) + twice * turn_v,
        inner(normal, flat),
        spot,
        p[3] * slope * (inner(normal, spots) - spot),
        lone,
        rim_sum,
        echo_sum,
    ]
    for s in range(parts):

        @pl.when(step == s)
        def _():
            for i in range(8):
                out_refs[s][i] = right[i]


def solve_kernel(low_ref, par_ref, *refs):
    right_refs, out_ref = refs[:-1], refs[-1]
    lower = {}
    for where, (i, j) in enumerate(ENTRIES):
        lower[j, i] = low_ref[where]
    right = [total(ref[i] for ref in right_refs) - low_ref[36 + i] for i in range(8)]
    forward = []
    for i in range(8):
        accum = right[i]
        for k in range(i):
            accum = accum - lower[i, k] * forward[k]
        forward.append(accum * lower[i, i])
    answer = [None] * 8
    for i in range(7, -1, -1):
        accum = forward[i]
        for k in range(i + 1, 8):
            accum = accum - lower[k, i] * answer[k]
        answer[i] = accum * lower[i, i]
    for i in range(8):
        out_ref[i] = par_ref[i] + answer[i]


def smem():
    return pl.BlockSpec(memory_space=pltpu.SMEM)


def vmem():
    return pl.BlockSpec(memory_space=pltpu.VMEM)


def params_of():
    return pltpu.CompilerParams(vmem_limit_bytes=VMEM_BYTES)


def normal_call(cam_table, par, vis, gain_row, tables):
    _, rows, cols = par.shape
    depth = tables["lobe"].shape[1]
    return pl.pallas_call(
        normal_kernel,
        name="normal_factor",
        out_shape=jax.ShapeDtypeStruct((44, rows, cols), f32),
        in_specs=[smem()] + [vmem()] * 6,
        out_specs=vmem(),
        scratch_shapes=[
            pltpu.VMEM((cols // LANES, depth * rows, LANES), f32),
            pltpu.VMEM((cols // LANES, 96 * rows, LANES), f32),
            pltpu.VMEM((64, CAMS * LIGHTS), bf16),
            pltpu.VMEM((32, CAMS * LIGHTS), bf16),
        ],
        compiler_params=params_of(),
    )(cam_table, par, vis, gain_row, tables["lobe"], tables["mixed"], tables["square"])


def sample_call(place, cam_table, own, got, gain_row, tables, pars, vises):
    parts = len(pars)
    samples, rows, _ = own.shape
    cols = pars[0].shape[2]
    held = 2 * samples
    whole2 = lambda s, place: (0, 0)
    whole3 = lambda s, place: (0, 0, 0)

    def full(x):
        return pl.BlockSpec(x.shape, whole2 if x.ndim == 2 else whole3)

    outs = [jax.ShapeDtypeStruct((8, rows, cols), f32) for _ in range(parts)]
    outs.append(jax.ShapeDtypeStruct((8, 2 * LIGHTS), f32))
    small = [gain_row, tables["lobe_here"], tables["shade"], tables["plain"], tables["peak"]]
    return pl.pallas_call(
        functools.partial(sample_kernel, parts=parts),
        name="sample_sums",
        out_shape=outs,
        grid_spec=pltpu.PrefetchScalarGridSpec(
            num_scalar_prefetch=1,
            grid=(parts,),
            in_specs=[
                smem(),
                pl.BlockSpec((samples, rows, cols), lambda s, place: (0, 0, place[s])),
                pl.BlockSpec((samples, rows, cols), lambda s, place: (0, 0, place[s] // 2)),
            ]
            + [full(x) for x in small]
            + [full(x) for x in pars]
            + [full(x) for x in vises],
            out_specs=[full(x) for x in outs],
            scratch_shapes=[
                pltpu.VMEM((8, rows, cols), f32),
                pltpu.VMEM((rows, cols), jnp.int32),
                pltpu.VMEM((cols // LANES, held * rows, LANES), f32),
                pltpu.VMEM((cols // LANES, 72 * rows, LANES), f32),
                pltpu.VMEM((cols // LANES, 32 * rows, LANES), f32),
                pltpu.VMEM((2 * LIGHTS, LANES), f32),
            ],
        ),
        compiler_params=params_of(),
    )(place, cam_table, own, got, *small, *pars, *vises)


def solve_call(low, par, rights):
    return pl.pallas_call(
        solve_kernel,
        name="solve",
        out_shape=jax.ShapeDtypeStruct((8,) + par.shape[1:], f32),
        in_specs=[vmem()] * (2 + len(rights)),
        out_specs=vmem(),
        compiler_params=params_of(),
    )(low, par, *rights)


def shared_tables(lights, views, halves, echoes, first, held):
    samples = halves.shape[1]
    tiled = jnp.tile(lights, (1, CAMS))
    ones = jnp.ones((1, samples), f32)
    high = jnp.concatenate([ones, halves], axis=0)
    lobe = thirds(jnp.concatenate([halves, ones], axis=0))
    lobe = jnp.concatenate([lobe[k] for k in (0, 0, 1, 0, 1, 2)], axis=0)
    cam = jnp.arange(samples, dtype=jnp.int32)[None] // LIGHTS
    one_hot = (cam == jnp.arange(CAMS, dtype=jnp.int32)[:, None]).astype(f32)
    pad = jnp.zeros((8, samples), f32)
    mixed = [high[i : i + 1] * low for i in range(4) for low in (tiled[0:1], tiled[1:2], tiled[2:3], echoes)]
    quads = (cam % 4 == jnp.arange(4, dtype=jnp.int32)[:, None]).astype(f32)
    peaks = [quads[c : c + 1] * high for c in range(4)]
    square = [high[i : i + 1] * high[j : j + 1] for i in range(4) for j in range(i, 4)]

    def here(x):
        return lax.dynamic_slice_in_dim(x, first, held, axis=1)

    cams = held // LIGHTS
    local = one_hot[:cams, :held]
    shade = thirds(jnp.concatenate([tiled, ones, echoes], axis=0))
    shade = here(jnp.concatenate([shade[0], shade[0], shade[1]], axis=0))
    near = jnp.concatenate([ones, tiled], axis=0)[:, :held]
    return {
        "lobe": jnp.concatenate([lobe, one_hot, pad], axis=0).T.astype(bf16),
        "mixed": jnp.concatenate(mixed + peaks, axis=0),
        "square": jnp.concatenate(square + [jnp.zeros((6, samples), f32)], axis=0),
        "lobe_here": jnp.concatenate([here(lobe), local, jnp.zeros((8 - cams, held), f32)], axis=0).T.astype(bf16),
        "shade": jnp.concatenate([shade, local, local, jnp.zeros((17 - 2 * cams, held), f32)], axis=0).T.astype(bf16),
        "plain": (local[:, None, :] * near[None]).reshape(4 * cams, held),
        "peak": jnp.concatenate([here(high), jnp.zeros((4, held), f32)], axis=0),
    }


def camera_table(views, lights, gains):
    near = jnp.concatenate([lights, jnp.ones((1, LIGHTS), f32)], axis=0)
    gram = jnp.sum(near[:, None] * near[None] * (gains * gains), axis=-1)
    spread = jnp.sum(gram[:3, :3, None] * views[None], axis=1)
    echo_sq = jnp.sum(spread * views, axis=0, keepdims=True)
    lit = jnp.sum(gram[:3, 3:4] * views, axis=0, keepdims=True)
    return jnp.concatenate([views, echo_sq, lit, gram.reshape(1, 16)], axis=0)


def shifted(x, by, nz):
    return lax.ppermute(x, "tile", [(2 * z + c, 2 * ((z + by) % nz) + c) for z in range(nz) for c in range(2)])


def padded_2(cells, sides, width):
    for axis, dim in sides:
        count = lax.axis_size(axis)
        ends = count - 1
        head = lax.slice_in_dim(cells, 0, width, axis=dim)
        tail = lax.slice_in_dim(cells, cells.shape[dim] - width, cells.shape[dim], axis=dim)
        cells = jnp.concatenate(
            [
                lax.ppermute(tail, axis, [(i, i + 1) for i in range(ends)]),
                cells,
                lax.ppermute(head, axis, [(i + 1, i) for i in range(ends)]),
            ],
            axis=dim,
        )
    return cells


def smooth_tilts(tilt):
    rows = tilt.shape[1]
    cols = tilt.shape[2]
    padded = padded_2(tilt, (("grp", 1), ("tile", 2)), 1)
    boxed = jnp.zeros(tilt.shape, f32)
    for i in range(3):
        for j in range(3):
            boxed = boxed + padded[:, i : i + rows, j : j + cols]
    return 0.5 * tilt + boxed * (0.5 / 9.0)


def summed_everywhere(x):
    for axis in ("tile", "grp"):
        size = lax.axis_size(axis)
        bit = 1
        while bit < size:
            x = x + lax.ppermute(x, axis, [(i, i ^ bit) for i in range(size)])
            bit *= 2
    return x


def on_device(observed, visible, params_start, light_directions, view_dirs, gains_start):
    samples, rows, _ = observed.shape
    cols = visible.shape[1]
    tiles = lax.axis_size("tile")
    nz = tiles // 2
    tile = lax.axis_index("tile")
    chip, core = tile // 2, tile % 2
    held = 2 * samples
    cams = held // LIGHTS

    split = observed.reshape(samples, rows, nz, 2, cols)
    send = lax.dynamic_index_in_dim(split, 1 - core, axis=3, keepdims=False).reshape(samples, rows, nz * cols)
    got = lax.ppermute(send, "tile", [(i, i ^ 1) for i in range(tiles)])
    first = jnp.concatenate([params_start, visible.astype(f32)[None]], axis=0)
    blocks = [first] + [shifted(first, s, nz) for s in range(1, nz)]
    vises = [b[8].astype(jnp.int32) for b in blocks]
    place = jnp.stack([2 * ((chip - s) % nz) + core for s in range(nz)] + [core]).astype(jnp.int32)

    lights, views, halves, echoes = geometry(light_directions, view_dirs)
    tables = shared_tables(lights, views, halves, echoes, chip * held, held)
    near_views = lax.dynamic_slice_in_dim(views, chip * cams, cams, axis=1)
    near_table = jnp.concatenate([near_views, jnp.full((1, cams), chip * cams, jnp.int32).astype(f32)], axis=0)

    params = params_start
    gains = gains_start
    for iteration in range(ITERS):
        row = jnp.tile(gains[None], (1, CAMS))
        low = normal_call(camera_table(views, lights, gains), params, visible, row, tables)
        *rights, light = sample_call(
            place, near_table, observed, got, row[:, :held], tables, blocks, vises
        )
        moved = [rights[0]] + [shifted(rights[s], -s, nz) for s in range(1, nz)]
        params = solve_call(low, params, moved)
        sums = summed_everywhere(light[0].reshape(2, LIGHTS))
        gains = gains + (sums[0] - gains * sums[1]) / (sums[1] + 1.0)
        params = jnp.concatenate([smooth_tilts(params[:2]), params[2:]], axis=0)
        if iteration + 1 < ITERS:
            blocks = [params] + [shifted(params, s, nz) for s in range(1, nz)]
    return params, gains


def solution(mesh):
    return jax.shard_map(
        on_device,
        mesh=mesh,
        in_specs=(P("tile", "grp", None), P("grp", "tile"), P(None, "grp", "tile"), P(), P(), P()),
        out_specs=(P(None, "grp", "tile"), P()),
        check_vma=False,
    )
```

```python
import functools

import jax
import jax.numpy as jnp
from jax import lax
from jax.experimental import pallas as pl
from jax.experimental.pallas import tpu as pltpu
from jax.sharding import PartitionSpec as P

CAMS = 16
LIGHTS = 32
ITERS = 2

damping = 4.0
lift_z = 1.6
hidden = 1024.0
f32 = jnp.float32
bf16 = jnp.bfloat16
LANES = 128
VMEM_BYTES = 16 * 1024 * 1024
LINEAR = (2, 3, 5, 6, 7)
ENTRIES = [(i, j) for i in range(8) for j in range(i, 8)]


def split_value(x, count):
    pieces = []
    for _ in range(count - 1):
        head = x.astype(bf16).astype(f32)
        pieces.append(head)
        x = x - head
    pieces.append(x)
    return pieces


def split_pair(x):
    head = x.astype(bf16)
    return head, (x - head.astype(f32)).astype(bf16)


def dot(a, b):
    return jnp.dot(a, b, preferred_element_type=f32)


def total(terms):
    terms = list(terms)
    out = terms[0]
    for t in terms[1:]:
        out = out + t
    return out


def inner(a, b):
    return total(x * y for x, y in zip(a, b))


def texel_forms(p):
    tu, tv, diffuse, spec, raw, ambient, rim, retro = p
    q = 1.0 / jnp.sqrt(1.0 + tu * tu + tv * tv)
    nx, ny, nz = tu * q, tv * q, q
    side = -(nx * ny) * q
    by_u = ((1.0 - nx * nx) * q, side, -(nz * nx) * q)
    by_v = (side, (1.0 - ny * ny) * q, -(nz * ny) * q)
    sigma = 1.0 / (1.0 + jnp.exp(-raw))
    sharp = 1.0 + 20.0 * sigma
    slope = 20.0 * sigma * (1.0 - sigma)
    return (nx, ny, nz), by_u, by_v, sharp, slope


def seen(mask, c):
    return jnp.bitwise_and(jnp.right_shift(mask, c), 1).astype(f32)


def put_slab(ref, k, value):
    rows, cols = value.shape
    for h in range(cols // LANES):
        ref[h, k * rows : (k + 1) * rows, :] = value[:, h * LANES : (h + 1) * LANES]


def get_slab(ref, k, rows):
    return jnp.concatenate([ref[h, k * rows : (k + 1) * rows, :] for h in range(ref.shape[0])], axis=1)


def get_rows(ref, start, count, stride):
    return jnp.concatenate([ref[h, pl.ds(start, count, stride=stride), :] for h in range(ref.shape[0])], axis=1)


def put_rows(ref, start, stride, value):
    count, cols = value.shape
    for h in range(cols // LANES):
        ref[h, pl.ds(start, count, stride=stride), :] = value[:, h * LANES : (h + 1) * LANES]


def put_lobe_rows(slab, normal, sharp):
    base = [sharp * normal[0], sharp * normal[1], sharp * normal[2], -sharp]
    parts = [split_value(x, 3) for x in base]
    row = 0
    for which in (0, 1, 0, 2, 1, 0):
        for part in parts:
            slab(row, part[which])
            row += 1
    return row


def normal_kernel(
    par_ref, vis_ref, gain_ref, near_ref, cams_ref, lobe_ref, mixed_ref, square_ref, out_ref,
    rows_ref, sums_ref, mixed_scr, square_scr, cam_scr, gram_scr,
):
    rows, cols = par_ref.shape[1], par_ref.shape[2]
    depth = lobe_ref.shape[1]
    chunk = 4 * LIGHTS
    chunks = CAMS // 4

    near, views = near_ref[...], cams_ref[...]
    gain2 = gain_ref[...] * gain_ref[...]
    grams = [jnp.sum(near * near[i : i + 1] * gain2, axis=1, keepdims=True) for i in range(4)]
    for i in range(4):
        gram_scr[8 * i : 8 * i + 8, :] = jnp.broadcast_to(grams[i], (8, LANES))
    spread = [total(grams[i][k : k + 1] * views[k : k + 1] for k in range(3)) for i in range(4)]
    echo_sq = total(spread[k] * views[k : k + 1] for k in range(3))
    row = iota(views.shape, 0)
    full = jnp.where(row == 3, echo_sq, jnp.where(row == 4, spread[3], views))
    for c in range(CAMS):
        cam_scr[8 * c : 8 * c + 8, :] = jnp.broadcast_to(full[:, c : c + 1], (8, LANES))

    across = CAMS * LIGHTS
    at_light = pick(iota((LIGHTS, across), 1) % LIGHTS == iota((LIGHTS, across), 0))
    gain2 = exact(jnp.broadcast_to(gain2, (8, LIGHTS)), at_light, ((1,), (0,)))[0:1]
    for src, dst in ((mixed_ref, mixed_scr), (square_ref, square_scr)):
        head, tail = split_pair(src[...] * gain2)
        count = src.shape[0]
        dst[0:count, :] = head
        dst[count : 2 * count, :] = tail

    def slab(k, value):
        put_slab(rows_ref, k, value)

    p = [par_ref[i] for i in range(8)]
    normal, _, _, sharp, _ = texel_forms(p)
    used = put_lobe_rows(slab, normal, sharp)
    mask = vis_ref[...]
    for c in range(CAMS):
        slab(used + c, (seen(mask, c) - 1.0) * hidden)
    for k in range(used + CAMS, depth):
        slab(k, jnp.zeros((rows, cols), f32))

    def one_row(r, carry):
        texel = get_rows(rows_ref, r, depth, rows).astype(bf16)
        mixed = jnp.zeros((16, cols), f32)
        square = jnp.zeros((16, cols), f32)
        for ch in range(chunks):
            at = slice(ch * chunk, (ch + 1) * chunk)
            lobe = jnp.exp(dot(lobe_ref[at, :], texel))
            head, tail = split_pair(lobe)
            both = dot(mixed_scr[:, at], head)
            got = both[0:32] + both[32:64] + dot(mixed_scr[0:32, at], tail)
            mixed = mixed + got[0:16]
            put_rows(sums_ref, (32 + 16 * ch) * rows + r, rows, got[16:32])
            head, tail = split_pair(lobe * lobe)
            both = dot(square_scr[:, at], head)
            square = square + both[0:16] + both[16:32] + dot(square_scr[0:16, at], tail)
        put_rows(sums_ref, r, rows, mixed)
        put_rows(sums_ref, 16 * rows + r, rows, square)
        return carry

    lax.fori_loop(0, rows, one_row, 0, unroll=4)

    def one_part(h, carry):
        at = pl.ds(pl.multiple_of(h * LANES, LANES), LANES)

        def cam(c, i):
            return cam_scr[8 * c + i : 8 * c + i + 1, :]

        def sums(k):
            return sums_ref[h, k * rows : (k + 1) * rows, :]

        p = [par_ref[i, :, at] for i in range(8)]
        mask = vis_ref[:, at]
        normal, by_u, by_v, sharp, slope = texel_forms(p)
        diffuse, spec, rim = p[2], p[3], p[6]
        zero = jnp.zeros((rows, LANES), f32)
        gam = {i: zero for i in (0, 1, 5, 6)}
        own = {(i, j): zero for i in (0, 1, 5, 6) for j in (0, 1, 5, 6) if i <= j and j != 5 and i != 5}
        lit = {i: zero for i in (0, 1, 5, 6)}
        grid = {(i, k): zero for i in (0, 1, 5, 6) for k in range(4)}
        echo_sq = zero
        view_sum = [zero, zero, zero]
        for c in range(CAMS):
            w = seen(mask, c)
            v = [cam(c, i) for i in range(3)]
            back = 1.0 - inner(v, normal)
            turn = (-2.0 * rim) * back
            shape = {0: turn * inner(v, by_u), 1: turn * inner(v, by_v), 6: back * back}
            weighted = {i: w * shape[i] for i in shape}
            weighted[5] = w
            for i in gam:
                gam[i] = gam[i] + weighted[i]
                lit[i] = lit[i] + weighted[i] * cam(c, 4)
            for i, j in own:
                own[i, j] = own[i, j] + weighted[i] * shape[j]
            echo_sq = echo_sq + w * cam(c, 3)
            view_sum = [s + w * x for s, x in zip(view_sum, v)]
            for k in range(4):
                peak = sums(32 + 4 * c + k)
                for i in (0, 1, 6):
                    grid[i, k] = grid[i, k] + shape[i] * peak
                grid[5, k] = grid[5, k] + peak
        own[5, 5] = gam[5]
        for i in (0, 1):
            own[i, 5] = gam[i]
        own[5, 6] = gam[6]

        def gram(i, j):
            return gram_scr[8 * i + j : 8 * i + j + 1, :]

        entries = {ij: None for ij in ENTRIES}

        def add(i, j, value):
            ij = (min(i, j), max(i, j))
            entries[ij] = value if entries[ij] is None else entries[ij] + value

        def cross(i, j, value):
            add(i, j, value + value if i == j else value)

        flat = {0: [diffuse * x for x in by_u], 1: [diffuse * x for x in by_v], 2: list(normal)}
        edge = spec * sharp
        tilt = spec * slope
        glow = {
            0: {1 + k: edge * by_u[k] for k in range(3)},
            1: {1 + k: edge * by_v[k] for k in range(3)},
            3: {0: None},
            4: {0: -tilt, 1: tilt * normal[0], 2: tilt * normal[1], 3: tilt * normal[2]},
        }

        def combine(coefs, values):
            return total(values[k] if x is None else x * values[k] for k, x in coefs.items())

        count = gam[5]
        spread = {i: [total(gram(r, k) * flat[i][k] for k in range(3)) for r in range(3)] for i in flat}
        reach = {i: total(gram(3, k) * flat[i][k] for k in range(3)) for i in flat}
        view_spread = [total(gram(r, k) * view_sum[k] for k in range(3)) for r in range(3)]
        for i in flat:
            for j in flat:
                if i <= j:
                    add(i, j, count * inner(flat[j], spread[i]))
            for j in gam:
                cross(i, j, reach[i] * gam[j])
            cross(i, 7, inner(flat[i], view_spread))
        for i, j in own:
            add(i, j, gram(3, 3) * own[i, j])
        for i in lit:
            cross(i, 7, lit[i])
        add(7, 7, echo_sq)
        for j in glow:
            for i in flat:
                cross(i, j, total(flat[i][x] * combine(glow[j], {k: sums(4 * k + x) for k in glow[j]}) for x in range(3)))
            for i in gam:
                cross(i, j, combine(glow[j], {k: grid[i, k] for k in glow[j]}))
            cross(j, 7, combine(glow[j], {k: sums(4 * k + 3) for k in glow[j]}))
        packed = {}
        where = 0
        for i in range(4):
            for j in range(i, 4):
                packed[i, j] = packed[j, i] = where
                where += 1
        for i in glow:
            for j in glow:
                if i <= j:
                    half = {k: combine(glow[j], {x: sums(16 + packed[k, x]) for x in glow[j]}) for k in glow[i]}
                    add(i, j, combine(glow[i], half))

        def entry(i, j):
            return entries[min(i, j), max(i, j)]

        for i in range(8):
            out_ref[36 + i, :, at] = total(entry(i, j) * p[j] for j in LINEAR)
        lower = {}
        for j in range(8):
            accum = entries[j, j] + damping
            for k in range(j):
                accum = accum - lower[j, k] * lower[j, k]
            inverse = lax.rsqrt(accum)
            lower[j, j] = inverse
            for i in range(j + 1, 8):
                accum = entries[j, i]
                for k in range(j):
                    accum = accum - lower[i, k] * lower[j, k]
                lower[i, j] = accum * inverse
        for where, (i, j) in enumerate(ENTRIES):
            out_ref[where, :, at] = lower[j, i]
        return carry

    lax.fori_loop(0, cols // LANES, one_part, 0)


def sample_kernel(
    tile_ref, own_ref, got_ref, gain_ref, lobe_ref, shade_ref, plain_ref, peak_ref, slab_ref, *refs, parts
):
    par_refs, vis_refs = refs[:parts], refs[parts : 2 * parts]
    out_refs = refs[2 * parts : 3 * parts]
    light_ref = refs[3 * parts]
    par_scr, vis_scr, obs_scr, rows_ref, sums_ref, light_scr = refs[3 * parts + 1 :]
    step = pl.program_id(0)
    samples, rows, cols = own_ref.shape
    held = 2 * samples
    cams = held // LIGHTS
    for s in range(parts):

        @pl.when(step == s)
        def _():
            par_scr[...] = par_refs[s][0:8]
            vis_scr[...] = vis_refs[s][8].astype(jnp.int32)

    core = tile_ref[0] % 2
    mine = pl.multiple_of(core * (samples * rows), rows)
    theirs = pl.multiple_of((1 - core) * (samples * rows), rows)
    for h in range(cols // LANES):
        lanes = slice(h * LANES, (h + 1) * LANES)
        for src, at in ((own_ref, mine), (got_ref, theirs)):
            obs_scr[h, pl.ds(at, samples * rows), :] = src[:, :, lanes].astype(f32).reshape(samples * rows, LANES)

    def slab(k, value):
        put_slab(rows_ref, k, value)

    p = [par_scr[i] for i in range(8)]
    mask = vis_scr[...]
    normal, by_u, by_v, sharp, slope = texel_forms(p)
    base = (tile_ref[0] // 2) * cams

    def cam(c, i):
        return slab_ref[8 * c + i : 8 * c + i + 1, :][:, 0:1]

    used = put_lobe_rows(slab, normal, sharp)
    weights = [seen(mask, base + c) for c in range(cams)]
    for c in range(cams):
        slab(used + c, (weights[c] - 1.0) * hidden)
        slab(65 + c, weights[c])
    for k in range(used + cams, 32):
        slab(k, jnp.zeros((rows, cols), f32))
    shade = [p[2] * normal[0], p[2] * normal[1], p[2] * normal[2], p[5], p[7]]
    pieces = [split_value(x, 2) for x in shade]
    at = 32
    for which in (0, 1, 0):
        for piece in pieces:
            slab(at, piece[which])
            at += 1
    for c in range(cams):
        back = 1.0 - inner([cam(c, i) for i in range(3)], normal)
        head, tail = split_value(p[6] * (back * back), 2)
        slab(at + c, head)
        slab(at + cams + c, tail)
    for k in range(at + 2 * cams, 64):
        slab(k, jnp.zeros((rows, cols), f32))
    slab(64, p[3])

    at_light = pick(iota((LIGHTS, held), 1) % LIGHTS == iota((LIGHTS, held), 0))
    gains = exact(jnp.broadcast_to(gain_ref[...], (8, LIGHTS)), at_light, ((1,), (0,)))[0:1]
    plain = jnp.concatenate(split_value(plain_ref[...] * gains, 2), axis=0).astype(bf16)
    peak = jnp.concatenate(split_value(peak_ref[...] * gains, 2), axis=0).astype(bf16)
    count = plain_ref.shape[0]

    def fold(x):
        return total(x[:, k * LANES : (k + 1) * LANES] for k in range(cols // LANES))

    def one_row(r, carry):
        lift, energy = carry
        lobe = jnp.exp(dot(lobe_ref[...], get_rows(rows_ref, r, 32, rows).astype(bf16)))
        shade = dot(shade_ref[...], get_rows(rows_ref, 32 * rows + r, 32, rows).astype(bf16))
        misc = get_rows(rows_ref, 64 * rows + r, 8, rows)
        obs = get_rows(obs_scr, r, held, rows)
        for c in range(cams):
            part = slice(c * LIGHTS, (c + 1) * LIGHTS)
            full = shade[part] + misc[0:1] * lobe[part]
            kept = full * misc[1 + c : 2 + c]
            lift = lift + fold(kept * obs[part])
            energy = energy + fold(kept * full)
        head, tail = split_pair(obs * lobe)
        both = dot(plain, obs.astype(bf16))
        put_rows(sums_ref, r, rows, both[0:count] + both[count : 2 * count])
        both = dot(peak, head)
        put_rows(sums_ref, count * rows + r, rows, both[0:8] + both[8:16] + dot(peak[0:8], tail))
        return lift, energy

    zero = jnp.zeros((LIGHTS, LANES), f32)
    lift, energy = lax.fori_loop(0, rows, one_row, (zero, zero), unroll=4)

    @pl.when(step == 0)
    def _():
        light_scr[0:LIGHTS, :] = lift
        light_scr[LIGHTS : 2 * LIGHTS, :] = energy

    @pl.when(step != 0)
    def _():
        light_scr[0:LIGHTS, :] = light_scr[0:LIGHTS, :] + lift
        light_scr[LIGHTS : 2 * LIGHTS, :] = light_scr[LIGHTS : 2 * LIGHTS, :] + energy

    @pl.when(step == parts - 1)
    def _():
        for k in range(2):
            part = light_scr[k * LIGHTS : (k + 1) * LIGHTS, :]
            light_ref[k : k + 1, :] = exact(jnp.ones((8, LANES), f32), part, ((1,), (1,)))[0:1]

    def sums(k):
        return get_slab(sums_ref, k, rows)

    flat = [None, None, None]
    lone, rim_sum, echo_sum, turn_u, turn_v = None, None, None, None, None

    def grow(old, new):
        return new if old is None else old + new

    for c in range(cams):
        v = [cam(c, i) for i in range(3)]
        w = weights[c]
        one = w * sums(4 * c)
        lit = [w * sums(4 * c + 1 + x) for x in range(3)]
        back = 1.0 - inner(v, normal)
        bent = back * one
        lone = grow(lone, one)
        rim_sum = grow(rim_sum, back * bent)
        turn_u = grow(turn_u, bent * inner(v, by_u))
        turn_v = grow(turn_v, bent * inner(v, by_v))
        echo_sum = grow(echo_sum, inner(v, lit))
        flat = [grow(f, x) for f, x in zip(flat, lit)]
    spot = sums(count)
    spots = [sums(count + 1 + x) for x in range(3)]
    edge = p[3] * sharp
    twice = -2.0 * p[6]
    right = [
        p[2] * inner(by_u, flat) + edge * inner(by_u, spots) + twice * turn_u,
        p[2] * inner(by_v, flat) + edge * inner(by_v, spots) + twice * turn_v,
        inner(normal, flat),
        spot,
        p[3] * slope * (inner(normal, spots) - spot),
        lone,
        rim_sum,
        echo_sum,
    ]
    for s in range(parts):

        @pl.when(step == s)
        def _():
            for i in range(8):
                out_refs[s][i] = right[i]


def solve_kernel(low_ref, par_ref, *refs):
    right_refs, out_ref = refs[:-1], refs[-1]
    lower = {}
    for where, (i, j) in enumerate(ENTRIES):
        lower[j, i] = low_ref[where]
    right = [total(ref[i] for ref in right_refs) - low_ref[36 + i] for i in range(8)]
    forward = []
    for i in range(8):
        accum = right[i]
        for k in range(i):
            accum = accum - lower[i, k] * forward[k]
        forward.append(accum * lower[i, i])
    answer = [None] * 8
    for i in range(7, -1, -1):
        accum = forward[i]
        for k in range(i + 1, 8):
            accum = accum - lower[k, i] * answer[k]
        answer[i] = accum * lower[i, i]
    for i in range(8):
        out_ref[i] = par_ref[i] + answer[i]


def smem():
    return pl.BlockSpec(memory_space=pltpu.SMEM)


def vmem():
    return pl.BlockSpec(memory_space=pltpu.VMEM)


def params_of():
    return pltpu.CompilerParams(vmem_limit_bytes=VMEM_BYTES)


def normal_call(par, vis, gains, tables):
    _, rows, cols = par.shape
    parts = cols // LANES
    small = [tables[n] for n in ("near", "cams", "lobe", "mixed", "square")]
    return pl.pallas_call(
        normal_kernel,
        name="normal_factor",
        out_shape=jax.ShapeDtypeStruct((44, rows, cols), f32),
        in_specs=[vmem()] * 8,
        out_specs=vmem(),
        scratch_shapes=[
            pltpu.VMEM((parts, 48 * rows, LANES), f32),
            pltpu.VMEM((parts, 96 * rows, LANES), f32),
            pltpu.VMEM((64, CAMS * LIGHTS), bf16),
            pltpu.VMEM((32, CAMS * LIGHTS), bf16),
            pltpu.VMEM((8 * CAMS, LANES), f32),
            pltpu.VMEM((32, LANES), f32),
        ],
        compiler_params=params_of(),
    )(par, vis, gains, *small)


def sample_call(tile, own, got, gains, tables, pars, vises):
    parts = len(pars)
    samples, rows, _ = own.shape
    cols = pars[0].shape[2]
    held = 2 * samples

    def full(x):
        zeros = (0,) * len(x.shape)
        return pl.BlockSpec(x.shape, lambda s, tile: zeros)

    def chip(s, tile):
        return lax.rem(tile[0] // 2 + (parts - s), parts)

    outs = [jax.ShapeDtypeStruct((8, rows, cols), f32) for _ in range(parts)]
    outs.append(jax.ShapeDtypeStruct((2, LIGHTS), f32))
    small = [gains] + [tables[n] for n in ("here", "shade", "plain", "peak", "slab")]
    return pl.pallas_call(
        functools.partial(sample_kernel, parts=parts),
        name="sample_sums",
        out_shape=outs,
        grid_spec=pltpu.PrefetchScalarGridSpec(
            num_scalar_prefetch=1,
            grid=(parts,),
            in_specs=[
                pl.BlockSpec((samples, rows, cols), lambda s, tile: (0, 0, 2 * chip(s, tile) + lax.rem(tile[0], 2))),
                pl.BlockSpec((samples, rows, cols), lambda s, tile: (0, 0, chip(s, tile))),
            ]
            + [full(x) for x in small]
            + [full(x) for x in pars]
            + [full(x) for x in vises],
            out_specs=[full(x) for x in outs],
            scratch_shapes=[
                pltpu.VMEM((8, rows, cols), f32),
                pltpu.VMEM((rows, cols), jnp.int32),
                pltpu.VMEM((cols // LANES, held * rows, LANES), f32),
                pltpu.VMEM((cols // LANES, 72 * rows, LANES), f32),
                pltpu.VMEM((cols // LANES, 32 * rows, LANES), f32),
                pltpu.VMEM((2 * LIGHTS, LANES), f32),
            ],
        ),
        compiler_params=params_of(),
    )(tile, own, got, *small, *pars, *vises)


def solve_call(low, par, rights):
    return pl.pallas_call(
        solve_kernel,
        name="solve",
        out_shape=jax.ShapeDtypeStruct((8,) + par.shape[1:], f32),
        in_specs=[vmem()] * (2 + len(rights)),
        out_specs=vmem(),
        compiler_params=params_of(),
    )(low, par, *rights)


def exact(a, b, sides):
    return lax.dot_general(
        a, b, (sides, ((), ())), precision=lax.Precision.HIGHEST, preferred_element_type=f32
    )


def iota(shape, axis):
    return lax.broadcasted_iota(jnp.int32, shape, axis)


def pick(test):
    return jnp.where(test, 1.0, 0.0).astype(f32)


def setup_kernel(
    tile_ref, light_ref, view_ref,
    near_ref, cams_ref, lobe_ref, mixed_ref, square_ref,
    here_ref, shade_ref, plain_ref, peak_ref, slab_ref, light_scr, view_scr,
):
    samples = lobe_ref.shape[0]
    held = here_ref.shape[0]
    cams = held // LIGHTS
    first = (tile_ref[0] // 2) * cams

    def unit(raw_ref, scr):
        scr[...] = jnp.zeros(scr.shape, f32)
        scr[0:3, :] = raw_ref[...]
        scr[2:3, :] = scr[2:3, :] + lift_z
        lifted = scr[...]
        return lifted / jnp.sqrt(jnp.sum(lifted * lifted, axis=0, keepdims=True))

    lights = unit(light_ref, light_scr)
    views = unit(view_ref, view_scr)
    near = jnp.where(iota(lights.shape, 0) == 3, 1.0, lights)
    near_ref[...] = near
    cams_ref[...] = views

    def across(count, start):
        at_light = pick(iota((LIGHTS, count), 1) % LIGHTS == iota((LIGHTS, count), 0))
        at_view = pick(iota((CAMS, count), 1) // LIGHTS + start == iota((CAMS, count), 0))
        wide = exact(near, at_light, ((1,), (0,)))
        view = exact(views, at_view, ((1,), (0,)))
        row = iota((8, count), 0)
        raw = jnp.where(row < 3, wide + view, 0.0)
        half = raw / jnp.sqrt(jnp.sum(raw * raw, axis=0, keepdims=True))
        echo = jnp.sum(wide * view, axis=0, keepdims=True)
        return wide, half, echo

    def down(count, start):
        at_light = pick(iota((count, LIGHTS), 0) % LIGHTS == iota((count, LIGHTS), 1))
        at_view = pick(iota((count, CAMS), 0) // LIGHTS + start == iota((count, CAMS), 1))
        tall = exact(at_light, near, ((1,), (1,)))
        view = exact(at_view, views, ((1,), (1,)))
        lane = iota((count, 8), 1)
        raw = jnp.where(lane < 3, tall + view, 0.0)
        half = raw / jnp.sqrt(jnp.sum(raw * raw, axis=1, keepdims=True))
        half = jnp.where(lane == 3, 1.0, half)
        echo = jnp.sum(tall * view, axis=1, keepdims=True)
        return half, jnp.where(lane == 4, echo, tall)

    def spread(values, width, depth, order):
        lane = iota((8, depth), 1)
        out = None
        for which in range(max(order) + 1):
            head = values.astype(bf16)
            values = values - head.astype(f32)
            group = None
            for g, k in enumerate(order):
                if k == which:
                    hit = lane // width == g
                    group = hit if group is None else jnp.logical_or(group, hit)
            place = pick(jnp.logical_and(group, lane % width == iota((8, depth), 0)))
            place = jnp.where(iota((8, depth), 0) < width, place, 0.0).astype(bf16)
            got = dot(head, place)
            out = got if out is None else out + got
        return out

    wide, half, echo = across(samples, 0)
    high = [jnp.ones((1, samples), f32)] + [half[k : k + 1] for k in range(3)]
    low = [wide[k : k + 1] for k in range(3)] + [echo]
    which = iota((1, samples), 1) // LIGHTS % 4
    for i in range(4):
        for j in range(4):
            mixed_ref[4 * i + j : 4 * i + j + 1, :] = high[i] * low[j]
            mixed_ref[16 + 4 * i + j : 17 + 4 * i + j, :] = jnp.where(which == i, high[j], 0.0)
    at = 0
    square_ref[8:16, :] = jnp.zeros((8, samples), f32)
    for i in range(4):
        for j in range(i, 4):
            square_ref[at : at + 1, :] = high[i] * high[j]
            at += 1

    depth = lobe_ref.shape[1]
    half, _ = down(samples, 0)
    hot = pick(iota((samples, depth), 0) // LIGHTS + 24 == iota((samples, depth), 1))
    lobe_ref[...] = (spread(half, 4, depth, (0, 0, 1, 0, 1, 2)) + hot).astype(bf16)

    half, tall = down(held, first)
    cam = iota((held, 32), 0) // LIGHTS
    lane = iota((held, 32), 1)
    hot = pick(cam + 24 == lane)
    here_ref[...] = (spread(half, 4, 32, (0, 0, 1, 0, 1, 2)) + hot).astype(bf16)
    hot = pick(cam + 15 == lane) + pick(cam + (15 + cams) == lane)
    shade_ref[...] = (spread(tall, 5, 32, (0, 0, 1)) + hot).astype(bf16)

    wide, half, _ = across(held, first)
    peak_ref[...] = jnp.zeros(peak_ref.shape, f32)
    peak_ref[0:1, :] = jnp.ones((1, held), f32)
    plain_ref[...] = jnp.zeros(plain_ref.shape, f32)
    for k in range(3):
        peak_ref[k + 1 : k + 2, :] = half[k : k + 1]
    which = iota((1, held), 1) // LIGHTS
    for c in range(cams):
        plain_ref[4 * c : 4 * c + 1, :] = pick(which == c)
        for k in range(3):
            plain_ref[4 * c + 1 + k : 4 * c + 2 + k, :] = jnp.where(which == c, wide[k : k + 1], 0.0)
        mine = jnp.sum(jnp.where(iota(views.shape, 1) == first + c, views, 0.0), axis=1, keepdims=True)
        slab_ref[8 * c : 8 * c + 8, :] = jnp.broadcast_to(mine, (8, LANES))


TABLES = ("near", "cams", "lobe", "mixed", "square", "here", "shade", "plain", "peak", "slab")


def setup_call(tile, light_directions, view_dirs, held):
    samples = CAMS * LIGHTS
    cams = held // LIGHTS
    count = max(8, 4 * cams)
    shapes = [
        ((8, LIGHTS), f32), ((8, CAMS), f32), ((samples, 48), bf16), ((32, samples), f32),
        ((16, samples), f32), ((held, 32), bf16), ((held, 32), bf16), ((count, held), f32),
        ((8, held), f32), ((8 * cams, LANES), f32),
    ]
    outs = pl.pallas_call(
        setup_kernel,
        name="tables",
        out_shape=[jax.ShapeDtypeStruct(a, b) for a, b in shapes],
        in_specs=[smem(), vmem(), vmem()],
        out_specs=[vmem()] * len(shapes),
        scratch_shapes=[pltpu.VMEM((8, LIGHTS), f32), pltpu.VMEM((8, CAMS), f32)],
        compiler_params=params_of(),
    )(tile, light_directions, view_dirs)
    return dict(zip(TABLES, outs))


def shifted(x, by, nz):
    return lax.ppermute(x, "tile", [(2 * z + c, 2 * ((z + by) % nz) + c) for z in range(nz) for c in range(2)])


def padded_2(cells, sides):
    for axis, dim, width in sides:
        count = lax.axis_size(axis)
        ends = count - 1
        size = cells.shape[dim]
        head = lax.slice_in_dim(cells, 0, width, axis=dim)
        tail = lax.slice_in_dim(cells, size - width, size, axis=dim)
        before = lax.ppermute(tail, axis, [(i, i + 1) for i in range(ends)])
        after = lax.ppermute(head, axis, [(i + 1, i) for i in range(ends)])
        cells = jnp.concatenate(
            [
                lax.slice_in_dim(before, width - 1, width, axis=dim),
                cells,
                lax.slice_in_dim(after, 0, 1, axis=dim),
            ],
            axis=dim,
        )
    return cells


def smooth_tilts(tilt):
    rows = tilt.shape[1]
    cols = tilt.shape[2]
    padded = padded_2(tilt, (("grp", 1, 1), ("tile", 2, LANES)))
    boxed = jnp.zeros(tilt.shape, f32)
    for i in range(3):
        for j in range(3):
            boxed = boxed + padded[:, i : i + rows, j : j + cols]
    return 0.5 * tilt + boxed * (0.5 / 9.0)


def summed_everywhere(x):
    for axis in ("tile", "grp"):
        size = lax.axis_size(axis)
        bit = 1
        while bit < size:
            x = x + lax.ppermute(x, axis, [(i, i ^ bit) for i in range(size)])
            bit *= 2
    return x


def on_device(observed, visible, params_start, light_directions, view_dirs, gains_start):
    samples, rows, _ = observed.shape
    cols = visible.shape[1]
    tiles = lax.axis_size("tile")
    nz = tiles // 2
    tile = lax.axis_index("tile")
    core = tile % 2
    held = 2 * samples

    split = observed.reshape(samples, rows, nz, 2, cols)
    send = lax.dynamic_index_in_dim(split, 1 - core, axis=3, keepdims=False).reshape(samples, rows, nz * cols)
    got = lax.ppermute(send, "tile", [(i, i ^ 1) for i in range(tiles)])
    first = jnp.concatenate([params_start, visible.astype(f32)[None]], axis=0)
    blocks = [first] + [shifted(first, s, nz) for s in range(1, nz)]
    vises = blocks
    here = tile.astype(jnp.int32).reshape(1)
    tables = setup_call(here, light_directions, view_dirs, held)

    params = params_start
    gains = gains_start.reshape(1, LIGHTS)
    for iteration in range(ITERS):
        low = normal_call(params, visible, gains, tables)
        *rights, light = sample_call(here, observed, got, gains, tables, blocks, vises)
        moved = [rights[0]] + [shifted(rights[s], -s, nz) for s in range(1, nz)]
        params = solve_call(low, params, moved)
        sums = summed_everywhere(light)
        gains = gains + (sums[0:1] - gains * sums[1:2]) / (sums[1:2] + 1.0)
        params = jnp.concatenate([smooth_tilts(params[:2]), params[2:]], axis=0)
        if iteration + 1 < ITERS:
            blocks = [params] + [shifted(params, s, nz) for s in range(1, nz)]
    return params, gains.reshape(LIGHTS)


def solution(mesh):
    return jax.shard_map(
        on_device,
        mesh=mesh,
        in_specs=(P("tile", "grp", None), P("grp", "tile"), P(None, "grp", "tile"), P(), P(), P()),
        out_specs=(P(None, "grp", "tile"), P()),
        check_vma=False,
    )
```

```python
import functools

import jax
import jax.numpy as jnp
from jax import lax
from jax.experimental import pallas as pl
from jax.experimental.pallas import tpu as pltpu
from jax.sharding import PartitionSpec as P

CAMS = 16
LIGHTS = 32
ITERS = 2

damping = 4.0
lift_z = 1.6
hidden = 1024.0
f32 = jnp.float32
bf16 = jnp.bfloat16
LANES = 128
VMEM_BYTES = 16 * 1024 * 1024
LINEAR = (2, 3, 5, 6, 7)
ENTRIES = [(i, j) for i in range(8) for j in range(i, 8)]


PLACE = 4096


def tile_of(ref):
    return lax.rem(ref[0], PLACE)


def row_is_odd(ref):
    return lax.rem(ref[0] // PLACE, 2) == 1


def column_is_odd(ref):
    return lax.rem(ref[0], 2) == 1


def split_value(x, count):
    pieces = []
    for _ in range(count - 1):
        head = x.astype(bf16).astype(f32)
        pieces.append(head)
        x = x - head
    pieces.append(x)
    return pieces


def split_pair(x):
    head = x.astype(bf16)
    return head, (x - head.astype(f32)).astype(bf16)


def dot(a, b):
    return jnp.dot(a, b, preferred_element_type=f32)


def total(terms):
    terms = list(terms)
    out = terms[0]
    for t in terms[1:]:
        out = out + t
    return out


def inner(a, b):
    return total(x * y for x, y in zip(a, b))


def texel_forms(p):
    tu, tv, diffuse, spec, raw, ambient, rim, retro = p
    q = 1.0 / jnp.sqrt(1.0 + tu * tu + tv * tv)
    nx, ny, nz = tu * q, tv * q, q
    side = -(nx * ny) * q
    by_u = ((1.0 - nx * nx) * q, side, -(nz * nx) * q)
    by_v = (side, (1.0 - ny * ny) * q, -(nz * ny) * q)
    sigma = 1.0 / (1.0 + jnp.exp(-raw))
    sharp = 1.0 + 20.0 * sigma
    slope = 20.0 * sigma * (1.0 - sigma)
    return (nx, ny, nz), by_u, by_v, sharp, slope


def seen(mask, c):
    return jnp.bitwise_and(jnp.right_shift(mask, c), 1).astype(f32)


def put_slab(ref, k, value):
    rows, cols = value.shape
    for h in range(cols // LANES):
        ref[h, k * rows : (k + 1) * rows, :] = value[:, h * LANES : (h + 1) * LANES]


def get_slab(ref, k, rows):
    return jnp.concatenate([ref[h, k * rows : (k + 1) * rows, :] for h in range(ref.shape[0])], axis=1)


def get_rows(ref, start, count, stride):
    return jnp.concatenate([ref[h, pl.ds(start, count, stride=stride), :] for h in range(ref.shape[0])], axis=1)


def put_rows(ref, start, stride, value):
    count, cols = value.shape
    for h in range(cols // LANES):
        ref[h, pl.ds(start, count, stride=stride), :] = value[:, h * LANES : (h + 1) * LANES]


def put_lobe_rows(slab, normal, sharp):
    base = [sharp * normal[0], sharp * normal[1], sharp * normal[2], -sharp]
    parts = [split_value(x, 3) for x in base]
    row = 0
    for which in (0, 1, 0, 2, 1, 0):
        for part in parts:
            slab(row, part[which])
            row += 1
    return row


def normal_kernel(
    par_ref, vis_ref, gain_ref, near_ref, cams_ref, lobe_ref, mixed_ref, square_ref, out_ref,
    rows_ref, sums_ref, mixed_scr, square_scr, cam_scr, gram_scr,
):
    rows, cols = par_ref.shape[1], par_ref.shape[2]
    depth = lobe_ref.shape[1]
    chunk = 4 * LIGHTS
    chunks = CAMS // 4

    near, views = near_ref[...], cams_ref[...]
    gain2 = gain_ref[...] * gain_ref[...]
    grams = [jnp.sum(near * near[i : i + 1] * gain2, axis=1, keepdims=True) for i in range(4)]
    for i in range(4):
        gram_scr[8 * i : 8 * i + 8, :] = jnp.broadcast_to(grams[i], (8, LANES))
    spread = [total(grams[i][k : k + 1] * views[k : k + 1] for k in range(3)) for i in range(4)]
    echo_sq = total(spread[k] * views[k : k + 1] for k in range(3))
    row = iota(views.shape, 0)
    full = jnp.where(row == 3, echo_sq, jnp.where(row == 4, spread[3], views))
    for c in range(CAMS):
        cam_scr[8 * c : 8 * c + 8, :] = jnp.broadcast_to(full[:, c : c + 1], (8, LANES))

    across = CAMS * LIGHTS
    at_light = pick(iota((LIGHTS, across), 1) % LIGHTS == iota((LIGHTS, across), 0))
    gain2 = exact(jnp.broadcast_to(gain2, (8, LIGHTS)), at_light, ((1,), (0,)))[0:1]
    for src, dst in ((mixed_ref, mixed_scr), (square_ref, square_scr)):
        head, tail = split_pair(src[...] * gain2)
        count = src.shape[0]
        dst[0:count, :] = head
        dst[count : 2 * count, :] = tail

    def slab(k, value):
        put_slab(rows_ref, k, value)

    p = [par_ref[i] for i in range(8)]
    normal, _, _, sharp, _ = texel_forms(p)
    used = put_lobe_rows(slab, normal, sharp)
    mask = vis_ref[...]
    for c in range(CAMS):
        slab(used + c, (seen(mask, c) - 1.0) * hidden)
    for k in range(used + CAMS, depth):
        slab(k, jnp.zeros((rows, cols), f32))

    def one_row(r, carry):
        texel = get_rows(rows_ref, r, depth, rows).astype(bf16)
        mixed = jnp.zeros((16, cols), f32)
        square = jnp.zeros((16, cols), f32)
        for ch in range(chunks):
            at = slice(ch * chunk, (ch + 1) * chunk)
            lobe = jnp.exp(dot(lobe_ref[at, :], texel))
            head, tail = split_pair(lobe)
            both = dot(mixed_scr[:, at], head)
            got = both[0:32] + both[32:64] + dot(mixed_scr[0:32, at], tail)
            mixed = mixed + got[0:16]
            put_rows(sums_ref, (32 + 16 * ch) * rows + r, rows, got[16:32])
            head, tail = split_pair(lobe * lobe)
            both = dot(square_scr[:, at], head)
            square = square + both[0:16] + both[16:32] + dot(square_scr[0:16, at], tail)
        put_rows(sums_ref, r, rows, mixed)
        put_rows(sums_ref, 16 * rows + r, rows, square)
        return carry

    lax.fori_loop(0, rows, one_row, 0, unroll=4)

    def one_part(h, carry):
        at = pl.ds(pl.multiple_of(h * LANES, LANES), LANES)

        def cam(c, i):
            return cam_scr[8 * c + i : 8 * c + i + 1, :]

        def sums(k):
            return sums_ref[h, k * rows : (k + 1) * rows, :]

        p = [par_ref[i, :, at] for i in range(8)]
        mask = vis_ref[:, at]
        normal, by_u, by_v, sharp, slope = texel_forms(p)
        diffuse, spec, rim = p[2], p[3], p[6]
        zero = jnp.zeros((rows, LANES), f32)
        gam = {i: zero for i in (0, 1, 5, 6)}
        own = {(i, j): zero for i in (0, 1, 5, 6) for j in (0, 1, 5, 6) if i <= j and j != 5 and i != 5}
        lit = {i: zero for i in (0, 1, 5, 6)}
        grid = {(i, k): zero for i in (0, 1, 5, 6) for k in range(4)}
        echo_sq = zero
        view_sum = [zero, zero, zero]
        for c in range(CAMS):
            w = seen(mask, c)
            v = [cam(c, i) for i in range(3)]
            back = 1.0 - inner(v, normal)
            turn = (-2.0 * rim) * back
            shape = {0: turn * inner(v, by_u), 1: turn * inner(v, by_v), 6: back * back}
            weighted = {i: w * shape[i] for i in shape}
            weighted[5] = w
            for i in gam:
                gam[i] = gam[i] + weighted[i]
                lit[i] = lit[i] + weighted[i] * cam(c, 4)
            for i, j in own:
                own[i, j] = own[i, j] + weighted[i] * shape[j]
            echo_sq = echo_sq + w * cam(c, 3)
            view_sum = [s + w * x for s, x in zip(view_sum, v)]
            for k in range(4):
                peak = sums(32 + 4 * c + k)
                for i in (0, 1, 6):
                    grid[i, k] = grid[i, k] + shape[i] * peak
                grid[5, k] = grid[5, k] + peak
        own[5, 5] = gam[5]
        for i in (0, 1):
            own[i, 5] = gam[i]
        own[5, 6] = gam[6]

        def gram(i, j):
            return gram_scr[8 * i + j : 8 * i + j + 1, :]

        entries = {ij: None for ij in ENTRIES}

        def add(i, j, value):
            ij = (min(i, j), max(i, j))
            entries[ij] = value if entries[ij] is None else entries[ij] + value

        def cross(i, j, value):
            add(i, j, value + value if i == j else value)

        flat = {0: [diffuse * x for x in by_u], 1: [diffuse * x for x in by_v], 2: list(normal)}
        edge = spec * sharp
        tilt = spec * slope
        glow = {
            0: {1 + k: edge * by_u[k] for k in range(3)},
            1: {1 + k: edge * by_v[k] for k in range(3)},
            3: {0: None},
            4: {0: -tilt, 1: tilt * normal[0], 2: tilt * normal[1], 3: tilt * normal[2]},
        }

        def combine(coefs, values):
            return total(values[k] if x is None else x * values[k] for k, x in coefs.items())

        count = gam[5]
        spread = {i: [total(gram(r, k) * flat[i][k] for k in range(3)) for r in range(3)] for i in flat}
        reach = {i: total(gram(3, k) * flat[i][k] for k in range(3)) for i in flat}
        view_spread = [total(gram(r, k) * view_sum[k] for k in range(3)) for r in range(3)]
        for i in flat:
            for j in flat:
                if i <= j:
                    add(i, j, count * inner(flat[j], spread[i]))
            for j in gam:
                cross(i, j, reach[i] * gam[j])
            cross(i, 7, inner(flat[i], view_spread))
        for i, j in own:
            add(i, j, gram(3, 3) * own[i, j])
        for i in lit:
            cross(i, 7, lit[i])
        add(7, 7, echo_sq)
        for j in glow:
            for i in flat:
                cross(i, j, total(flat[i][x] * combine(glow[j], {k: sums(4 * k + x) for k in glow[j]}) for x in range(3)))
            for i in gam:
                cross(i, j, combine(glow[j], {k: grid[i, k] for k in glow[j]}))
            cross(j, 7, combine(glow[j], {k: sums(4 * k + 3) for k in glow[j]}))
        packed = {}
        where = 0
        for i in range(4):
            for j in range(i, 4):
                packed[i, j] = packed[j, i] = where
                where += 1
        for i in glow:
            for j in glow:
                if i <= j:
                    half = {k: combine(glow[j], {x: sums(16 + packed[k, x]) for x in glow[j]}) for k in glow[i]}
                    add(i, j, combine(glow[i], half))

        def entry(i, j):
            return entries[min(i, j), max(i, j)]

        for i in range(8):
            out_ref[36 + i, :, at] = total(entry(i, j) * p[j] for j in LINEAR)
        lower = {}
        for j in range(8):
            accum = entries[j, j] + damping
            for k in range(j):
                accum = accum - lower[j, k] * lower[j, k]
            inverse = lax.rsqrt(accum)
            lower[j, j] = inverse
            for i in range(j + 1, 8):
                accum = entries[j, i]
                for k in range(j):
                    accum = accum - lower[i, k] * lower[j, k]
                lower[i, j] = accum * inverse
        for where, (i, j) in enumerate(ENTRIES):
            out_ref[where, :, at] = lower[j, i]
        return carry

    lax.fori_loop(0, cols // LANES, one_part, 0)


def sample_kernel(
    tile_ref, own_ref, got_ref, gain_ref, lobe_ref, shade_ref, plain_ref, peak_ref, slab_ref, *refs, parts
):
    par_refs, vis_refs = refs[:parts], refs[parts : 2 * parts]
    out_refs = refs[2 * parts : 3 * parts]
    par_scr, vis_scr, obs_scr, rows_ref, sums_ref, light_scr = refs[3 * parts :]
    step = pl.program_id(0)
    samples, rows, cols = own_ref.shape
    held = 2 * samples
    cams = held // LIGHTS
    for s in range(parts):

        @pl.when(step == s)
        def _():
            par_scr[...] = par_refs[s][0:8]
            vis_scr[...] = vis_refs[s][8].astype(jnp.int32)

    core = tile_of(tile_ref) % 2
    mine = pl.multiple_of(core * (samples * rows), rows)
    theirs = pl.multiple_of((1 - core) * (samples * rows), rows)
    for h in range(cols // LANES):
        lanes = slice(h * LANES, (h + 1) * LANES)
        for src, at in ((own_ref, mine), (got_ref, theirs)):
            obs_scr[h, pl.ds(at, samples * rows), :] = src[:, :, lanes].astype(f32).reshape(samples * rows, LANES)

    def slab(k, value):
        put_slab(rows_ref, k, value)

    p = [par_scr[i] for i in range(8)]
    mask = vis_scr[...]
    normal, by_u, by_v, sharp, slope = texel_forms(p)
    base = (tile_of(tile_ref) // 2) * cams

    def cam(c, i):
        return slab_ref[8 * c + i : 8 * c + i + 1, :][:, 0:1]

    used = put_lobe_rows(slab, normal, sharp)
    weights = [seen(mask, base + c) for c in range(cams)]
    for c in range(cams):
        slab(used + c, (weights[c] - 1.0) * hidden)
        slab(65 + c, weights[c])
    for k in range(used + cams, 32):
        slab(k, jnp.zeros((rows, cols), f32))
    shade = [p[2] * normal[0], p[2] * normal[1], p[2] * normal[2], p[5], p[7]]
    pieces = [split_value(x, 2) for x in shade]
    at = 32
    for which in (0, 1, 0):
        for piece in pieces:
            slab(at, piece[which])
            at += 1
    for c in range(cams):
        back = 1.0 - inner([cam(c, i) for i in range(3)], normal)
        head, tail = split_value(p[6] * (back * back), 2)
        slab(at + c, head)
        slab(at + cams + c, tail)
    for k in range(at + 2 * cams, 64):
        slab(k, jnp.zeros((rows, cols), f32))
    slab(64, p[3])

    at_light = pick(iota((LIGHTS, held), 1) % LIGHTS == iota((LIGHTS, held), 0))
    gains = exact(jnp.broadcast_to(gain_ref[...], (8, LIGHTS)), at_light, ((1,), (0,)))[0:1]
    plain = jnp.concatenate(split_value(plain_ref[...] * gains, 2), axis=0).astype(bf16)
    peak = jnp.concatenate(split_value(peak_ref[...] * gains, 2), axis=0).astype(bf16)
    count = plain_ref.shape[0]

    def fold(x):
        return total(x[:, k * LANES : (k + 1) * LANES] for k in range(cols // LANES))

    def one_row(r, carry):
        lift, energy = carry
        lobe = jnp.exp(dot(lobe_ref[...], get_rows(rows_ref, r, 32, rows).astype(bf16)))
        shade = dot(shade_ref[...], get_rows(rows_ref, 32 * rows + r, 32, rows).astype(bf16))
        misc = get_rows(rows_ref, 64 * rows + r, 8, rows)
        obs = get_rows(obs_scr, r, held, rows)
        for c in range(cams):
            part = slice(c * LIGHTS, (c + 1) * LIGHTS)
            full = shade[part] + misc[0:1] * lobe[part]
            kept = full * misc[1 + c : 2 + c]
            lift = lift + fold(kept * obs[part])
            energy = energy + fold(kept * full)
        head, tail = split_pair(obs * lobe)
        both = dot(plain, obs.astype(bf16))
        put_rows(sums_ref, r, rows, both[0:count] + both[count : 2 * count])
        both = dot(peak, head)
        put_rows(sums_ref, count * rows + r, rows, both[0:8] + both[8:16] + dot(peak[0:8], tail))
        return lift, energy

    zero = jnp.zeros((LIGHTS, LANES), f32)
    lift, energy = lax.fori_loop(0, rows, one_row, (zero, zero), unroll=4)

    @pl.when(step == 0)
    def _():
        light_scr[0:LIGHTS, :] = lift
        light_scr[LIGHTS : 2 * LIGHTS, :] = energy

    @pl.when(step != 0)
    def _():
        light_scr[0:LIGHTS, :] = light_scr[0:LIGHTS, :] + lift
        light_scr[LIGHTS : 2 * LIGHTS, :] = light_scr[LIGHTS : 2 * LIGHTS, :] + energy

    @pl.when(step == parts - 1)
    def _():
        out_refs[parts - 1][8] = jnp.zeros((rows, cols), f32)
        for k in range(2):
            part = light_scr[k * LIGHTS : (k + 1) * LIGHTS, :]
            line = exact(jnp.ones((8, LANES), f32), part, ((1,), (1,)))[0:1]
            for ref in out_refs:
                ref[8, k : k + 1, 0:LIGHTS] = line

    def sums(k):
        return get_slab(sums_ref, k, rows)

    flat = [None, None, None]
    lone, rim_sum, echo_sum, turn_u, turn_v = None, None, None, None, None

    def grow(old, new):
        return new if old is None else old + new

    for c in range(cams):
        v = [cam(c, i) for i in range(3)]
        w = weights[c]
        one = w * sums(4 * c)
        lit = [w * sums(4 * c + 1 + x) for x in range(3)]
        back = 1.0 - inner(v, normal)
        bent = back * one
        lone = grow(lone, one)
        rim_sum = grow(rim_sum, back * bent)
        turn_u = grow(turn_u, bent * inner(v, by_u))
        turn_v = grow(turn_v, bent * inner(v, by_v))
        echo_sum = grow(echo_sum, inner(v, lit))
        flat = [grow(f, x) for f, x in zip(flat, lit)]
    spot = sums(count)
    spots = [sums(count + 1 + x) for x in range(3)]
    edge = p[3] * sharp
    twice = -2.0 * p[6]
    right = [
        p[2] * inner(by_u, flat) + edge * inner(by_u, spots) + twice * turn_u,
        p[2] * inner(by_v, flat) + edge * inner(by_v, spots) + twice * turn_v,
        inner(normal, flat),
        spot,
        p[3] * slope * (inner(normal, spots) - spot),
        lone,
        rim_sum,
        echo_sum,
    ]
    for s in range(parts):

        @pl.when(step == s)
        def _():
            for i in range(8):
                out_refs[s][i] = right[i]
            if s < parts - 1:
                out_refs[s][8] = jnp.zeros((rows, cols), f32)


def ring_total(terms):
    while len(terms) > 1:
        half = len(terms) // 2
        terms = [terms[k] + terms[k + half] for k in range(half)]
    return terms[0]


def solve_kernel(tile_ref, low_ref, par_ref, *refs):
    right_refs, (out_ref, first_ref, second_ref) = refs[:-3], refs[-3:]
    lower = {}
    for where, (i, j) in enumerate(ENTRIES):
        lower[j, i] = low_ref[where]
    right = [total(ref[i] for ref in right_refs) - low_ref[36 + i] for i in range(8)]
    forward = []
    for i in range(8):
        accum = right[i]
        for k in range(i):
            accum = accum - lower[i, k] * forward[k]
        forward.append(accum * lower[i, i])
    answer = [None] * 8
    for i in range(7, -1, -1):
        accum = forward[i]
        for k in range(i + 1, 8):
            accum = accum - lower[k, i] * answer[k]
        answer[i] = accum * lower[i, i]
    rows = par_ref.shape[1]
    odd = row_is_odd(tile_ref)
    first_ref[...] = jnp.zeros(first_ref.shape, f32)
    second_ref[...] = jnp.zeros(second_ref.shape, f32)
    for i in range(8):
        fresh = par_ref[i] + answer[i]
        out_ref[i] = fresh
        if i < 2:
            top, bottom = fresh[0:1], fresh[rows - 1 : rows]
            first_ref[i : i + 1, :] = jnp.where(odd, top, bottom)
            second_ref[i : i + 1, :] = jnp.where(odd, bottom, top)
    first_ref[2:4, 0:LANES] = ring_total([ref[8, 0:2, 0:LANES] for ref in right_refs])


def rows_kernel(tile_ref, par_ref, sent_ref, first_ref, second_ref, tall_ref, near_ref, far_ref, scr):
    rows, cols = par_ref.shape[1:]
    odd, side = row_is_odd(tile_ref), column_is_odd(tile_ref)
    near_ref[...] = jnp.zeros(near_ref.shape, f32)
    far_ref[...] = jnp.zeros(far_ref.shape, f32)
    for k in range(2):
        one, two = first_ref[k : k + 1, :], second_ref[k : k + 1, :]
        scr[7:8, :] = jnp.where(odd, one, two)
        scr[8 : 8 + rows, :] = par_ref[k]
        scr[8 + rows : 9 + rows, :] = jnp.where(odd, two, one)
        tall = scr[7 : 7 + rows, :] + scr[8 : 8 + rows, :] + scr[9 : 9 + rows, :]
        tall_ref[k] = tall
        left, right = tall[:, 0:LANES], tall[:, cols - LANES : cols]
        near_ref[k * rows : (k + 1) * rows, :] = jnp.where(side, left, right)
        far_ref[k * rows : (k + 1) * rows, :] = jnp.where(side, right, left)
    near_ref[2 * rows : 2 * rows + 2, :] = sent_ref[2:4, 0:LANES] + first_ref[2:4, 0:LANES]


def smooth_kernel(tile_ref, par_ref, tall_ref, sent_ref, near_ref, far_ref, out_ref, light_ref):
    rows, cols = par_ref.shape[1:]
    side = column_is_odd(tile_ref)
    lane = iota((rows, cols), 1)
    for k in range(2):
        at = slice(k * rows, (k + 1) * rows)
        tall = tall_ref[k]
        near_first, near_last = near_ref[at, 0:1], near_ref[at, LANES - 1 : LANES]
        far_first, far_last = far_ref[at, 0:1], far_ref[at, LANES - 1 : LANES]
        before = jnp.where(side, near_last, far_last)
        after = jnp.where(side, far_first, near_first)
        left = jnp.where(lane == 0, before, pltpu.roll(tall, 1, 1))
        right = jnp.where(lane == cols - 1, after, pltpu.roll(tall, cols - 1, 1))
        out_ref[k] = 0.5 * par_ref[k] + (tall + left + right) * (0.5 / 9.0)
    for k in range(2, 8):
        out_ref[k] = par_ref[k]
    light_ref[...] = jnp.zeros(light_ref.shape, f32)
    light_ref[0:2, :] = sent_ref[2 * rows : 2 * rows + 2, :] + near_ref[2 * rows : 2 * rows + 2, :]


def smem():
    return pl.BlockSpec(memory_space=pltpu.SMEM)


def vmem():
    return pl.BlockSpec(memory_space=pltpu.VMEM)


def params_of():
    return pltpu.CompilerParams(vmem_limit_bytes=VMEM_BYTES)


def normal_call(par, vis, gains, tables):
    _, rows, cols = par.shape
    parts = cols // LANES
    small = [tables[n] for n in ("near", "cams", "lobe", "mixed", "square")]
    return pl.pallas_call(
        normal_kernel,
        name="normal_factor",
        out_shape=jax.ShapeDtypeStruct((44, rows, cols), f32),
        in_specs=[vmem()] * 8,
        out_specs=vmem(),
        scratch_shapes=[
            pltpu.VMEM((parts, 48 * rows, LANES), f32),
            pltpu.VMEM((parts, 96 * rows, LANES), f32),
            pltpu.VMEM((64, CAMS * LIGHTS), bf16),
            pltpu.VMEM((32, CAMS * LIGHTS), bf16),
            pltpu.VMEM((8 * CAMS, LANES), f32),
            pltpu.VMEM((32, LANES), f32),
        ],
        compiler_params=params_of(),
    )(par, vis, gains, *small)


def sample_call(tile, own, got, gains, tables, pars, vises):
    parts = len(pars)
    samples, rows, _ = own.shape
    cols = pars[0].shape[2]
    held = 2 * samples

    def full(x):
        zeros = (0,) * len(x.shape)
        return pl.BlockSpec(x.shape, lambda s, tile: zeros)

    def chip(s, tile):
        return lax.rem(tile_of(tile) // 2 + (parts - s), parts)

    outs = [jax.ShapeDtypeStruct((9, rows, cols), f32) for _ in range(parts)]
    small = [gains] + [tables[n] for n in ("here", "shade", "plain", "peak", "slab")]
    return pl.pallas_call(
        functools.partial(sample_kernel, parts=parts),
        name="sample_sums",
        out_shape=outs,
        grid_spec=pltpu.PrefetchScalarGridSpec(
            num_scalar_prefetch=1,
            grid=(parts,),
            in_specs=[
                pl.BlockSpec((samples, rows, cols), lambda s, tile: (0, 0, 2 * chip(s, tile) + lax.rem(tile[0], 2))),
                pl.BlockSpec((samples, rows, cols), lambda s, tile: (0, 0, chip(s, tile))),
            ]
            + [full(x) for x in small]
            + [full(x) for x in pars]
            + [full(x) for x in vises],
            out_specs=[full(x) for x in outs],
            scratch_shapes=[
                pltpu.VMEM((8, rows, cols), f32),
                pltpu.VMEM((rows, cols), jnp.int32),
                pltpu.VMEM((cols // LANES, held * rows, LANES), f32),
                pltpu.VMEM((cols // LANES, 72 * rows, LANES), f32),
                pltpu.VMEM((cols // LANES, 32 * rows, LANES), f32),
                pltpu.VMEM((2 * LIGHTS, LANES), f32),
            ],
        ),
        compiler_params=params_of(),
    )(tile, own, got, *small, *pars, *vises)


def plain_call(kernel, name, shapes, scratch, tile, *args):
    return pl.pallas_call(
        kernel,
        name=name,
        out_shape=[jax.ShapeDtypeStruct(shape, f32) for shape in shapes],
        in_specs=[smem()] + [vmem()] * len(args),
        out_specs=[vmem()] * len(shapes),
        scratch_shapes=[pltpu.VMEM(shape, f32) for shape in scratch],
        compiler_params=params_of(),
    )(tile, *args)


def pairs(count, start):
    out = []
    for i in range(start, count - 1, 2):
        out += [(i, i + 1), (i + 1, i)]
    return out


def settle(tile, low, params, moved):
    _, rows, cols = params.shape
    grps, tiles = lax.axis_size("grp"), lax.axis_size("tile")
    strip = (8, cols)
    params, sent, other = plain_call(
        solve_kernel, "solve", [params.shape, strip, strip], [], tile, low, params, *moved
    )
    first = lax.ppermute(sent, "grp", pairs(grps, 0))
    second = lax.ppermute(other, "grp", pairs(grps, 1))
    patch = (2 * rows + 8, LANES)
    tall, sent, other = plain_call(
        rows_kernel, "rows", [(2, rows, cols), patch, patch], [(24, cols)], tile, params, sent, first, second
    )
    near = lax.ppermute(sent, "tile", pairs(tiles, 0))
    far = lax.ppermute(other, "tile", pairs(tiles, 1))
    params, light = plain_call(
        smooth_kernel, "smooth", [params.shape, (8, LANES)], [], tile, params, tall, sent, near, far
    )
    bit = 2
    while bit < grps:
        light = light + lax.ppermute(light, "grp", [(i, i ^ bit) for i in range(grps)])
        bit *= 2
    return params, light[0:1, 0:LIGHTS], light[1:2, 0:LIGHTS]


def exact(a, b, sides):
    return lax.dot_general(
        a, b, (sides, ((), ())), precision=lax.Precision.HIGHEST, preferred_element_type=f32
    )


def iota(shape, axis):
    return lax.broadcasted_iota(jnp.int32, shape, axis)


def pick(test):
    return jnp.where(test, 1.0, 0.0).astype(f32)


def setup_kernel(
    tile_ref, light_ref, view_ref,
    near_ref, cams_ref, lobe_ref, mixed_ref, square_ref,
    here_ref, shade_ref, plain_ref, peak_ref, slab_ref, light_scr, view_scr,
):
    samples = lobe_ref.shape[0]
    held = here_ref.shape[0]
    cams = held // LIGHTS
    first = (tile_of(tile_ref) // 2) * cams

    def unit(raw_ref, scr):
        scr[...] = jnp.zeros(scr.shape, f32)
        scr[0:3, :] = raw_ref[...]
        scr[2:3, :] = scr[2:3, :] + lift_z
        lifted = scr[...]
        return lifted / jnp.sqrt(jnp.sum(lifted * lifted, axis=0, keepdims=True))

    lights = unit(light_ref, light_scr)
    views = unit(view_ref, view_scr)
    near = jnp.where(iota(lights.shape, 0) == 3, 1.0, lights)
    near_ref[...] = near
    cams_ref[...] = views

    def across(count, start):
        at_light = pick(iota((LIGHTS, count), 1) % LIGHTS == iota((LIGHTS, count), 0))
        at_view = pick(iota((CAMS, count), 1) // LIGHTS + start == iota((CAMS, count), 0))
        wide = exact(near, at_light, ((1,), (0,)))
        view = exact(views, at_view, ((1,), (0,)))
        row = iota((8, count), 0)
        raw = jnp.where(row < 3, wide + view, 0.0)
        half = raw / jnp.sqrt(jnp.sum(raw * raw, axis=0, keepdims=True))
        echo = jnp.sum(wide * view, axis=0, keepdims=True)
        return wide, half, echo

    def down(count, start):
        at_light = pick(iota((count, LIGHTS), 0) % LIGHTS == iota((count, LIGHTS), 1))
        at_view = pick(iota((count, CAMS), 0) // LIGHTS + start == iota((count, CAMS), 1))
        tall = exact(at_light, near, ((1,), (1,)))
        view = exact(at_view, views, ((1,), (1,)))
        lane = iota((count, 8), 1)
        raw = jnp.where(lane < 3, tall + view, 0.0)
        half = raw / jnp.sqrt(jnp.sum(raw * raw, axis=1, keepdims=True))
        half = jnp.where(lane == 3, 1.0, half)
        echo = jnp.sum(tall * view, axis=1, keepdims=True)
        return half, jnp.where(lane == 4, echo, tall)

    def spread(values, width, depth, order):
        lane = iota((8, depth), 1)
        out = None
        for which in range(max(order) + 1):
            head = values.astype(bf16)
            values = values - head.astype(f32)
            group = None
            for g, k in enumerate(order):
                if k == which:
                    hit = lane // width == g
                    group = hit if group is None else jnp.logical_or(group, hit)
            place = pick(jnp.logical_and(group, lane % width == iota((8, depth), 0)))
            place = jnp.where(iota((8, depth), 0) < width, place, 0.0).astype(bf16)
            got = dot(head, place)
            out = got if out is None else out + got
        return out

    wide, half, echo = across(samples, 0)
    high = [jnp.ones((1, samples), f32)] + [half[k : k + 1] for k in range(3)]
    low = [wide[k : k + 1] for k in range(3)] + [echo]
    which = iota((1, samples), 1) // LIGHTS % 4
    for i in range(4):
        for j in range(4):
            mixed_ref[4 * i + j : 4 * i + j + 1, :] = high[i] * low[j]
            mixed_ref[16 + 4 * i + j : 17 + 4 * i + j, :] = jnp.where(which == i, high[j], 0.0)
    at = 0
    square_ref[8:16, :] = jnp.zeros((8, samples), f32)
    for i in range(4):
        for j in range(i, 4):
            square_ref[at : at + 1, :] = high[i] * high[j]
            at += 1

    depth = lobe_ref.shape[1]
    half, _ = down(samples, 0)
    hot = pick(iota((samples, depth), 0) // LIGHTS + 24 == iota((samples, depth), 1))
    lobe_ref[...] = (spread(half, 4, depth, (0, 0, 1, 0, 1, 2)) + hot).astype(bf16)

    half, tall = down(held, first)
    cam = iota((held, 32), 0) // LIGHTS
    lane = iota((held, 32), 1)
    hot = pick(cam + 24 == lane)
    here_ref[...] = (spread(half, 4, 32, (0, 0, 1, 0, 1, 2)) + hot).astype(bf16)
    hot = pick(cam + 15 == lane) + pick(cam + (15 + cams) == lane)
    shade_ref[...] = (spread(tall, 5, 32, (0, 0, 1)) + hot).astype(bf16)

    wide, half, _ = across(held, first)
    peak_ref[...] = jnp.zeros(peak_ref.shape, f32)
    peak_ref[0:1, :] = jnp.ones((1, held), f32)
    plain_ref[...] = jnp.zeros(plain_ref.shape, f32)
    for k in range(3):
        peak_ref[k + 1 : k + 2, :] = half[k : k + 1]
    which = iota((1, held), 1) // LIGHTS
    for c in range(cams):
        plain_ref[4 * c : 4 * c + 1, :] = pick(which == c)
        for k in range(3):
            plain_ref[4 * c + 1 + k : 4 * c + 2 + k, :] = jnp.where(which == c, wide[k : k + 1], 0.0)
        mine = jnp.sum(jnp.where(iota(views.shape, 1) == first + c, views, 0.0), axis=1, keepdims=True)
        slab_ref[8 * c : 8 * c + 8, :] = jnp.broadcast_to(mine, (8, LANES))


TABLES = ("near", "cams", "lobe", "mixed", "square", "here", "shade", "plain", "peak", "slab")


def setup_call(tile, light_directions, view_dirs, held):
    samples = CAMS * LIGHTS
    cams = held // LIGHTS
    count = max(8, 4 * cams)
    shapes = [
        ((8, LIGHTS), f32), ((8, CAMS), f32), ((samples, 48), bf16), ((32, samples), f32),
        ((16, samples), f32), ((held, 32), bf16), ((held, 32), bf16), ((count, held), f32),
        ((8, held), f32), ((8 * cams, LANES), f32),
    ]
    outs = pl.pallas_call(
        setup_kernel,
        name="tables",
        out_shape=[jax.ShapeDtypeStruct(a, b) for a, b in shapes],
        in_specs=[smem(), vmem(), vmem()],
        out_specs=[vmem()] * len(shapes),
        scratch_shapes=[pltpu.VMEM((8, LIGHTS), f32), pltpu.VMEM((8, CAMS), f32)],
        compiler_params=params_of(),
    )(tile, light_directions, view_dirs)
    return dict(zip(TABLES, outs))


def shifted(x, by, nz):
    return lax.ppermute(x, "tile", [(2 * z + c, 2 * ((z + by) % nz) + c) for z in range(nz) for c in range(2)])


def on_device(observed, visible, params_start, light_directions, view_dirs, gains_start):
    samples, rows, _ = observed.shape
    cols = visible.shape[1]
    tiles = lax.axis_size("tile")
    nz = tiles // 2
    tile = lax.axis_index("tile")
    core = tile % 2
    held = 2 * samples

    split = observed.reshape(samples, rows, nz, 2, cols)
    send = lax.dynamic_index_in_dim(split, 1 - core, axis=3, keepdims=False).reshape(samples, rows, nz * cols)
    got = lax.ppermute(send, "tile", [(i, i ^ 1) for i in range(tiles)])
    first = jnp.concatenate([params_start, visible.astype(f32)[None]], axis=0)
    blocks = [first] + [shifted(first, s, nz) for s in range(1, nz)]
    vises = blocks
    here = (tile + PLACE * lax.axis_index("grp")).astype(jnp.int32).reshape(1)
    tables = setup_call(here, light_directions, view_dirs, held)

    params = params_start
    gains = gains_start.reshape(1, LIGHTS)
    for iteration in range(ITERS):
        low = normal_call(params, visible, gains, tables)
        rights = sample_call(here, observed, got, gains, tables, blocks, vises)
        moved = [rights[0]] + [shifted(rights[s], -s, nz) for s in range(1, nz)]
        params, lifted, energy = settle(here, low, params, moved)
        gains = gains + (lifted - gains * energy) / (energy + 1.0)
        if iteration + 1 < ITERS:
            blocks = [params] + [shifted(params, s, nz) for s in range(1, nz)]
    return params, gains.reshape(LIGHTS)


def solution(mesh):
    return jax.shard_map(
        on_device,
        mesh=mesh,
        in_specs=(P("tile", "grp", None), P("grp", "tile"), P(None, "grp", "tile"), P(), P(), P()),
        out_specs=(P(None, "grp", "tile"), P()),
        check_vma=False,
    )
```

```python
import functools

import jax
import jax.numpy as jnp
from jax import lax
from jax.experimental import pallas as pl
from jax.experimental.pallas import tpu as pltpu
from jax.sharding import PartitionSpec as P

CAMS = 16
LIGHTS = 32
ITERS = 2

damping = 4.0
lift_z = 1.6
hidden = 1024.0
f32 = jnp.float32
bf16 = jnp.bfloat16
LANES = 128
VMEM_BYTES = 16 * 1024 * 1024
LINEAR = (2, 3, 5, 6, 7)
ENTRIES = [(i, j) for i in range(8) for j in range(i, 8)]


PLACE = 4096


def tile_of(ref):
    return lax.rem(ref[0], PLACE)


def row_is_odd(ref):
    return lax.rem(ref[0] // PLACE, 2) == 1


def column_is_odd(ref):
    return lax.rem(ref[0], 2) == 1


def split_value(x, count):
    pieces = []
    for _ in range(count - 1):
        head = x.astype(bf16).astype(f32)
        pieces.append(head)
        x = x - head
    pieces.append(x)
    return pieces


def split_pair(x):
    head = x.astype(bf16)
    return head, (x - head.astype(f32)).astype(bf16)


def dot(a, b):
    return jnp.dot(a, b, preferred_element_type=f32)


def total(terms):
    terms = list(terms)
    out = terms[0]
    for t in terms[1:]:
        out = out + t
    return out


def inner(a, b):
    return total(x * y for x, y in zip(a, b))


def texel_forms(p):
    tu, tv, diffuse, spec, raw, ambient, rim, retro = p
    q = 1.0 / jnp.sqrt(1.0 + tu * tu + tv * tv)
    nx, ny, nz = tu * q, tv * q, q
    side = -(nx * ny) * q
    by_u = ((1.0 - nx * nx) * q, side, -(nz * nx) * q)
    by_v = (side, (1.0 - ny * ny) * q, -(nz * ny) * q)
    sigma = 1.0 / (1.0 + jnp.exp(-raw))
    sharp = 1.0 + 20.0 * sigma
    slope = 20.0 * sigma * (1.0 - sigma)
    return (nx, ny, nz), by_u, by_v, sharp, slope


def seen(mask, c):
    return jnp.bitwise_and(jnp.right_shift(mask, c), 1).astype(f32)


def put_slab(ref, k, value):
    rows, cols = value.shape
    for h in range(cols // LANES):
        ref[h, k * rows : (k + 1) * rows, :] = value[:, h * LANES : (h + 1) * LANES]


def get_slab(ref, k, rows):
    return jnp.concatenate([ref[h, k * rows : (k + 1) * rows, :] for h in range(ref.shape[0])], axis=1)


def get_rows(ref, start, count, stride):
    return jnp.concatenate([ref[h, pl.ds(start, count, stride=stride), :] for h in range(ref.shape[0])], axis=1)


def put_rows(ref, start, stride, value):
    count, cols = value.shape
    for h in range(cols // LANES):
        ref[h, pl.ds(start, count, stride=stride), :] = value[:, h * LANES : (h + 1) * LANES]


def put_lobe_rows(slab, normal, sharp):
    base = [sharp * normal[0], sharp * normal[1], sharp * normal[2], -sharp]
    parts = [split_value(x, 3) for x in base]
    row = 0
    for which in (0, 1, 0, 2, 1, 0):
        for part in parts:
            slab(row, part[which])
            row += 1
    return row


def normal_kernel(
    par_ref, vis_ref, gain_ref, near_ref, cams_ref, lobe_ref, mixed_ref, square_ref, out_ref,
    rows_ref, sums_ref, mixed_scr, square_scr, cam_scr, gram_scr,
):
    rows, cols = par_ref.shape[1], par_ref.shape[2]
    depth = lobe_ref.shape[1]
    chunk = 4 * LIGHTS
    chunks = CAMS // 4

    near, views = near_ref[...], cams_ref[...]
    gain2 = gain_ref[...] * gain_ref[...]
    grams = [jnp.sum(near * near[i : i + 1] * gain2, axis=1, keepdims=True) for i in range(4)]
    for i in range(4):
        gram_scr[8 * i : 8 * i + 8, :] = jnp.broadcast_to(grams[i], (8, LANES))
    spread = [total(grams[i][k : k + 1] * views[k : k + 1] for k in range(3)) for i in range(4)]
    echo_sq = total(spread[k] * views[k : k + 1] for k in range(3))
    row = iota(views.shape, 0)
    full = jnp.where(row == 3, echo_sq, jnp.where(row == 4, spread[3], views))
    for c in range(CAMS):
        cam_scr[8 * c : 8 * c + 8, :] = jnp.broadcast_to(full[:, c : c + 1], (8, LANES))

    across = CAMS * LIGHTS
    at_light = pick(iota((LIGHTS, across), 1) % LIGHTS == iota((LIGHTS, across), 0))
    gain2 = exact(jnp.broadcast_to(gain2, (8, LIGHTS)), at_light, ((1,), (0,)))[0:1]
    for src, dst in ((mixed_ref, mixed_scr), (square_ref, square_scr)):
        head, tail = split_pair(src[...] * gain2)
        count = src.shape[0]
        dst[0:count, :] = head
        dst[count : 2 * count, :] = tail

    def slab(k, value):
        put_slab(rows_ref, k, value)

    p = [par_ref[i] for i in range(8)]
    normal, _, _, sharp, _ = texel_forms(p)
    used = put_lobe_rows(slab, normal, sharp)
    mask = vis_ref[...]
    for c in range(CAMS):
        slab(used + c, (seen(mask, c) - 1.0) * hidden)
    for k in range(used + CAMS, depth):
        slab(k, jnp.zeros((rows, cols), f32))

    def one_row(r, carry):
        texel = get_rows(rows_ref, r, depth, rows).astype(bf16)
        mixed = jnp.zeros((16, cols), f32)
        square = jnp.zeros((16, cols), f32)
        for ch in range(chunks):
            at = slice(ch * chunk, (ch + 1) * chunk)
            lobe = jnp.exp(dot(lobe_ref[at, :], texel))
            head, tail = split_pair(lobe)
            both = dot(mixed_scr[:, at], head)
            got = both[0:32] + both[32:64] + dot(mixed_scr[0:32, at], tail)
            mixed = mixed + got[0:16]
            put_rows(sums_ref, (32 + 16 * ch) * rows + r, rows, got[16:32])
            head, tail = split_pair(lobe * lobe)
            both = dot(square_scr[:, at], head)
            square = square + both[0:16] + both[16:32] + dot(square_scr[0:16, at], tail)
        put_rows(sums_ref, r, rows, mixed)
        put_rows(sums_ref, 16 * rows + r, rows, square)
        return carry

    lax.fori_loop(0, rows, one_row, 0, unroll=4)

    def one_part(h, carry):
        at = pl.ds(pl.multiple_of(h * LANES, LANES), LANES)

        def cam(c, i):
            return cam_scr[8 * c + i : 8 * c + i + 1, :]

        def sums(k):
            return sums_ref[h, k * rows : (k + 1) * rows, :]

        p = [par_ref[i, :, at] for i in range(8)]
        mask = vis_ref[:, at]
        normal, by_u, by_v, sharp, slope = texel_forms(p)
        diffuse, spec, rim = p[2], p[3], p[6]
        zero = jnp.zeros((rows, LANES), f32)
        gam = {i: zero for i in (0, 1, 5, 6)}
        own = {(i, j): zero for i in (0, 1, 5, 6) for j in (0, 1, 5, 6) if i <= j and j != 5 and i != 5}
        lit = {i: zero for i in (0, 1, 5, 6)}
        grid = {(i, k): zero for i in (0, 1, 5, 6) for k in range(4)}
        echo_sq = zero
        view_sum = [zero, zero, zero]
        for c in range(CAMS):
            w = seen(mask, c)
            v = [cam(c, i) for i in range(3)]
            back = 1.0 - inner(v, normal)
            turn = (-2.0 * rim) * back
            shape = {0: turn * inner(v, by_u), 1: turn * inner(v, by_v), 6: back * back}
            weighted = {i: w * shape[i] for i in shape}
            weighted[5] = w
            for i in gam:
                gam[i] = gam[i] + weighted[i]
                lit[i] = lit[i] + weighted[i] * cam(c, 4)
            for i, j in own:
                own[i, j] = own[i, j] + weighted[i] * shape[j]
            echo_sq = echo_sq + w * cam(c, 3)
            view_sum = [s + w * x for s, x in zip(view_sum, v)]
            for k in range(4):
                peak = sums(32 + 4 * c + k)
                for i in (0, 1, 6):
                    grid[i, k] = grid[i, k] + shape[i] * peak
                grid[5, k] = grid[5, k] + peak
        own[5, 5] = gam[5]
        for i in (0, 1):
            own[i, 5] = gam[i]
        own[5, 6] = gam[6]

        def gram(i, j):
            return gram_scr[8 * i + j : 8 * i + j + 1, :]

        entries = {ij: None for ij in ENTRIES}

        def add(i, j, value):
            ij = (min(i, j), max(i, j))
            entries[ij] = value if entries[ij] is None else entries[ij] + value

        def cross(i, j, value):
            add(i, j, value + value if i == j else value)

        flat = {0: [diffuse * x for x in by_u], 1: [diffuse * x for x in by_v], 2: list(normal)}
        edge = spec * sharp
        tilt = spec * slope
        glow = {
            0: {1 + k: edge * by_u[k] for k in range(3)},
            1: {1 + k: edge * by_v[k] for k in range(3)},
            3: {0: None},
            4: {0: -tilt, 1: tilt * normal[0], 2: tilt * normal[1], 3: tilt * normal[2]},
        }

        def combine(coefs, values):
            return total(values[k] if x is None else x * values[k] for k, x in coefs.items())

        count = gam[5]
        spread = {i: [total(gram(r, k) * flat[i][k] for k in range(3)) for r in range(3)] for i in flat}
        reach = {i: total(gram(3, k) * flat[i][k] for k in range(3)) for i in flat}
        view_spread = [total(gram(r, k) * view_sum[k] for k in range(3)) for r in range(3)]
        for i in flat:
            for j in flat:
                if i <= j:
                    add(i, j, count * inner(flat[j], spread[i]))
            for j in gam:
                cross(i, j, reach[i] * gam[j])
            cross(i, 7, inner(flat[i], view_spread))
        for i, j in own:
            add(i, j, gram(3, 3) * own[i, j])
        for i in lit:
            cross(i, 7, lit[i])
        add(7, 7, echo_sq)
        for j in glow:
            for i in flat:
                cross(i, j, total(flat[i][x] * combine(glow[j], {k: sums(4 * k + x) for k in glow[j]}) for x in range(3)))
            for i in gam:
                cross(i, j, combine(glow[j], {k: grid[i, k] for k in glow[j]}))
            cross(j, 7, combine(glow[j], {k: sums(4 * k + 3) for k in glow[j]}))
        packed = {}
        where = 0
        for i in range(4):
            for j in range(i, 4):
                packed[i, j] = packed[j, i] = where
                where += 1
        for i in glow:
            for j in glow:
                if i <= j:
                    half = {k: combine(glow[j], {x: sums(16 + packed[k, x]) for x in glow[j]}) for k in glow[i]}
                    add(i, j, combine(glow[i], half))

        def entry(i, j):
            return entries[min(i, j), max(i, j)]

        for i in range(8):
            out_ref[36 + i, :, at] = total(entry(i, j) * p[j] for j in LINEAR)
        lower = {}
        for j in range(8):
            accum = entries[j, j] + damping
            for k in range(j):
                accum = accum - lower[j, k] * lower[j, k]
            inverse = lax.rsqrt(accum)
            lower[j, j] = inverse
            for i in range(j + 1, 8):
                accum = entries[j, i]
                for k in range(j):
                    accum = accum - lower[i, k] * lower[j, k]
                lower[i, j] = accum * inverse
        for where, (i, j) in enumerate(ENTRIES):
            out_ref[where, :, at] = lower[j, i]
        return carry

    lax.fori_loop(0, cols // LANES, one_part, 0)


def sample_kernel(
    tile_ref, own_ref, got_ref, gain_ref, lobe_ref, shade_ref, plain_ref, peak_ref, slab_ref, *refs, parts
):
    par_refs, vis_refs = refs[:parts], refs[parts : 2 * parts]
    out_refs = refs[2 * parts : 3 * parts]
    par_scr, vis_scr, obs_scr, rows_ref, sums_ref, light_scr = refs[3 * parts :]
    step = pl.program_id(0)
    samples, rows, cols = own_ref.shape
    held = 2 * samples
    cams = held // LIGHTS
    for s in range(parts):

        @pl.when(step == s)
        def _():
            par_scr[...] = par_refs[s][0:8]
            vis_scr[...] = vis_refs[s][8].astype(jnp.int32)

    core = tile_of(tile_ref) % 2
    mine = pl.multiple_of(core * (samples * rows), rows)
    theirs = pl.multiple_of((1 - core) * (samples * rows), rows)
    for h in range(cols // LANES):
        lanes = slice(h * LANES, (h + 1) * LANES)
        for src, at in ((own_ref, mine), (got_ref, theirs)):
            obs_scr[h, pl.ds(at, samples * rows), :] = src[:, :, lanes].astype(f32).reshape(samples * rows, LANES)

    def slab(k, value):
        put_slab(rows_ref, k, value)

    p = [par_scr[i] for i in range(8)]
    mask = vis_scr[...]
    normal, by_u, by_v, sharp, slope = texel_forms(p)
    base = (tile_of(tile_ref) // 2) * cams

    def cam(c, i):
        return slab_ref[8 * c + i : 8 * c + i + 1, :][:, 0:1]

    used = put_lobe_rows(slab, normal, sharp)
    weights = [seen(mask, base + c) for c in range(cams)]
    for c in range(cams):
        slab(used + c, (weights[c] - 1.0) * hidden)
        slab(65 + c, weights[c])
    for k in range(used + cams, 32):
        slab(k, jnp.zeros((rows, cols), f32))
    shade = [p[2] * normal[0], p[2] * normal[1], p[2] * normal[2], p[5], p[7]]
    pieces = [split_value(x, 2) for x in shade]
    at = 32
    for which in (0, 1, 0):
        for piece in pieces:
            slab(at, piece[which])
            at += 1
    for c in range(cams):
        back = 1.0 - inner([cam(c, i) for i in range(3)], normal)
        head, tail = split_value(p[6] * (back * back), 2)
        slab(at + c, head)
        slab(at + cams + c, tail)
    for k in range(at + 2 * cams, 64):
        slab(k, jnp.zeros((rows, cols), f32))
    slab(64, p[3])

    at_light = pick(iota((LIGHTS, held), 1) % LIGHTS == iota((LIGHTS, held), 0))
    gains = exact(jnp.broadcast_to(gain_ref[...], (8, LIGHTS)), at_light, ((1,), (0,)))[0:1]
    plain = jnp.concatenate(split_value(plain_ref[...] * gains, 2), axis=0).astype(bf16)
    peak = jnp.concatenate(split_value(peak_ref[...] * gains, 2), axis=0).astype(bf16)
    count = plain_ref.shape[0]

    def fold(x):
        return total(x[:, k * LANES : (k + 1) * LANES] for k in range(cols // LANES))

    def one_row(r, carry):
        lift, energy = carry
        lobe = jnp.exp(dot(lobe_ref[...], get_rows(rows_ref, r, 32, rows).astype(bf16)))
        shade = dot(shade_ref[...], get_rows(rows_ref, 32 * rows + r, 32, rows).astype(bf16))
        misc = get_rows(rows_ref, 64 * rows + r, 8, rows)
        obs = get_rows(obs_scr, r, held, rows)
        for c in range(cams):
            part = slice(c * LIGHTS, (c + 1) * LIGHTS)
            full = shade[part] + misc[0:1] * lobe[part]
            kept = full * misc[1 + c : 2 + c]
            lift = lift + fold(kept * obs[part])
            energy = energy + fold(kept * full)
        head, tail = split_pair(obs * lobe)
        both = dot(plain, obs.astype(bf16))
        put_rows(sums_ref, r, rows, both[0:count] + both[count : 2 * count])
        both = dot(peak, head)
        put_rows(sums_ref, count * rows + r, rows, both[0:8] + both[8:16] + dot(peak[0:8], tail))
        return lift, energy

    zero = jnp.zeros((LIGHTS, LANES), f32)
    lift, energy = lax.fori_loop(0, rows, one_row, (zero, zero), unroll=4)

    @pl.when(step == 0)
    def _():
        light_scr[0:LIGHTS, :] = lift
        light_scr[LIGHTS : 2 * LIGHTS, :] = energy

    @pl.when(step != 0)
    def _():
        light_scr[0:LIGHTS, :] = light_scr[0:LIGHTS, :] + lift
        light_scr[LIGHTS : 2 * LIGHTS, :] = light_scr[LIGHTS : 2 * LIGHTS, :] + energy

    @pl.when(step == parts - 1)
    def _():
        out_refs[parts - 1][8] = jnp.zeros((rows, cols), f32)
        for k in range(2):
            part = light_scr[k * LIGHTS : (k + 1) * LIGHTS, :]
            line = exact(jnp.ones((8, LANES), f32), part, ((1,), (1,)))[0:1]
            for ref in out_refs:
                ref[8, k : k + 1, 0:LIGHTS] = line

    def sums(k):
        return get_slab(sums_ref, k, rows)

    flat = [None, None, None]
    lone, rim_sum, echo_sum, turn_u, turn_v = None, None, None, None, None

    def grow(old, new):
        return new if old is None else old + new

    for c in range(cams):
        v = [cam(c, i) for i in range(3)]
        w = weights[c]
        one = w * sums(4 * c)
        lit = [w * sums(4 * c + 1 + x) for x in range(3)]
        back = 1.0 - inner(v, normal)
        bent = back * one
        lone = grow(lone, one)
        rim_sum = grow(rim_sum, back * bent)
        turn_u = grow(turn_u, bent * inner(v, by_u))
        turn_v = grow(turn_v, bent * inner(v, by_v))
        echo_sum = grow(echo_sum, inner(v, lit))
        flat = [grow(f, x) for f, x in zip(flat, lit)]
    spot = sums(count)
    spots = [sums(count + 1 + x) for x in range(3)]
    edge = p[3] * sharp
    twice = -2.0 * p[6]
    right = [
        p[2] * inner(by_u, flat) + edge * inner(by_u, spots) + twice * turn_u,
        p[2] * inner(by_v, flat) + edge * inner(by_v, spots) + twice * turn_v,
        inner(normal, flat),
        spot,
        p[3] * slope * (inner(normal, spots) - spot),
        lone,
        rim_sum,
        echo_sum,
    ]
    for s in range(parts):

        @pl.when(step == s)
        def _():
            for i in range(8):
                out_refs[s][i] = right[i]
            if s < parts - 1:
                out_refs[s][8] = jnp.zeros((rows, cols), f32)


def ring_total(terms):
    while len(terms) > 1:
        half = len(terms) // 2
        terms = [terms[k] + terms[k + half] for k in range(half)]
    return terms[0]


def solve_kernel(tile_ref, low_ref, par_ref, *refs):
    right_refs, (out_ref, sent_ref) = refs[:-2], refs[-2:]
    lower = {}
    for where, (i, j) in enumerate(ENTRIES):
        lower[j, i] = low_ref[where]
    right = [total(ref[i] for ref in right_refs) - low_ref[36 + i] for i in range(8)]
    forward = []
    for i in range(8):
        accum = right[i]
        for k in range(i):
            accum = accum - lower[i, k] * forward[k]
        forward.append(accum * lower[i, i])
    answer = [None] * 8
    for i in range(7, -1, -1):
        accum = forward[i]
        for k in range(i + 1, 8):
            accum = accum - lower[k, i] * answer[k]
        answer[i] = accum * lower[i, i]
    rows = par_ref.shape[1]
    sent_ref[...] = jnp.zeros(sent_ref.shape, f32)
    for i in range(8):
        fresh = par_ref[i] + answer[i]
        out_ref[i] = fresh
        if i < 2:
            sent_ref[i : i + 1, :] = fresh[0:1]
            sent_ref[2 + i : 3 + i, :] = fresh[rows - 1 : rows]
    sent_ref[4:6, 0:LANES] = ring_total([ref[8, 0:2, 0:LANES] for ref in right_refs])


def relay_kernel(tile_ref, sent_ref, first_ref, out_ref):
    odd = row_is_odd(tile_ref)
    out_ref[...] = sent_ref[...] + first_ref[...]
    out_ref[0:2, :] = jnp.where(odd, first_ref[0:2, :], first_ref[2:4, :])


def rows_kernel(tile_ref, par_ref, first_ref, edge_ref, *refs, last):
    light_refs, (tall_ref, near_ref, far_ref, scr) = refs[:-4], refs[-4:]
    rows, cols = par_ref.shape[1:]
    place = tile_ref[0] // PLACE
    odd, side = row_is_odd(tile_ref), column_is_odd(tile_ref)
    outer = jnp.where(jnp.logical_or(place == 0, place == last), 0.0, 1.0)
    near_ref[...] = jnp.zeros(near_ref.shape, f32)
    far_ref[...] = jnp.zeros(far_ref.shape, f32)
    for k in range(2):
        other = outer * edge_ref[k : k + 1, :]
        scr[7:8, :] = jnp.where(odd, first_ref[2 + k : 3 + k, :], other)
        scr[8 : 8 + rows, :] = par_ref[k]
        scr[8 + rows : 9 + rows, :] = jnp.where(odd, other, first_ref[k : k + 1, :])
        tall = scr[7 : 7 + rows, :] + scr[8 : 8 + rows, :] + scr[9 : 9 + rows, :]
        tall_ref[k] = tall
        left, right = tall[:, 0:LANES], tall[:, cols - LANES : cols]
        near_ref[k * rows : (k + 1) * rows, :] = jnp.where(side, left, right)
        far_ref[k * rows : (k + 1) * rows, :] = jnp.where(side, right, left)
    near_ref[2 * rows : 2 * rows + 2, :] = total(ref[4:6, 0:LANES] for ref in light_refs)


def smooth_kernel(tile_ref, par_ref, tall_ref, sent_ref, near_ref, far_ref, gain_ref, out_ref, gain_out_ref):
    rows, cols = par_ref.shape[1:]
    side = column_is_odd(tile_ref)
    lane = iota((rows, cols), 1)
    for k in range(2):
        at = slice(k * rows, (k + 1) * rows)
        tall = tall_ref[k]
        near_first, near_last = near_ref[at, 0:1], near_ref[at, LANES - 1 : LANES]
        far_first, far_last = far_ref[at, 0:1], far_ref[at, LANES - 1 : LANES]
        before = jnp.where(side, near_last, far_last)
        after = jnp.where(side, far_first, near_first)
        left = jnp.where(lane == 0, before, pltpu.roll(tall, 1, 1))
        right = jnp.where(lane == cols - 1, after, pltpu.roll(tall, cols - 1, 1))
        out_ref[k] = 0.5 * par_ref[k] + (tall + left + right) * (0.5 / 9.0)
    for k in range(2, 8):
        out_ref[k] = par_ref[k]
    light = sent_ref[2 * rows : 2 * rows + 2, 0:LIGHTS] + near_ref[2 * rows : 2 * rows + 2, 0:LIGHTS]
    gains = gain_ref[...]
    gain_out_ref[...] = gains + (light[0:1] - gains * light[1:2]) / (light[1:2] + 1.0)


def smem():
    return pl.BlockSpec(memory_space=pltpu.SMEM)


def vmem():
    return pl.BlockSpec(memory_space=pltpu.VMEM)


def params_of():
    return pltpu.CompilerParams(vmem_limit_bytes=VMEM_BYTES)


def normal_call(par, vis, gains, tables):
    _, rows, cols = par.shape
    parts = cols // LANES
    small = [tables[n] for n in ("near", "cams", "lobe", "mixed", "square")]
    return pl.pallas_call(
        normal_kernel,
        name="normal_factor",
        out_shape=jax.ShapeDtypeStruct((44, rows, cols), f32),
        in_specs=[vmem()] * 8,
        out_specs=vmem(),
        scratch_shapes=[
            pltpu.VMEM((parts, 48 * rows, LANES), f32),
            pltpu.VMEM((parts, 96 * rows, LANES), f32),
            pltpu.VMEM((64, CAMS * LIGHTS), bf16),
            pltpu.VMEM((32, CAMS * LIGHTS), bf16),
            pltpu.VMEM((8 * CAMS, LANES), f32),
            pltpu.VMEM((32, LANES), f32),
        ],
        compiler_params=params_of(),
    )(par, vis, gains, *small)


def sample_call(tile, own, got, gains, tables, pars, vises):
    parts = len(pars)
    samples, rows, _ = own.shape
    cols = pars[0].shape[2]
    held = 2 * samples

    def full(x):
        zeros = (0,) * len(x.shape)
        return pl.BlockSpec(x.shape, lambda s, tile: zeros)

    def chip(s, tile):
        return lax.rem(tile_of(tile) // 2 + (parts - s), parts)

    outs = [jax.ShapeDtypeStruct((9, rows, cols), f32) for _ in range(parts)]
    small = [gains] + [tables[n] for n in ("here", "shade", "plain", "peak", "slab")]
    return pl.pallas_call(
        functools.partial(sample_kernel, parts=parts),
        name="sample_sums",
        out_shape=outs,
        grid_spec=pltpu.PrefetchScalarGridSpec(
            num_scalar_prefetch=1,
            grid=(parts,),
            in_specs=[
                pl.BlockSpec((samples, rows, cols), lambda s, tile: (0, 0, 2 * chip(s, tile) + lax.rem(tile[0], 2))),
                pl.BlockSpec((samples, rows, cols), lambda s, tile: (0, 0, chip(s, tile))),
            ]
            + [full(x) for x in small]
            + [full(x) for x in pars]
            + [full(x) for x in vises],
            out_specs=[full(x) for x in outs],
            scratch_shapes=[
                pltpu.VMEM((8, rows, cols), f32),
                pltpu.VMEM((rows, cols), jnp.int32),
                pltpu.VMEM((cols // LANES, held * rows, LANES), f32),
                pltpu.VMEM((cols // LANES, 72 * rows, LANES), f32),
                pltpu.VMEM((cols // LANES, 32 * rows, LANES), f32),
                pltpu.VMEM((2 * LIGHTS, LANES), f32),
            ],
        ),
        compiler_params=params_of(),
    )(tile, own, got, *small, *pars, *vises)


def pack_kernel(tile_ref, seen_ref, par_ref, vis_ref, send_ref, first_ref, sems):
    parts = sems.shape[0]
    width = send_ref.shape[2] // parts
    copies = []
    for z in range(parts):
        start = pl.multiple_of((2 * z + 1 - lax.rem(tile_ref[0], 2)) * width, LANES)
        copies.append(
            pltpu.make_async_copy(
                seen_ref.at[:, :, pl.ds(start, width)],
                send_ref.at[:, :, z * width : (z + 1) * width],
                sems.at[z],
            )
        )
        copies[z].start()
    first_ref[0:8] = par_ref[...]
    first_ref[8] = vis_ref[...].astype(f32)
    for copy in copies:
        copy.wait()


def pack_call(tile, observed, params, visible, parts):
    far = pl.BlockSpec(memory_space=pltpu.MemorySpace.HBM)
    samples, rows, width = observed.shape
    return pl.pallas_call(
        pack_kernel,
        name="pack",
        out_shape=[
            jax.ShapeDtypeStruct((samples, rows, width // 2), observed.dtype),
            jax.ShapeDtypeStruct((9,) + params.shape[1:], f32),
        ],
        in_specs=[smem(), far, vmem(), vmem()],
        out_specs=[far, vmem()],
        scratch_shapes=[pltpu.SemaphoreType.DMA((parts,))],
        compiler_params=params_of(),
    )(tile, observed, params, visible)


def plain_call(kernel, name, shapes, scratch, tile, *args):
    return pl.pallas_call(
        kernel,
        name=name,
        out_shape=[jax.ShapeDtypeStruct(shape, f32) for shape in shapes],
        in_specs=[smem()] + [vmem()] * len(args),
        out_specs=[vmem()] * len(shapes),
        scratch_shapes=[pltpu.VMEM(shape, f32) for shape in scratch],
        compiler_params=params_of(),
    )(tile, *args)


def pairs(count, start):
    out = []
    for i in range(start, count - 1, 2):
        out += [(i, i + 1), (i + 1, i)]
    return out


def settle(tile, low, params, moved, gains):
    _, rows, cols = params.shape
    grps, tiles = lax.axis_size("grp"), lax.axis_size("tile")
    strip = (8, cols)
    params, sent = plain_call(solve_kernel, "solve", [params.shape, strip], [], tile, low, params, *moved)
    first = lax.ppermute(sent, "grp", pairs(grps, 0))
    if grps == 4:
        (relay,) = plain_call(relay_kernel, "relay", [strip], [], tile, sent, first)
        edge = lax.ppermute(relay, "grp", [(i, i ^ 2) for i in range(grps)])
        lights = [relay, edge]
    else:
        second = lax.ppermute(sent, "grp", pairs(grps, 1))
        odd = lax.axis_index("grp") % 2 == 1
        edge = jnp.where(odd, second, jnp.roll(second, -2, axis=0))
        light = sent + first
        bit = 2
        while bit < grps:
            light = light + lax.ppermute(light, "grp", [(i, i ^ bit) for i in range(grps)])
            bit *= 2
        lights = [light]
    patch = (2 * rows + 8, LANES)
    tall, sent, other = plain_call(
        functools.partial(rows_kernel, last=grps - 1), "rows", [(2, rows, cols), patch, patch], [(24, cols)],
        tile, params, first, edge, *lights,
    )
    far = lax.ppermute(other, "tile", pairs(tiles, 1))
    near = lax.ppermute(sent, "tile", pairs(tiles, 0))
    return plain_call(
        smooth_kernel, "smooth", [params.shape, gains.shape], [], tile, params, tall, sent, near, far, gains
    )


def exact(a, b, sides):
    return lax.dot_general(
        a, b, (sides, ((), ())), precision=lax.Precision.HIGHEST, preferred_element_type=f32
    )


def iota(shape, axis):
    return lax.broadcasted_iota(jnp.int32, shape, axis)


def pick(test):
    return jnp.where(test, 1.0, 0.0).astype(f32)


def setup_kernel(
    tile_ref, light_ref, view_ref,
    near_ref, cams_ref, lobe_ref, mixed_ref, square_ref,
    here_ref, shade_ref, plain_ref, peak_ref, slab_ref, light_scr, view_scr,
):
    samples = lobe_ref.shape[0]
    held = here_ref.shape[0]
    cams = held // LIGHTS
    first = (tile_of(tile_ref) // 2) * cams

    def unit(raw_ref, scr):
        scr[...] = jnp.zeros(scr.shape, f32)
        scr[0:3, :] = raw_ref[...]
        scr[2:3, :] = scr[2:3, :] + lift_z
        lifted = scr[...]
        return lifted / jnp.sqrt(jnp.sum(lifted * lifted, axis=0, keepdims=True))

    lights = unit(light_ref, light_scr)
    views = unit(view_ref, view_scr)
    near = jnp.where(iota(lights.shape, 0) == 3, 1.0, lights)
    near_ref[...] = near
    cams_ref[...] = views

    def across(count, start):
        at_light = pick(iota((LIGHTS, count), 1) % LIGHTS == iota((LIGHTS, count), 0))
        at_view = pick(iota((CAMS, count), 1) // LIGHTS + start == iota((CAMS, count), 0))
        wide = exact(near, at_light, ((1,), (0,)))
        view = exact(views, at_view, ((1,), (0,)))
        row = iota((8, count), 0)
        raw = jnp.where(row < 3, wide + view, 0.0)
        half = raw / jnp.sqrt(jnp.sum(raw * raw, axis=0, keepdims=True))
        echo = jnp.sum(wide * view, axis=0, keepdims=True)
        return wide, half, echo

    def down(count, start):
        at_light = pick(iota((count, LIGHTS), 0) % LIGHTS == iota((count, LIGHTS), 1))
        at_view = pick(iota((count, CAMS), 0) // LIGHTS + start == iota((count, CAMS), 1))
        tall = exact(at_light, near, ((1,), (1,)))
        view = exact(at_view, views, ((1,), (1,)))
        lane = iota((count, 8), 1)
        raw = jnp.where(lane < 3, tall + view, 0.0)
        half = raw / jnp.sqrt(jnp.sum(raw * raw, axis=1, keepdims=True))
        half = jnp.where(lane == 3, 1.0, half)
        echo = jnp.sum(tall * view, axis=1, keepdims=True)
        return half, jnp.where(lane == 4, echo, tall)

    def spread(values, width, depth, order):
        lane = iota((8, depth), 1)
        out = None
        for which in range(max(order) + 1):
            head = values.astype(bf16)
            values = values - head.astype(f32)
            group = None
            for g, k in enumerate(order):
                if k == which:
                    hit = lane // width == g
                    group = hit if group is None else jnp.logical_or(group, hit)
            place = pick(jnp.logical_and(group, lane % width == iota((8, depth), 0)))
            place = jnp.where(iota((8, depth), 0) < width, place, 0.0).astype(bf16)
            got = dot(head, place)
            out = got if out is None else out + got
        return out

    wide, half, echo = across(samples, 0)
    high = [jnp.ones((1, samples), f32)] + [half[k : k + 1] for k in range(3)]
    low = [wide[k : k + 1] for k in range(3)] + [echo]
    which = iota((1, samples), 1) // LIGHTS % 4
    for i in range(4):
        for j in range(4):
            mixed_ref[4 * i + j : 4 * i + j + 1, :] = high[i] * low[j]
            mixed_ref[16 + 4 * i + j : 17 + 4 * i + j, :] = jnp.where(which == i, high[j], 0.0)
    at = 0
    square_ref[8:16, :] = jnp.zeros((8, samples), f32)
    for i in range(4):
        for j in range(i, 4):
            square_ref[at : at + 1, :] = high[i] * high[j]
            at += 1

    depth = lobe_ref.shape[1]
    half, _ = down(samples, 0)
    hot = pick(iota((samples, depth), 0) // LIGHTS + 24 == iota((samples, depth), 1))
    lobe_ref[...] = (spread(half, 4, depth, (0, 0, 1, 0, 1, 2)) + hot).astype(bf16)

    half, tall = down(held, first)
    cam = iota((held, 32), 0) // LIGHTS
    lane = iota((held, 32), 1)
    hot = pick(cam + 24 == lane)
    here_ref[...] = (spread(half, 4, 32, (0, 0, 1, 0, 1, 2)) + hot).astype(bf16)
    hot = pick(cam + 15 == lane) + pick(cam + (15 + cams) == lane)
    shade_ref[...] = (spread(tall, 5, 32, (0, 0, 1)) + hot).astype(bf16)

    wide, half, _ = across(held, first)
    peak_ref[...] = jnp.zeros(peak_ref.shape, f32)
    peak_ref[0:1, :] = jnp.ones((1, held), f32)
    plain_ref[...] = jnp.zeros(plain_ref.shape, f32)
    for k in range(3):
        peak_ref[k + 1 : k + 2, :] = half[k : k + 1]
    which = iota((1, held), 1) // LIGHTS
    for c in range(cams):
        plain_ref[4 * c : 4 * c + 1, :] = pick(which == c)
        for k in range(3):
            plain_ref[4 * c + 1 + k : 4 * c + 2 + k, :] = jnp.where(which == c, wide[k : k + 1], 0.0)
        mine = jnp.sum(jnp.where(iota(views.shape, 1) == first + c, views, 0.0), axis=1, keepdims=True)
        slab_ref[8 * c : 8 * c + 8, :] = jnp.broadcast_to(mine, (8, LANES))


TABLES = ("near", "cams", "lobe", "mixed", "square", "here", "shade", "plain", "peak", "slab")


def setup_call(tile, light_directions, view_dirs, held):
    samples = CAMS * LIGHTS
    cams = held // LIGHTS
    count = max(8, 4 * cams)
    shapes = [
        ((8, LIGHTS), f32), ((8, CAMS), f32), ((samples, 48), bf16), ((32, samples), f32),
        ((16, samples), f32), ((held, 32), bf16), ((held, 32), bf16), ((count, held), f32),
        ((8, held), f32), ((8 * cams, LANES), f32),
    ]
    outs = pl.pallas_call(
        setup_kernel,
        name="tables",
        out_shape=[jax.ShapeDtypeStruct(a, b) for a, b in shapes],
        in_specs=[smem(), vmem(), vmem()],
        out_specs=[vmem()] * len(shapes),
        scratch_shapes=[pltpu.VMEM((8, LIGHTS), f32), pltpu.VMEM((8, CAMS), f32)],
        compiler_params=params_of(),
    )(tile, light_directions, view_dirs)
    return dict(zip(TABLES, outs))


def shifted(x, by, nz):
    return lax.ppermute(x, "tile", [(2 * z + c, 2 * ((z + by) % nz) + c) for z in range(nz) for c in range(2)])


def on_device(observed, visible, params_start, light_directions, view_dirs, gains_start):
    samples = observed.shape[0]
    tiles = lax.axis_size("tile")
    nz = tiles // 2
    tile = lax.axis_index("tile")
    held = 2 * samples

    here = (tile + PLACE * lax.axis_index("grp")).astype(jnp.int32).reshape(1)
    send, first = pack_call(here, observed, params_start, visible, nz)
    got = lax.ppermute(send, "tile", [(i, i ^ 1) for i in range(tiles)])
    blocks = [first] + [shifted(first, s, nz) for s in range(1, nz)]
    vises = blocks
    tables = setup_call(here, light_directions, view_dirs, held)

    params = params_start
    gains = gains_start.reshape(1, LIGHTS)
    for iteration in range(ITERS):
        low = normal_call(params, visible, gains, tables)
        rights = sample_call(here, observed, got, gains, tables, blocks, vises)
        moved = [rights[0]] + [shifted(rights[s], -s, nz) for s in range(1, nz)]
        params, gains = settle(here, low, params, moved, gains)
        if iteration + 1 < ITERS:
            blocks = [params] + [shifted(params, s, nz) for s in range(1, nz)]
    return params, gains.reshape(LIGHTS)


def solution(mesh):
    return jax.shard_map(
        on_device,
        mesh=mesh,
        in_specs=(P("tile", "grp", None), P("grp", "tile"), P(None, "grp", "tile"), P(), P(), P()),
        out_specs=(P(None, "grp", "tile"), P()),
        check_vma=False,
    )
```

```python
import functools

import jax
import jax.numpy as jnp
from jax import lax
from jax.experimental import pallas as pl
from jax.experimental.pallas import tpu as pltpu
from jax.sharding import PartitionSpec as P

CAMS = 16
LIGHTS = 32
ITERS = 2

damping = 4.0
lift_z = 1.6
hidden = 1024.0
f32 = jnp.float32
bf16 = jnp.bfloat16
LANES = 128
VMEM_BYTES = 16 * 1024 * 1024
LINEAR = (2, 3, 5, 6, 7)
ENTRIES = [(i, j) for i in range(8) for j in range(i, 8)]


PLACE = 4096


def tile_of(ref):
    return lax.rem(ref[0], PLACE)


def row_is_odd(ref):
    return lax.rem(ref[0] // PLACE, 2) == 1


def column_is_odd(ref):
    return lax.rem(ref[0], 2) == 1


def split_value(x, count):
    pieces = []
    for _ in range(count - 1):
        head = x.astype(bf16).astype(f32)
        pieces.append(head)
        x = x - head
    pieces.append(x)
    return pieces


def split_pair(x):
    head = x.astype(bf16)
    return head, (x - head.astype(f32)).astype(bf16)


def dot(a, b):
    return jnp.dot(a, b, preferred_element_type=f32)


def total(terms):
    terms = list(terms)
    out = terms[0]
    for t in terms[1:]:
        out = out + t
    return out


def inner(a, b):
    return total(x * y for x, y in zip(a, b))


def texel_forms(p):
    tu, tv, diffuse, spec, raw, ambient, rim, retro = p
    q = 1.0 / jnp.sqrt(1.0 + tu * tu + tv * tv)
    nx, ny, nz = tu * q, tv * q, q
    side = -(nx * ny) * q
    by_u = ((1.0 - nx * nx) * q, side, -(nz * nx) * q)
    by_v = (side, (1.0 - ny * ny) * q, -(nz * ny) * q)
    sigma = 1.0 / (1.0 + jnp.exp(-raw))
    sharp = 1.0 + 20.0 * sigma
    slope = 20.0 * sigma * (1.0 - sigma)
    return (nx, ny, nz), by_u, by_v, sharp, slope


def seen(mask, c):
    return jnp.bitwise_and(jnp.right_shift(mask, c), 1).astype(f32)


def put_slab(ref, k, value):
    rows, cols = value.shape
    for h in range(cols // LANES):
        ref[h, k * rows : (k + 1) * rows, :] = value[:, h * LANES : (h + 1) * LANES]


def get_slab(ref, k, rows):
    return jnp.concatenate([ref[h, k * rows : (k + 1) * rows, :] for h in range(ref.shape[0])], axis=1)


def get_rows(ref, start, count, stride):
    return jnp.concatenate([ref[h, pl.ds(start, count, stride=stride), :] for h in range(ref.shape[0])], axis=1)


def put_rows(ref, start, stride, value):
    count, cols = value.shape
    for h in range(cols // LANES):
        ref[h, pl.ds(start, count, stride=stride), :] = value[:, h * LANES : (h + 1) * LANES]


def gain_columns(gains):
    same = pick(iota((LIGHTS, LIGHTS), 0) == iota((LIGHTS, LIGHTS), 1))
    tall = exact(same, jnp.broadcast_to(gains, (8, LIGHTS)), ((1,), (1,)))
    return jnp.broadcast_to(tall[:, 0:1], (LIGHTS, LANES))


def eights(x):
    return total(x[i : i + 8] for i in range(0, x.shape[0], 8))


def put_lobe_rows(slab, normal, sharp):
    base = [sharp * normal[0], sharp * normal[1], sharp * normal[2], -sharp]
    parts = [split_value(x, 3) for x in base]
    row = 0
    for which in (0, 1, 0, 2, 1, 0):
        for part in parts:
            slab(row, part[which])
            row += 1
    return row


def normal_kernel(
    par_ref, vis_ref, gain_ref, near_ref, cams_ref, lobe_ref, mixed_ref, tall_ref, out_ref,
    rows_ref, sums_ref, mixed_scr, gain_scr, cam_scr, gram_scr, lobe_scr,
):
    rows, cols = par_ref.shape[1], par_ref.shape[2]
    depth = lobe_ref.shape[1]
    chunk = 4 * LIGHTS
    chunks = CAMS // 4

    near, views = near_ref[...], cams_ref[...]
    gain2 = gain_ref[...] * gain_ref[...]
    grams = [jnp.sum(near * near[i : i + 1] * gain2, axis=1, keepdims=True) for i in range(4)]
    for i in range(4):
        gram_scr[8 * i : 8 * i + 8, :] = jnp.broadcast_to(grams[i], (8, LANES))
    spread = [total(grams[i][k : k + 1] * views[k : k + 1] for k in range(3)) for i in range(4)]
    echo_sq = total(spread[k] * views[k : k + 1] for k in range(3))
    row = iota(views.shape, 0)
    full = jnp.where(row == 3, echo_sq, jnp.where(row == 4, spread[3], views))
    for c in range(CAMS):
        cam_scr[8 * c : 8 * c + 8, :] = jnp.broadcast_to(full[:, c : c + 1], (8, LANES))

    gain_scr[...] = gain_columns(gain2)
    across = CAMS * LIGHTS
    at_light = pick(iota((LIGHTS, across), 1) % LIGHTS == iota((LIGHTS, across), 0))
    gain2 = exact(jnp.broadcast_to(gain2, (8, LIGHTS)), at_light, ((1,), (0,)))[0:1]
    for src, dst in ((mixed_ref, mixed_scr),):
        head, tail = split_pair(src[...] * gain2)
        count = src.shape[0]
        for ch in range(chunks):
            part = slice(ch * chunk, (ch + 1) * chunk)
            first = slice(2 * ch * chunk, (2 * ch + 1) * chunk)
            second = slice((2 * ch + 1) * chunk, (2 * ch + 2) * chunk)
            dst[0:count, first] = head[:, part]
            dst[0:count, second] = head[:, part]
            dst[count : 2 * count, first] = tail[:, part]
            dst[count : 2 * count, second] = jnp.zeros((count, chunk), bf16)

    def slab(k, value):
        put_slab(rows_ref, k, value)

    p = [par_ref[i] for i in range(8)]
    normal, _, _, sharp, _ = texel_forms(p)
    used = put_lobe_rows(slab, normal, sharp)
    mask = vis_ref[...]
    for c in range(CAMS):
        slab(used + c, (seen(mask, c) - 1.0) * hidden)
    for k in range(used + CAMS, depth):
        slab(k, jnp.zeros((rows, cols), f32))

    quads = [(i, j) for i in range(4) for j in range(i, 4)]

    def one_row(r):
        texel = get_rows(rows_ref, r, depth, rows).astype(bf16)
        mixed = jnp.zeros((16, cols), f32)
        bent = {(h, ij): None for h in range(cols // LANES) for ij in quads}
        for ch in range(chunks):
            for c in range(4):
                part = slice(ch * chunk + c * LIGHTS, ch * chunk + (c + 1) * LIGHTS)
                lobe = jnp.exp(dot(lobe_ref[part, :], texel))
                head, tail = split_pair(lobe)
                lobe_scr[r, ch, c * LIGHTS : (c + 1) * LIGHTS, :] = head
                lobe_scr[r, ch, chunk + c * LIGHTS : chunk + (c + 1) * LIGHTS, :] = tail
                tall = [None] + [tall_ref[k, part, :] for k in range(3)]
                for h in range(cols // LANES):
                    lobe_h = lobe[:, h * LANES : (h + 1) * LANES]
                    single = [lobe_h * lobe_h * gain_scr[...]]
                    single += [single[0] * tall[k] for k in (1, 2, 3)]
                    for i, j in quads:
                        value = eights(single[j] if i == 0 else single[i] * tall[j])
                        old = bent[h, (i, j)]
                        bent[h, (i, j)] = value if old is None else old + value
            at = slice(2 * ch * chunk, (2 * ch + 2) * chunk)
            both = dot(mixed_scr[:, at], lobe_scr[r, ch])
            got = both[0:32] + both[32:64]
            mixed = mixed + got[0:16]
            put_rows(sums_ref, (32 + 16 * ch) * rows + r, rows, got[16:32])
        put_rows(sums_ref, r, rows, mixed)
        for h in range(cols // LANES):
            for k, ij in enumerate(quads):
                line = (16 + k) * rows + r
                sums_ref[h, line : line + 1, :] = jnp.sum(bent[h, ij], axis=0, keepdims=True)

    for r in range(rows):
        one_row(r)

    def one_part(h, carry):
        at = pl.ds(pl.multiple_of(h * LANES, LANES), LANES)

        def cam(c, i):
            return cam_scr[8 * c + i : 8 * c + i + 1, :]

        def sums(k):
            return sums_ref[h, k * rows : (k + 1) * rows, :]

        p = [par_ref[i, :, at] for i in range(8)]
        mask = vis_ref[:, at]
        normal, by_u, by_v, sharp, slope = texel_forms(p)
        diffuse, spec, rim = p[2], p[3], p[6]
        zero = jnp.zeros((rows, LANES), f32)
        gam = {i: zero for i in (0, 1, 5, 6)}
        own = {(i, j): zero for i in (0, 1, 5, 6) for j in (0, 1, 5, 6) if i <= j and j != 5 and i != 5}
        lit = {i: zero for i in (0, 1, 5, 6)}
        grid = {(i, k): zero for i in (0, 1, 5, 6) for k in range(4)}
        echo_sq = zero
        view_sum = [zero, zero, zero]
        for c in range(CAMS):
            w = seen(mask, c)
            v = [cam(c, i) for i in range(3)]
            back = 1.0 - inner(v, normal)
            turn = (-2.0 * rim) * back
            shape = {0: turn * inner(v, by_u), 1: turn * inner(v, by_v), 6: back * back}
            weighted = {i: w * shape[i] for i in shape}
            weighted[5] = w
            for i in gam:
                gam[i] = gam[i] + weighted[i]
                lit[i] = lit[i] + weighted[i] * cam(c, 4)
            for i, j in own:
                own[i, j] = own[i, j] + weighted[i] * shape[j]
            echo_sq = echo_sq + w * cam(c, 3)
            view_sum = [s + w * x for s, x in zip(view_sum, v)]
            for k in range(4):
                peak = sums(32 + 4 * c + k)
                for i in (0, 1, 6):
                    grid[i, k] = grid[i, k] + shape[i] * peak
                grid[5, k] = grid[5, k] + peak
        own[5, 5] = gam[5]
        for i in (0, 1):
            own[i, 5] = gam[i]
        own[5, 6] = gam[6]

        def gram(i, j):
            return gram_scr[8 * i + j : 8 * i + j + 1, :]

        entries = {ij: None for ij in ENTRIES}

        def add(i, j, value):
            ij = (min(i, j), max(i, j))
            entries[ij] = value if entries[ij] is None else entries[ij] + value

        def cross(i, j, value):
            add(i, j, value + value if i == j else value)

        flat = {0: [diffuse * x for x in by_u], 1: [diffuse * x for x in by_v], 2: list(normal)}
        edge = spec * sharp
        tilt = spec * slope
        glow = {
            0: {1 + k: edge * by_u[k] for k in range(3)},
            1: {1 + k: edge * by_v[k] for k in range(3)},
            3: {0: None},
            4: {0: -tilt, 1: tilt * normal[0], 2: tilt * normal[1], 3: tilt * normal[2]},
        }

        def combine(coefs, values):
            return total(values[k] if x is None else x * values[k] for k, x in coefs.items())

        count = gam[5]
        spread = {i: [total(gram(r, k) * flat[i][k] for k in range(3)) for r in range(3)] for i in flat}
        reach = {i: total(gram(3, k) * flat[i][k] for k in range(3)) for i in flat}
        view_spread = [total(gram(r, k) * view_sum[k] for k in range(3)) for r in range(3)]
        for i in flat:
            for j in flat:
                if i <= j:
                    add(i, j, count * inner(flat[j], spread[i]))
            for j in gam:
                cross(i, j, reach[i] * gam[j])
            cross(i, 7, inner(flat[i], view_spread))
        for i, j in own:
            add(i, j, gram(3, 3) * own[i, j])
        for i in lit:
            cross(i, 7, lit[i])
        add(7, 7, echo_sq)
        for j in glow:
            for i in flat:
                cross(i, j, total(flat[i][x] * combine(glow[j], {k: sums(4 * k + x) for k in glow[j]}) for x in range(3)))
            for i in gam:
                cross(i, j, combine(glow[j], {k: grid[i, k] for k in glow[j]}))
            cross(j, 7, combine(glow[j], {k: sums(4 * k + 3) for k in glow[j]}))
        packed = {}
        where = 0
        for i in range(4):
            for j in range(i, 4):
                packed[i, j] = packed[j, i] = where
                where += 1
        for i in glow:
            for j in glow:
                if i <= j:
                    half = {k: combine(glow[j], {x: sums(16 + packed[k, x]) for x in glow[j]}) for k in glow[i]}
                    add(i, j, combine(glow[i], half))

        def entry(i, j):
            return entries[min(i, j), max(i, j)]

        for i in range(8):
            out_ref[36 + i, :, at] = total(entry(i, j) * p[j] for j in LINEAR)
        lower = {}
        for j in range(8):
            accum = entries[j, j] + damping
            for k in range(j):
                accum = accum - lower[j, k] * lower[j, k]
            inverse = lax.rsqrt(accum)
            lower[j, j] = inverse
            for i in range(j + 1, 8):
                accum = entries[j, i]
                for k in range(j):
                    accum = accum - lower[i, k] * lower[j, k]
                lower[i, j] = accum * inverse
        for where, (i, j) in enumerate(ENTRIES):
            out_ref[where, :, at] = lower[j, i]
        return carry

    lax.fori_loop(0, cols // LANES, one_part, 0)


def sample_kernel(
    tile_ref, own_ref, got_ref, gain_ref, lobe_ref, shade_ref, plain_ref, tall_ref, slab_ref, *refs, parts
):
    par_refs, vis_refs = refs[:parts], refs[parts : 2 * parts]
    out_refs = refs[2 * parts : 3 * parts]
    par_scr, vis_scr, obs_scr, rows_ref, sums_ref, light_scr, gain_scr, plain_scr, flat_scr = refs[3 * parts :]
    step = pl.program_id(0)
    samples, rows, cols = own_ref.shape
    held = 2 * samples
    cams = held // LIGHTS
    for s in range(parts):

        @pl.when(step == s)
        def _():
            par_scr[...] = par_refs[s][0:8]
            vis_scr[...] = vis_refs[s][8].astype(jnp.int32)

    core = tile_of(tile_ref) % 2
    mine = pl.multiple_of(core * (samples * rows), rows)
    theirs = pl.multiple_of((1 - core) * (samples * rows), rows)
    for h in range(cols // LANES):
        lanes = slice(h * LANES, (h + 1) * LANES)
        for src, at in ((own_ref, mine), (got_ref, theirs)):
            obs_scr[h, pl.ds(at, samples * rows), :] = src[:, :, lanes].astype(f32).reshape(samples * rows, LANES)

    def slab(k, value):
        put_slab(rows_ref, k, value)

    p = [par_scr[i] for i in range(8)]
    mask = vis_scr[...]
    normal, by_u, by_v, sharp, slope = texel_forms(p)
    base = (tile_of(tile_ref) // 2) * cams

    def cam(c, i):
        return slab_ref[8 * c + i : 8 * c + i + 1, :][:, 0:1]

    used = put_lobe_rows(slab, normal, sharp)
    weights = [seen(mask, base + c) for c in range(cams)]
    for c in range(cams):
        slab(used + c, (weights[c] - 1.0) * hidden)
        slab(65 + c, weights[c])
    for k in range(used + cams, 32):
        slab(k, jnp.zeros((rows, cols), f32))
    shade = [p[2] * normal[0], p[2] * normal[1], p[2] * normal[2], p[5], p[7]]
    pieces = [split_value(x, 2) for x in shade]
    at = 32
    for which in (0, 1, 0):
        for piece in pieces:
            slab(at, piece[which])
            at += 1
    for c in range(cams):
        back = 1.0 - inner([cam(c, i) for i in range(3)], normal)
        head, tail = split_value(p[6] * (back * back), 2)
        slab(at + c, head)
        slab(at + cams + c, tail)
    for k in range(at + 2 * cams, 64):
        slab(k, jnp.zeros((rows, cols), f32))
    slab(64, p[3])

    @pl.when(step == 0)
    def _():
        at_light = pick(iota((LIGHTS, held), 1) % LIGHTS == iota((LIGHTS, held), 0))
        gains = exact(jnp.broadcast_to(gain_ref[...], (8, LIGHTS)), at_light, ((1,), (0,)))[0:1]
        plain_scr[...] = jnp.concatenate(split_value(plain_ref[...] * gains, 2), axis=0).astype(bf16)
        gain_scr[...] = gain_columns(gain_ref[...])

    count = plain_ref.shape[0]

    def fold(x):
        return total(x[:, k * LANES : (k + 1) * LANES] for k in range(cols // LANES))

    def one_row(r, lift, energy):
        texel = get_rows(rows_ref, r, 32, rows).astype(bf16)
        tint = get_rows(rows_ref, 32 * rows + r, 32, rows).astype(bf16)
        misc = get_rows(rows_ref, 64 * rows + r, 8, rows)
        peak = {}
        for c in range(cams):
            part = slice(c * LIGHTS, (c + 1) * LIGHTS)
            lobe = jnp.exp(dot(lobe_ref[part, :], texel))
            full = dot(shade_ref[part, :], tint) + misc[0:1] * lobe
            obs = get_rows(obs_scr, c * LIGHTS * rows + r, LIGHTS, rows)
            kept = full * misc[1 + c : 2 + c]
            lift = lift + fold(kept * obs)
            energy = energy + fold(kept * full)
            flat_scr[r, part, :] = obs.astype(bf16)
            lit = obs * lobe
            for h in range(cols // LANES):
                base = lit[:, h * LANES : (h + 1) * LANES] * gain_scr[...]
                for k in range(4):
                    value = eights(base if k == 0 else base * tall_ref[k - 1, part, :])
                    peak[h, k] = value if c == 0 else peak[h, k] + value
        both = dot(plain_scr[...], flat_scr[r])
        put_rows(sums_ref, r, rows, both[0:count] + both[count : 2 * count])
        for h, k in peak:
            line = (count + k) * rows + r
            sums_ref[h, line : line + 1, :] = jnp.sum(peak[h, k], axis=0, keepdims=True)
        return lift, energy

    lift = energy = jnp.zeros((LIGHTS, LANES), f32)
    for r in range(rows):
        lift, energy = one_row(r, lift, energy)

    @pl.when(step == 0)
    def _():
        light_scr[0:LIGHTS, :] = lift
        light_scr[LIGHTS : 2 * LIGHTS, :] = energy

    @pl.when(step != 0)
    def _():
        light_scr[0:LIGHTS, :] = light_scr[0:LIGHTS, :] + lift
        light_scr[LIGHTS : 2 * LIGHTS, :] = light_scr[LIGHTS : 2 * LIGHTS, :] + energy

    @pl.when(step == parts - 1)
    def _():
        out_refs[parts - 1][8] = jnp.zeros((rows, cols), f32)
        for k in range(2):
            part = light_scr[k * LIGHTS : (k + 1) * LIGHTS, :]
            line = exact(jnp.ones((8, LANES), f32), part, ((1,), (1,)))[0:1]
            for ref in out_refs:
                ref[8, k : k + 1, 0:LIGHTS] = line

    def sums(k):
        return get_slab(sums_ref, k, rows)

    flat = [None, None, None]
    lone, rim_sum, echo_sum, turn_u, turn_v = None, None, None, None, None

    def grow(old, new):
        return new if old is None else old + new

    for c in range(cams):
        v = [cam(c, i) for i in range(3)]
        w = weights[c]
        one = w * sums(4 * c)
        lit = [w * sums(4 * c + 1 + x) for x in range(3)]
        back = 1.0 - inner(v, normal)
        bent = back * one
        lone = grow(lone, one)
        rim_sum = grow(rim_sum, back * bent)
        turn_u = grow(turn_u, bent * inner(v, by_u))
        turn_v = grow(turn_v, bent * inner(v, by_v))
        echo_sum = grow(echo_sum, inner(v, lit))
        flat = [grow(f, x) for f, x in zip(flat, lit)]
    spot = sums(count)
    spots = [sums(count + 1 + x) for x in range(3)]
    edge = p[3] * sharp
    twice = -2.0 * p[6]
    right = [
        p[2] * inner(by_u, flat) + edge * inner(by_u, spots) + twice * turn_u,
        p[2] * inner(by_v, flat) + edge * inner(by_v, spots) + twice * turn_v,
        inner(normal, flat),
        spot,
        p[3] * slope * (inner(normal, spots) - spot),
        lone,
        rim_sum,
        echo_sum,
    ]
    for s in range(parts):

        @pl.when(step == s)
        def _():
            for i in range(8):
                out_refs[s][i] = right[i]
            if s < parts - 1:
                out_refs[s][8] = jnp.zeros((rows, cols), f32)


def ring_total(terms):
    while len(terms) > 1:
        half = len(terms) // 2
        terms = [terms[k] + terms[k + half] for k in range(half)]
    return terms[0]


def solve_kernel(tile_ref, low_ref, par_ref, *refs):
    right_refs, (out_ref, sent_ref) = refs[:-2], refs[-2:]
    lower = {}
    for where, (i, j) in enumerate(ENTRIES):
        lower[j, i] = low_ref[where]
    right = [total(ref[i] for ref in right_refs) - low_ref[36 + i] for i in range(8)]
    forward = []
    for i in range(8):
        accum = right[i]
        for k in range(i):
            accum = accum - lower[i, k] * forward[k]
        forward.append(accum * lower[i, i])
    answer = [None] * 8
    for i in range(7, -1, -1):
        accum = forward[i]
        for k in range(i + 1, 8):
            accum = accum - lower[k, i] * answer[k]
        answer[i] = accum * lower[i, i]
    rows = par_ref.shape[1]
    sent_ref[...] = jnp.zeros(sent_ref.shape, f32)
    for i in range(8):
        fresh = par_ref[i] + answer[i]
        out_ref[i] = fresh
        if i < 2:
            sent_ref[i : i + 1, :] = fresh[0:1]
            sent_ref[2 + i : 3 + i, :] = fresh[rows - 1 : rows]
    sent_ref[4:6, 0:LANES] = ring_total([ref[8, 0:2, 0:LANES] for ref in right_refs])


def relay_kernel(tile_ref, sent_ref, first_ref, out_ref):
    odd = row_is_odd(tile_ref)
    out_ref[...] = sent_ref[...] + first_ref[...]
    out_ref[0:2, :] = jnp.where(odd, first_ref[0:2, :], first_ref[2:4, :])


def rows_kernel(tile_ref, par_ref, first_ref, edge_ref, *refs, last):
    light_refs, (tall_ref, near_ref, far_ref, scr) = refs[:-4], refs[-4:]
    rows, cols = par_ref.shape[1:]
    place = tile_ref[0] // PLACE
    odd, side = row_is_odd(tile_ref), column_is_odd(tile_ref)
    outer = jnp.where(jnp.logical_or(place == 0, place == last), 0.0, 1.0)
    near_ref[...] = jnp.zeros(near_ref.shape, f32)
    far_ref[...] = jnp.zeros(far_ref.shape, f32)
    for k in range(2):
        other = outer * edge_ref[k : k + 1, :]
        scr[7:8, :] = jnp.where(odd, first_ref[2 + k : 3 + k, :], other)
        scr[8 : 8 + rows, :] = par_ref[k]
        scr[8 + rows : 9 + rows, :] = jnp.where(odd, other, first_ref[k : k + 1, :])
        tall = scr[7 : 7 + rows, :] + scr[8 : 8 + rows, :] + scr[9 : 9 + rows, :]
        tall_ref[k] = tall
        left, right = tall[:, 0:LANES], tall[:, cols - LANES : cols]
        near_ref[k * rows : (k + 1) * rows, :] = jnp.where(side, left, right)
        far_ref[k * rows : (k + 1) * rows, :] = jnp.where(side, right, left)
    near_ref[2 * rows : 2 * rows + 2, :] = total(ref[4:6, 0:LANES] for ref in light_refs)


def smooth_kernel(tile_ref, par_ref, tall_ref, sent_ref, near_ref, far_ref, gain_ref, out_ref, gain_out_ref):
    rows, cols = par_ref.shape[1:]
    side = column_is_odd(tile_ref)
    lane = iota((rows, cols), 1)
    for k in range(2):
        at = slice(k * rows, (k + 1) * rows)
        tall = tall_ref[k]
        near_first, near_last = near_ref[at, 0:1], near_ref[at, LANES - 1 : LANES]
        far_first, far_last = far_ref[at, 0:1], far_ref[at, LANES - 1 : LANES]
        before = jnp.where(side, near_last, far_last)
        after = jnp.where(side, far_first, near_first)
        left = jnp.where(lane == 0, before, pltpu.roll(tall, 1, 1))
        right = jnp.where(lane == cols - 1, after, pltpu.roll(tall, cols - 1, 1))
        out_ref[k] = 0.5 * par_ref[k] + (tall + left + right) * (0.5 / 9.0)
    for k in range(2, 8):
        out_ref[k] = par_ref[k]
    light = sent_ref[2 * rows : 2 * rows + 2, 0:LIGHTS] + near_ref[2 * rows : 2 * rows + 2, 0:LIGHTS]
    gains = gain_ref[...]
    gain_out_ref[...] = gains + (light[0:1] - gains * light[1:2]) / (light[1:2] + 1.0)


def smem():
    return pl.BlockSpec(memory_space=pltpu.SMEM)


def vmem():
    return pl.BlockSpec(memory_space=pltpu.VMEM)


def params_of():
    return pltpu.CompilerParams(vmem_limit_bytes=VMEM_BYTES)


def normal_call(par, vis, gains, tables):
    _, rows, cols = par.shape
    parts = cols // LANES
    small = [tables[n] for n in ("near", "cams", "lobe", "mixed", "tall")]
    return pl.pallas_call(
        normal_kernel,
        name="normal_factor",
        out_shape=jax.ShapeDtypeStruct((44, rows, cols), f32),
        in_specs=[vmem()] * 8,
        out_specs=vmem(),
        scratch_shapes=[
            pltpu.VMEM((parts, 48 * rows, LANES), f32),
            pltpu.VMEM((parts, 96 * rows, LANES), f32),
            pltpu.VMEM((64, 2 * CAMS * LIGHTS), bf16),
            pltpu.VMEM((LIGHTS, LANES), f32),
            pltpu.VMEM((8 * CAMS, LANES), f32),
            pltpu.VMEM((32, LANES), f32),
            pltpu.VMEM((rows, 4, 8 * LIGHTS, cols), bf16),
        ],
        compiler_params=params_of(),
    )(par, vis, gains, *small)


def sample_call(tile, own, got, gains, tables, pars, vises):
    parts = len(pars)
    samples, rows, _ = own.shape
    cols = pars[0].shape[2]
    held = 2 * samples

    def full(x):
        zeros = (0,) * len(x.shape)
        return pl.BlockSpec(x.shape, lambda s, tile: zeros)

    def chip(s, tile):
        return lax.rem(tile_of(tile) // 2 + (parts - s), parts)

    outs = [jax.ShapeDtypeStruct((9, rows, cols), f32) for _ in range(parts)]
    small = [gains] + [tables[n] for n in ("here", "shade", "plain", "near_tall", "slab")]
    return pl.pallas_call(
        functools.partial(sample_kernel, parts=parts),
        name="sample_sums",
        out_shape=outs,
        grid_spec=pltpu.PrefetchScalarGridSpec(
            num_scalar_prefetch=1,
            grid=(parts,),
            in_specs=[
                pl.BlockSpec((samples, rows, cols), lambda s, tile: (0, 0, 2 * chip(s, tile) + lax.rem(tile[0], 2))),
                pl.BlockSpec((samples, rows, cols), lambda s, tile: (0, 0, chip(s, tile))),
            ]
            + [full(x) for x in small]
            + [full(x) for x in pars]
            + [full(x) for x in vises],
            out_specs=[full(x) for x in outs],
            scratch_shapes=[
                pltpu.VMEM((8, rows, cols), f32),
                pltpu.VMEM((rows, cols), jnp.int32),
                pltpu.VMEM((cols // LANES, held * rows, LANES), f32),
                pltpu.VMEM((cols // LANES, 72 * rows, LANES), f32),
                pltpu.VMEM((cols // LANES, 32 * rows, LANES), f32),
                pltpu.VMEM((2 * LIGHTS, LANES), f32),
                pltpu.VMEM((LIGHTS, LANES), f32),
                pltpu.VMEM((2 * tables["plain"].shape[0], held), bf16),
                pltpu.VMEM((rows, held, cols), bf16),
            ],
        ),
        compiler_params=params_of(),
    )(tile, own, got, *small, *pars, *vises)


def pack_kernel(tile_ref, seen_ref, par_ref, vis_ref, send_ref, first_ref, sems):
    parts = sems.shape[0]
    width = send_ref.shape[2] // parts
    copies = []
    for z in range(parts):
        start = pl.multiple_of((2 * z + 1 - lax.rem(tile_ref[0], 2)) * width, LANES)
        copies.append(
            pltpu.make_async_copy(
                seen_ref.at[:, :, pl.ds(start, width)],
                send_ref.at[:, :, z * width : (z + 1) * width],
                sems.at[z],
            )
        )
        copies[z].start()
    first_ref[0:8] = par_ref[...]
    first_ref[8] = vis_ref[...].astype(f32)
    for copy in copies:
        copy.wait()


def pack_call(tile, observed, params, visible, parts):
    far = pl.BlockSpec(memory_space=pltpu.MemorySpace.HBM)
    samples, rows, width = observed.shape
    return pl.pallas_call(
        pack_kernel,
        name="pack",
        out_shape=[
            jax.ShapeDtypeStruct((samples, rows, width // 2), observed.dtype),
            jax.ShapeDtypeStruct((9,) + params.shape[1:], f32),
        ],
        in_specs=[smem(), far, vmem(), vmem()],
        out_specs=[far, vmem()],
        scratch_shapes=[pltpu.SemaphoreType.DMA((parts,))],
        compiler_params=params_of(),
    )(tile, observed, params, visible)


def plain_call(kernel, name, shapes, scratch, tile, *args):
    return pl.pallas_call(
        kernel,
        name=name,
        out_shape=[jax.ShapeDtypeStruct(shape, f32) for shape in shapes],
        in_specs=[smem()] + [vmem()] * len(args),
        out_specs=[vmem()] * len(shapes),
        scratch_shapes=[pltpu.VMEM(shape, f32) for shape in scratch],
        compiler_params=params_of(),
    )(tile, *args)


def pairs(count, start):
    out = []
    for i in range(start, count - 1, 2):
        out += [(i, i + 1), (i + 1, i)]
    return out


def settle(tile, low, params, moved, gains):
    _, rows, cols = params.shape
    grps, tiles = lax.axis_size("grp"), lax.axis_size("tile")
    strip = (8, cols)
    params, sent = plain_call(solve_kernel, "solve", [params.shape, strip], [], tile, low, params, *moved)
    first = lax.ppermute(sent, "grp", pairs(grps, 0))
    if grps == 4:
        (relay,) = plain_call(relay_kernel, "relay", [strip], [], tile, sent, first)
        edge = lax.ppermute(relay, "grp", [(i, i ^ 2) for i in range(grps)])
        lights = [relay, edge]
    else:
        second = lax.ppermute(sent, "grp", pairs(grps, 1))
        odd = lax.axis_index("grp") % 2 == 1
        edge = jnp.where(odd, second, jnp.roll(second, -2, axis=0))
        light = sent + first
        bit = 2
        while bit < grps:
            light = light + lax.ppermute(light, "grp", [(i, i ^ bit) for i in range(grps)])
            bit *= 2
        lights = [light]
    patch = (2 * rows + 8, LANES)
    tall, sent, other = plain_call(
        functools.partial(rows_kernel, last=grps - 1), "rows", [(2, rows, cols), patch, patch], [(24, cols)],
        tile, params, first, edge, *lights,
    )
    far = lax.ppermute(other, "tile", pairs(tiles, 1))
    near = lax.ppermute(sent, "tile", pairs(tiles, 0))
    return plain_call(
        smooth_kernel, "smooth", [params.shape, gains.shape], [], tile, params, tall, sent, near, far, gains
    )


def exact(a, b, sides):
    return lax.dot_general(
        a, b, (sides, ((), ())), precision=lax.Precision.HIGHEST, preferred_element_type=f32
    )


def iota(shape, axis):
    return lax.broadcasted_iota(jnp.int32, shape, axis)


def pick(test):
    return jnp.where(test, 1.0, 0.0).astype(f32)


def setup_kernel(
    tile_ref, light_ref, view_ref,
    near_ref, cams_ref, lobe_ref, mixed_ref,
    here_ref, shade_ref, plain_ref, tall_ref, near_tall_ref, slab_ref, light_scr, view_scr,
):
    samples = lobe_ref.shape[0]
    held = here_ref.shape[0]
    cams = held // LIGHTS
    first = (tile_of(tile_ref) // 2) * cams

    def unit(raw_ref, scr):
        scr[...] = jnp.zeros(scr.shape, f32)
        scr[0:3, :] = raw_ref[...]
        scr[2:3, :] = scr[2:3, :] + lift_z
        lifted = scr[...]
        return lifted / jnp.sqrt(jnp.sum(lifted * lifted, axis=0, keepdims=True))

    lights = unit(light_ref, light_scr)
    views = unit(view_ref, view_scr)
    near = jnp.where(iota(lights.shape, 0) == 3, 1.0, lights)
    near_ref[...] = near
    cams_ref[...] = views

    def across(count, start, period):
        at_light = pick(iota((LIGHTS, count), 1) % LIGHTS == iota((LIGHTS, count), 0))
        at_view = pick(iota((CAMS, count), 1) // LIGHTS % period + start == iota((CAMS, count), 0))
        wide = exact(near, at_light, ((1,), (0,)))
        view = exact(views, at_view, ((1,), (0,)))
        row = iota((8, count), 0)
        raw = jnp.where(row < 3, wide + view, 0.0)
        half = raw / jnp.sqrt(jnp.sum(raw * raw, axis=0, keepdims=True))
        echo = jnp.sum(wide * view, axis=0, keepdims=True)
        return wide, half, echo

    def down(count, start):
        at_light = pick(iota((count, LIGHTS), 0) % LIGHTS == iota((count, LIGHTS), 1))
        at_view = pick(iota((count, CAMS), 0) // LIGHTS + start == iota((count, CAMS), 1))
        tall = exact(at_light, near, ((1,), (1,)))
        view = exact(at_view, views, ((1,), (1,)))
        lane = iota((count, 8), 1)
        raw = jnp.where(lane < 3, tall + view, 0.0)
        half = raw / jnp.sqrt(jnp.sum(raw * raw, axis=1, keepdims=True))
        half = jnp.where(lane == 3, 1.0, half)
        echo = jnp.sum(tall * view, axis=1, keepdims=True)
        return half, jnp.where(lane == 4, echo, tall)

    def spread(values, width, depth, order):
        lane = iota((8, depth), 1)
        out = None
        for which in range(max(order) + 1):
            head = values.astype(bf16)
            values = values - head.astype(f32)
            group = None
            for g, k in enumerate(order):
                if k == which:
                    hit = lane // width == g
                    group = hit if group is None else jnp.logical_or(group, hit)
            place = pick(jnp.logical_and(group, lane % width == iota((8, depth), 0)))
            place = jnp.where(iota((8, depth), 0) < width, place, 0.0).astype(bf16)
            got = dot(head, place)
            out = got if out is None else out + got
        return out

    wide, half, echo = across(samples, 0, CAMS)
    high = [jnp.ones((1, samples), f32)] + [half[k : k + 1] for k in range(3)]
    low = [wide[k : k + 1] for k in range(3)] + [echo]
    which = iota((1, samples), 1) // LIGHTS % 4
    for i in range(4):
        for j in range(4):
            mixed_ref[4 * i + j : 4 * i + j + 1, :] = high[i] * low[j]
            mixed_ref[16 + 4 * i + j : 17 + 4 * i + j, :] = jnp.where(which == i, high[j], 0.0)
    depth = lobe_ref.shape[1]
    half, _ = down(samples, 0)
    for k in range(3):
        tall_ref[k] = jnp.broadcast_to(half[:, k : k + 1], (samples, LANES))
    hot = pick(iota((samples, depth), 0) // LIGHTS + 24 == iota((samples, depth), 1))
    lobe_ref[...] = (spread(half, 4, depth, (0, 0, 1, 0, 1, 2)) + hot).astype(bf16)

    half, tall = down(held, first)
    for k in range(3):
        near_tall_ref[k] = jnp.broadcast_to(half[:, k : k + 1], (held, LANES))
    cam = iota((held, 32), 0) // LIGHTS
    lane = iota((held, 32), 1)
    hot = pick(cam + 24 == lane)
    here_ref[...] = (spread(half, 4, 32, (0, 0, 1, 0, 1, 2)) + hot).astype(bf16)
    hot = pick(cam + 15 == lane) + pick(cam + (15 + cams) == lane)
    shade_ref[...] = (spread(tall, 5, 32, (0, 0, 1)) + hot).astype(bf16)

    wide, _, _ = across(held, first, cams)
    plain_ref[...] = jnp.zeros(plain_ref.shape, f32)
    which = iota((1, held), 1) // LIGHTS
    for c in range(cams):
        plain_ref[4 * c : 4 * c + 1, :] = pick(which == c)
        for k in range(3):
            plain_ref[4 * c + 1 + k : 4 * c + 2 + k, :] = jnp.where(which == c, wide[k : k + 1], 0.0)
        mine = jnp.sum(jnp.where(iota(views.shape, 1) == first + c, views, 0.0), axis=1, keepdims=True)
        slab_ref[8 * c : 8 * c + 8, :] = jnp.broadcast_to(mine, (8, LANES))


TABLES = ("near", "cams", "lobe", "mixed", "here", "shade", "plain", "tall", "near_tall", "slab")


def setup_call(tile, light_directions, view_dirs, held):
    samples = CAMS * LIGHTS
    cams = held // LIGHTS
    count = max(8, 4 * cams)
    shapes = [
        ((8, LIGHTS), f32), ((8, CAMS), f32), ((samples, 48), bf16), ((32, samples), f32),
        ((held, 32), bf16), ((held, 32), bf16), ((count, held), f32),
        ((3, samples, LANES), f32), ((3, held, LANES), f32), ((8 * cams, LANES), f32),
    ]
    outs = pl.pallas_call(
        setup_kernel,
        name="tables",
        out_shape=[jax.ShapeDtypeStruct(a, b) for a, b in shapes],
        in_specs=[smem(), vmem(), vmem()],
        out_specs=[vmem()] * len(shapes),
        scratch_shapes=[pltpu.VMEM((8, LIGHTS), f32), pltpu.VMEM((8, CAMS), f32)],
        compiler_params=params_of(),
    )(tile, light_directions, view_dirs)
    return dict(zip(TABLES, outs))


def shifted(x, by, nz):
    return lax.ppermute(x, "tile", [(2 * z + c, 2 * ((z + by) % nz) + c) for z in range(nz) for c in range(2)])


def on_device(observed, visible, params_start, light_directions, view_dirs, gains_start):
    samples = observed.shape[0]
    tiles = lax.axis_size("tile")
    nz = tiles // 2
    tile = lax.axis_index("tile")
    held = 2 * samples

    here = (tile + PLACE * lax.axis_index("grp")).astype(jnp.int32).reshape(1)
    send, first = pack_call(here, observed, params_start, visible, nz)
    got = lax.ppermute(send, "tile", [(i, i ^ 1) for i in range(tiles)])
    blocks = [first] + [shifted(first, s, nz) for s in range(1, nz)]
    vises = blocks
    tables = setup_call(here, light_directions, view_dirs, held)

    params = params_start
    gains = gains_start.reshape(1, LIGHTS)
    for iteration in range(ITERS):
        low = normal_call(params, visible, gains, tables)
        rights = sample_call(here, observed, got, gains, tables, blocks, vises)
        moved = [rights[0]] + [shifted(rights[s], -s, nz) for s in range(1, nz)]
        params, gains = settle(here, low, params, moved, gains)
        if iteration + 1 < ITERS:
            blocks = [params] + [shifted(params, s, nz) for s in range(1, nz)]
    return params, gains.reshape(LIGHTS)


def solution(mesh):
    return jax.shard_map(
        on_device,
        mesh=mesh,
        in_specs=(P("tile", "grp", None), P("grp", "tile"), P(None, "grp", "tile"), P(), P(), P()),
        out_specs=(P(None, "grp", "tile"), P()),
        check_vma=False,
    )
```

```python
import functools

import jax
import jax.numpy as jnp
from jax import lax
from jax.experimental import pallas as pl
from jax.experimental.pallas import tpu as pltpu
from jax.sharding import PartitionSpec as P

CAMS = 16
LIGHTS = 32
ITERS = 2

damping = 4.0
lift_z = 1.6
hidden = 1024.0
f32 = jnp.float32
bf16 = jnp.bfloat16
LANES = 128
VMEM_BYTES = 16 * 1024 * 1024
LINEAR = (2, 3, 5, 6, 7)
ENTRIES = [(i, j) for i in range(8) for j in range(i, 8)]


PLACE = 4096


def tile_of(ref):
    return lax.rem(ref[0], PLACE)


def row_is_odd(ref):
    return lax.rem(ref[0] // PLACE, 2) == 1


def column_is_odd(ref):
    return lax.rem(ref[0], 2) == 1


def split_value(x, count):
    pieces = []
    for _ in range(count - 1):
        head = x.astype(bf16).astype(f32)
        pieces.append(head)
        x = x - head
    pieces.append(x)
    return pieces


def split_pair(x):
    head = x.astype(bf16)
    return head, (x - head.astype(f32)).astype(bf16)


def dot(a, b):
    return jnp.dot(a, b, preferred_element_type=f32)


def total(terms):
    terms = list(terms)
    out = terms[0]
    for t in terms[1:]:
        out = out + t
    return out


def inner(a, b):
    return total(x * y for x, y in zip(a, b))


def texel_forms(p):
    tu, tv, diffuse, spec, raw, ambient, rim, retro = p
    q = 1.0 / jnp.sqrt(1.0 + tu * tu + tv * tv)
    nx, ny, nz = tu * q, tv * q, q
    side = -(nx * ny) * q
    by_u = ((1.0 - nx * nx) * q, side, -(nz * nx) * q)
    by_v = (side, (1.0 - ny * ny) * q, -(nz * ny) * q)
    sigma = 1.0 / (1.0 + jnp.exp(-raw))
    sharp = 1.0 + 20.0 * sigma
    slope = 20.0 * sigma * (1.0 - sigma)
    return (nx, ny, nz), by_u, by_v, sharp, slope


def seen(mask, c):
    return jnp.bitwise_and(jnp.right_shift(mask, c), 1).astype(f32)


def put_slab(ref, k, value):
    rows, cols = value.shape
    for h in range(cols // LANES):
        ref[h, k * rows : (k + 1) * rows, :] = value[:, h * LANES : (h + 1) * LANES]


def get_slab(ref, k, rows):
    return jnp.concatenate([ref[h, k * rows : (k + 1) * rows, :] for h in range(ref.shape[0])], axis=1)


def get_rows(ref, start, count, stride):
    return jnp.concatenate([ref[h, pl.ds(start, count, stride=stride), :] for h in range(ref.shape[0])], axis=1)


def put_rows(ref, start, stride, value):
    count, cols = value.shape
    for h in range(cols // LANES):
        ref[h, pl.ds(start, count, stride=stride), :] = value[:, h * LANES : (h + 1) * LANES]


def gain_columns(gains):
    same = pick(iota((LIGHTS, LIGHTS), 0) == iota((LIGHTS, LIGHTS), 1))
    tall = exact(same, jnp.broadcast_to(gains, (8, LIGHTS)), ((1,), (1,)))
    return jnp.broadcast_to(tall[:, 0:1], (LIGHTS, LANES))


def eights(x):
    return total(x[i : i + 8] for i in range(0, x.shape[0], 8))


def put_lobe_rows(slab, normal, sharp):
    base = [sharp * normal[0], sharp * normal[1], sharp * normal[2], -sharp]
    parts = [split_value(x, 3) for x in base]
    row = 0
    for which in (0, 1, 0, 2, 1, 0):
        for part in parts:
            slab(row, part[which])
            row += 1
    return row


def normal_kernel(
    par_ref, vis_ref, gain_ref, near_ref, cams_ref, lobe_ref, mixed_ref, tall_ref, out_ref,
    rows_ref, sums_ref, mixed_scr, gain_scr, cam_scr, gram_scr, lobe_scr,
):
    rows, cols = par_ref.shape[1], par_ref.shape[2]
    depth = lobe_ref.shape[1]
    chunk = 4 * LIGHTS
    chunks = CAMS // 4

    near, views = near_ref[...], cams_ref[...]
    gain2 = gain_ref[...] * gain_ref[...]
    grams = [jnp.sum(near * near[i : i + 1] * gain2, axis=1, keepdims=True) for i in range(4)]
    for i in range(4):
        gram_scr[8 * i : 8 * i + 8, :] = jnp.broadcast_to(grams[i], (8, LANES))
    spread = [total(grams[i][k : k + 1] * views[k : k + 1] for k in range(3)) for i in range(4)]
    echo_sq = total(spread[k] * views[k : k + 1] for k in range(3))
    row = iota(views.shape, 0)
    full = jnp.where(row == 3, echo_sq, jnp.where(row == 4, spread[3], views))
    for c in range(CAMS):
        cam_scr[8 * c : 8 * c + 8, :] = jnp.broadcast_to(full[:, c : c + 1], (8, LANES))

    gain_scr[...] = gain_columns(gain2)
    across = CAMS * LIGHTS
    at_light = pick(iota((LIGHTS, across), 1) % LIGHTS == iota((LIGHTS, across), 0))
    gain2 = exact(jnp.broadcast_to(gain2, (8, LIGHTS)), at_light, ((1,), (0,)))[0:1]
    for src, dst in ((mixed_ref, mixed_scr),):
        head, tail = split_pair(src[...] * gain2)
        count = src.shape[0]
        for ch in range(chunks):
            part = slice(ch * chunk, (ch + 1) * chunk)
            first = slice(2 * ch * chunk, (2 * ch + 1) * chunk)
            second = slice((2 * ch + 1) * chunk, (2 * ch + 2) * chunk)
            dst[0:count, first] = head[:, part]
            dst[0:count, second] = head[:, part]
            dst[count : 2 * count, first] = tail[:, part]
            dst[count : 2 * count, second] = jnp.zeros((count, chunk), bf16)

    def slab(k, value):
        put_slab(rows_ref, k, value)

    p = [par_ref[i] for i in range(8)]
    normal, _, _, sharp, _ = texel_forms(p)
    used = put_lobe_rows(slab, normal, sharp)
    mask = vis_ref[...]
    for c in range(CAMS):
        slab(used + c, (seen(mask, c) - 1.0) * hidden)
    for k in range(used + CAMS, depth):
        slab(k, jnp.zeros((rows, cols), f32))

    quads = [(i, j) for i in range(4) for j in range(i, 4)]

    def one_row(r):
        texel = get_rows(rows_ref, r, depth, rows).astype(bf16)
        mixed = jnp.zeros((16, cols), f32)
        bent = {(h, ij): None for h in range(cols // LANES) for ij in quads}
        for ch in range(chunks):
            for c in range(4):
                part = slice(ch * chunk + c * LIGHTS, ch * chunk + (c + 1) * LIGHTS)
                lobe = jnp.exp(dot(lobe_ref[part, :], texel))
                head, tail = split_pair(lobe)
                lobe_scr[r, ch, c * LIGHTS : (c + 1) * LIGHTS, :] = head
                lobe_scr[r, ch, chunk + c * LIGHTS : chunk + (c + 1) * LIGHTS, :] = tail
                tall = [None] + [tall_ref[k, part, :] for k in range(3)]
                for h in range(cols // LANES):
                    lobe_h = lobe[:, h * LANES : (h + 1) * LANES]
                    single = [lobe_h * lobe_h * gain_scr[...]]
                    single += [single[0] * tall[k] for k in (1, 2, 3)]
                    for i, j in quads:
                        value = eights(single[j] if i == 0 else single[i] * tall[j])
                        old = bent[h, (i, j)]
                        bent[h, (i, j)] = value if old is None else old + value
            at = slice(2 * ch * chunk, (2 * ch + 2) * chunk)
            both = dot(mixed_scr[:, at], lobe_scr[r, ch])
            got = both[0:32] + both[32:64]
            mixed = mixed + got[0:16]
            put_rows(sums_ref, (32 + 16 * ch) * rows + r, rows, got[16:32])
        put_rows(sums_ref, r, rows, mixed)
        for h in range(cols // LANES):
            for k, ij in enumerate(quads):
                line = (16 + k) * rows + r
                sums_ref[h, line : line + 1, :] = jnp.sum(bent[h, ij], axis=0, keepdims=True)

    for r in range(rows):
        one_row(r)

    def one_part(h, carry):
        at = pl.ds(pl.multiple_of(h * LANES, LANES), LANES)

        def cam(c, i):
            return cam_scr[8 * c + i : 8 * c + i + 1, :]

        def sums(k):
            return sums_ref[h, k * rows : (k + 1) * rows, :]

        p = [par_ref[i, :, at] for i in range(8)]
        mask = vis_ref[:, at]
        normal, by_u, by_v, sharp, slope = texel_forms(p)
        diffuse, spec, rim = p[2], p[3], p[6]
        zero = jnp.zeros((rows, LANES), f32)
        gam = {i: zero for i in (0, 1, 5, 6)}
        own = {(i, j): zero for i in (0, 1, 5, 6) for j in (0, 1, 5, 6) if i <= j and j != 5 and i != 5}
        lit = {i: zero for i in (0, 1, 5, 6)}
        grid = {(i, k): zero for i in (0, 1, 5, 6) for k in range(4)}
        echo_sq = zero
        view_sum = [zero, zero, zero]
        for c in range(CAMS):
            w = seen(mask, c)
            v = [cam(c, i) for i in range(3)]
            back = 1.0 - inner(v, normal)
            turn = (-2.0 * rim) * back
            shape = {0: turn * inner(v, by_u), 1: turn * inner(v, by_v), 6: back * back}
            weighted = {i: w * shape[i] for i in shape}
            weighted[5] = w
            for i in gam:
                gam[i] = gam[i] + weighted[i]
                lit[i] = lit[i] + weighted[i] * cam(c, 4)
            for i, j in own:
                own[i, j] = own[i, j] + weighted[i] * shape[j]
            echo_sq = echo_sq + w * cam(c, 3)
            view_sum = [s + w * x for s, x in zip(view_sum, v)]
            for k in range(4):
                peak = sums(32 + 4 * c + k)
                for i in (0, 1, 6):
                    grid[i, k] = grid[i, k] + shape[i] * peak
                grid[5, k] = grid[5, k] + peak
        own[5, 5] = gam[5]
        for i in (0, 1):
            own[i, 5] = gam[i]
        own[5, 6] = gam[6]

        def gram(i, j):
            return gram_scr[8 * i + j : 8 * i + j + 1, :]

        entries = {ij: None for ij in ENTRIES}

        def add(i, j, value):
            ij = (min(i, j), max(i, j))
            entries[ij] = value if entries[ij] is None else entries[ij] + value

        def cross(i, j, value):
            add(i, j, value + value if i == j else value)

        flat = {0: [diffuse * x for x in by_u], 1: [diffuse * x for x in by_v], 2: list(normal)}
        edge = spec * sharp
        tilt = spec * slope
        glow = {
            0: {1 + k: edge * by_u[k] for k in range(3)},
            1: {1 + k: edge * by_v[k] for k in range(3)},
            3: {0: None},
            4: {0: -tilt, 1: tilt * normal[0], 2: tilt * normal[1], 3: tilt * normal[2]},
        }

        def combine(coefs, values):
            return total(values[k] if x is None else x * values[k] for k, x in coefs.items())

        count = gam[5]
        spread = {i: [total(gram(r, k) * flat[i][k] for k in range(3)) for r in range(3)] for i in flat}
        reach = {i: total(gram(3, k) * flat[i][k] for k in range(3)) for i in flat}
        view_spread = [total(gram(r, k) * view_sum[k] for k in range(3)) for r in range(3)]
        for i in flat:
            for j in flat:
                if i <= j:
                    add(i, j, count * inner(flat[j], spread[i]))
            for j in gam:
                cross(i, j, reach[i] * gam[j])
            cross(i, 7, inner(flat[i], view_spread))
        for i, j in own:
            add(i, j, gram(3, 3) * own[i, j])
        for i in lit:
            cross(i, 7, lit[i])
        add(7, 7, echo_sq)
        for j in glow:
            for i in flat:
                cross(i, j, total(flat[i][x] * combine(glow[j], {k: sums(4 * k + x) for k in glow[j]}) for x in range(3)))
            for i in gam:
                cross(i, j, combine(glow[j], {k: grid[i, k] for k in glow[j]}))
            cross(j, 7, combine(glow[j], {k: sums(4 * k + 3) for k in glow[j]}))
        packed = {}
        where = 0
        for i in range(4):
            for j in range(i, 4):
                packed[i, j] = packed[j, i] = where
                where += 1
        for i in glow:
            for j in glow:
                if i <= j:
                    half = {k: combine(glow[j], {x: sums(16 + packed[k, x]) for x in glow[j]}) for k in glow[i]}
                    add(i, j, combine(glow[i], half))

        def entry(i, j):
            return entries[min(i, j), max(i, j)]

        for i in range(8):
            out_ref[36 + i, :, at] = total(entry(i, j) * p[j] for j in LINEAR)
        lower = {}
        for j in range(8):
            accum = entries[j, j] + damping
            for k in range(j):
                accum = accum - lower[j, k] * lower[j, k]
            inverse = lax.rsqrt(accum)
            lower[j, j] = inverse
            for i in range(j + 1, 8):
                accum = entries[j, i]
                for k in range(j):
                    accum = accum - lower[i, k] * lower[j, k]
                lower[i, j] = accum * inverse
        for where, (i, j) in enumerate(ENTRIES):
            out_ref[where, :, at] = lower[j, i]
        return carry

    lax.fori_loop(0, cols // LANES, one_part, 0)


def sample_kernel(
    tile_ref, own_ref, got_ref, gain_ref, lobe_ref, shade_ref, plain_ref, tall_ref, slab_ref, *refs, parts, mend
):
    par_refs, vis_refs = refs[:parts], refs[parts : 2 * parts]
    out_refs = refs[2 * parts : 3 * parts]
    extra = 1 if mend else 0
    own_out_refs = refs[3 * parts : 3 * parts + extra]
    par_scr, vis_scr, obs_scr, rows_ref, sums_ref, light_scr, gain_scr, plain_scr, flat_scr = refs[3 * parts + extra :]
    step = pl.program_id(0)
    samples, rows, cols = own_ref.shape
    held = 2 * samples
    cams = held // LIGHTS
    for s in range(parts):

        @pl.when(step == s)
        def _():
            par_scr[...] = par_refs[s][0:8]
            if mend:
                side = column_is_odd(tile_ref)
                chip = lax.rem(tile_of(tile_ref) // 2 + (parts - s), parts)
                inside = jnp.where(side, chip, parts - 1 - chip) < parts - 1
                lane = iota((rows, cols), 1)
                hit = jnp.logical_and(lane == jnp.where(side, cols - 1, 0), inside)
                lower, upper = par_refs[(s + 1) % parts], par_refs[(s - 1) % parts]
                for k in range(2):
                    end = jnp.where(side, upper[8, :, k : k + 1], lower[8, :, k : k + 1])
                    par_scr[k] = par_refs[s][k] + jnp.where(hit, end, 0.0)
                if s == 0:
                    own_out_refs[0][...] = par_scr[...]
            vis_scr[...] = vis_refs[s][8].astype(jnp.int32)

    core = tile_of(tile_ref) % 2
    mine = pl.multiple_of(core * (samples * rows), rows)
    theirs = pl.multiple_of((1 - core) * (samples * rows), rows)
    for h in range(cols // LANES):
        lanes = slice(h * LANES, (h + 1) * LANES)
        for src, at in ((own_ref, mine), (got_ref, theirs)):
            obs_scr[h, pl.ds(at, samples * rows), :] = src[:, :, lanes].astype(f32).reshape(samples * rows, LANES)

    def slab(k, value):
        put_slab(rows_ref, k, value)

    p = [par_scr[i] for i in range(8)]
    mask = vis_scr[...]
    normal, by_u, by_v, sharp, slope = texel_forms(p)
    base = (tile_of(tile_ref) // 2) * cams

    def cam(c, i):
        return slab_ref[8 * c + i : 8 * c + i + 1, :][:, 0:1]

    used = put_lobe_rows(slab, normal, sharp)
    weights = [seen(mask, base + c) for c in range(cams)]
    for c in range(cams):
        slab(used + c, (weights[c] - 1.0) * hidden)
        slab(65 + c, weights[c])
    for k in range(used + cams, 32):
        slab(k, jnp.zeros((rows, cols), f32))
    shade = [p[2] * normal[0], p[2] * normal[1], p[2] * normal[2], p[5], p[7]]
    pieces = [split_value(x, 2) for x in shade]
    at = 32
    for which in (0, 1, 0):
        for piece in pieces:
            slab(at, piece[which])
            at += 1
    for c in range(cams):
        back = 1.0 - inner([cam(c, i) for i in range(3)], normal)
        head, tail = split_value(p[6] * (back * back), 2)
        slab(at + c, head)
        slab(at + cams + c, tail)
    for k in range(at + 2 * cams, 64):
        slab(k, jnp.zeros((rows, cols), f32))
    slab(64, p[3])

    @pl.when(step == 0)
    def _():
        at_light = pick(iota((LIGHTS, held), 1) % LIGHTS == iota((LIGHTS, held), 0))
        gains = exact(jnp.broadcast_to(gain_ref[...], (8, LIGHTS)), at_light, ((1,), (0,)))[0:1]
        plain_scr[...] = jnp.concatenate(split_value(plain_ref[...] * gains, 2), axis=0).astype(bf16)
        gain_scr[...] = gain_columns(gain_ref[...])

    count = plain_ref.shape[0]

    def fold(x):
        return total(x[:, k * LANES : (k + 1) * LANES] for k in range(cols // LANES))

    def one_row(r, lift, energy):
        texel = get_rows(rows_ref, r, 32, rows).astype(bf16)
        tint = get_rows(rows_ref, 32 * rows + r, 32, rows).astype(bf16)
        misc = get_rows(rows_ref, 64 * rows + r, 8, rows)
        peak = {}
        for c in range(cams):
            part = slice(c * LIGHTS, (c + 1) * LIGHTS)
            lobe = jnp.exp(dot(lobe_ref[part, :], texel))
            full = dot(shade_ref[part, :], tint) + misc[0:1] * lobe
            obs = get_rows(obs_scr, c * LIGHTS * rows + r, LIGHTS, rows)
            kept = full * misc[1 + c : 2 + c]
            lift = lift + fold(kept * obs)
            energy = energy + fold(kept * full)
            flat_scr[r, part, :] = obs.astype(bf16)
            lit = obs * lobe
            for h in range(cols // LANES):
                base = lit[:, h * LANES : (h + 1) * LANES] * gain_scr[...]
                for k in range(4):
                    value = eights(base if k == 0 else base * tall_ref[k - 1, part, :])
                    peak[h, k] = value if c == 0 else peak[h, k] + value
        both = dot(plain_scr[...], flat_scr[r])
        put_rows(sums_ref, r, rows, both[0:count] + both[count : 2 * count])
        for h, k in peak:
            line = (count + k) * rows + r
            sums_ref[h, line : line + 1, :] = jnp.sum(peak[h, k], axis=0, keepdims=True)
        return lift, energy

    lift = energy = jnp.zeros((LIGHTS, LANES), f32)
    for r in range(rows):
        lift, energy = one_row(r, lift, energy)

    @pl.when(step == 0)
    def _():
        light_scr[0:LIGHTS, :] = lift
        light_scr[LIGHTS : 2 * LIGHTS, :] = energy

    @pl.when(step != 0)
    def _():
        light_scr[0:LIGHTS, :] = light_scr[0:LIGHTS, :] + lift
        light_scr[LIGHTS : 2 * LIGHTS, :] = light_scr[LIGHTS : 2 * LIGHTS, :] + energy

    @pl.when(step == parts - 1)
    def _():
        out_refs[parts - 1][8] = jnp.zeros((rows, cols), f32)
        for k in range(2):
            part = light_scr[k * LIGHTS : (k + 1) * LIGHTS, :]
            line = exact(jnp.ones((8, LANES), f32), part, ((1,), (1,)))[0:1]
            for ref in out_refs:
                ref[8, k : k + 1, 0:LIGHTS] = line

    def sums(k):
        return get_slab(sums_ref, k, rows)

    flat = [None, None, None]
    lone, rim_sum, echo_sum, turn_u, turn_v = None, None, None, None, None

    def grow(old, new):
        return new if old is None else old + new

    for c in range(cams):
        v = [cam(c, i) for i in range(3)]
        w = weights[c]
        one = w * sums(4 * c)
        lit = [w * sums(4 * c + 1 + x) for x in range(3)]
        back = 1.0 - inner(v, normal)
        bent = back * one
        lone = grow(lone, one)
        rim_sum = grow(rim_sum, back * bent)
        turn_u = grow(turn_u, bent * inner(v, by_u))
        turn_v = grow(turn_v, bent * inner(v, by_v))
        echo_sum = grow(echo_sum, inner(v, lit))
        flat = [grow(f, x) for f, x in zip(flat, lit)]
    spot = sums(count)
    spots = [sums(count + 1 + x) for x in range(3)]
    edge = p[3] * sharp
    twice = -2.0 * p[6]
    right = [
        p[2] * inner(by_u, flat) + edge * inner(by_u, spots) + twice * turn_u,
        p[2] * inner(by_v, flat) + edge * inner(by_v, spots) + twice * turn_v,
        inner(normal, flat),
        spot,
        p[3] * slope * (inner(normal, spots) - spot),
        lone,
        rim_sum,
        echo_sum,
    ]
    for s in range(parts):

        @pl.when(step == s)
        def _():
            for i in range(8):
                out_refs[s][i] = right[i]
            if s < parts - 1:
                out_refs[s][8] = jnp.zeros((rows, cols), f32)


def ring_total(terms):
    while len(terms) > 1:
        half = len(terms) // 2
        terms = [terms[k] + terms[k + half] for k in range(half)]
    return terms[0]


def solve_kernel(tile_ref, low_ref, par_ref, *refs):
    right_refs, (out_ref, sent_ref) = refs[:-2], refs[-2:]
    lower = {}
    for where, (i, j) in enumerate(ENTRIES):
        lower[j, i] = low_ref[where]
    right = [total(ref[i] for ref in right_refs) - low_ref[36 + i] for i in range(8)]
    forward = []
    for i in range(8):
        accum = right[i]
        for k in range(i):
            accum = accum - lower[i, k] * forward[k]
        forward.append(accum * lower[i, i])
    answer = [None] * 8
    for i in range(7, -1, -1):
        accum = forward[i]
        for k in range(i + 1, 8):
            accum = accum - lower[k, i] * answer[k]
        answer[i] = accum * lower[i, i]
    rows = par_ref.shape[1]
    sent_ref[...] = jnp.zeros(sent_ref.shape, f32)
    for i in range(8):
        fresh = par_ref[i] + answer[i]
        out_ref[i] = fresh
        if i < 2:
            sent_ref[i : i + 1, :] = fresh[0:1]
            sent_ref[2 + i : 3 + i, :] = fresh[rows - 1 : rows]
    sent_ref[4:6, 0:LANES] = ring_total([ref[8, 0:2, 0:LANES] for ref in right_refs])


def relay_kernel(tile_ref, sent_ref, first_ref, out_ref):
    odd = row_is_odd(tile_ref)
    out_ref[...] = sent_ref[...] + first_ref[...]
    out_ref[0:2, :] = jnp.where(odd, first_ref[0:2, :], first_ref[2:4, :])


def rows_kernel(tile_ref, par_ref, first_ref, edge_ref, *refs, last):
    light_refs, (tall_ref, near_ref, scr) = refs[:-3], refs[-3:]
    rows, cols = par_ref.shape[1:]
    place = tile_ref[0] // PLACE
    odd = row_is_odd(tile_ref)
    outer = jnp.where(jnp.logical_or(place == 0, place == last), 0.0, 1.0)
    near_ref[...] = jnp.zeros(near_ref.shape, f32)
    lane = iota((rows, LANES), 1)
    for k in range(2):
        other = outer * edge_ref[k : k + 1, :]
        scr[7:8, :] = jnp.where(odd, first_ref[2 + k : 3 + k, :], other)
        scr[8 : 8 + rows, :] = par_ref[k]
        scr[8 + rows : 9 + rows, :] = jnp.where(odd, other, first_ref[k : k + 1, :])
        tall = scr[7 : 7 + rows, :] + scr[8 : 8 + rows, :] + scr[9 : 9 + rows, :]
        tall_ref[k] = tall
        ends = jnp.where(lane == 0, tall[:, 0:1], jnp.where(lane == 1, tall[:, cols - 1 : cols], 0.0))
        near_ref[k * rows : (k + 1) * rows, :] = ends
    near_ref[2 * rows : 2 * rows + 2, :] = total(ref[4:6, 0:LANES] for ref in light_refs)


def smooth_kernel(tile_ref, par_ref, tall_ref, gain_ref, sent_ref, near_ref, *refs):
    far_refs, (out_ref, gain_out_ref) = refs[:-2], refs[-2:]
    rows, cols = par_ref.shape[1:]
    side = column_is_odd(tile_ref)
    lane = iota((rows, cols), 1)
    spill = jnp.zeros((rows, cols), f32)
    for k in range(2):
        at = slice(k * rows, (k + 1) * rows)
        tall = tall_ref[k]
        near_left, near_right = near_ref[at, 0:1], near_ref[at, 1:2]
        far_left = far_right = jnp.zeros((rows, 1), f32)
        if far_refs:
            far_left, far_right = far_refs[0][at, 0:1], far_refs[0][at, 1:2]
        before = jnp.where(side, near_right, far_right)
        after = jnp.where(side, far_left, near_left)
        left = jnp.where(lane == 0, before, pltpu.roll(tall, 1, 1))
        right = jnp.where(lane == cols - 1, after, pltpu.roll(tall, cols - 1, 1))
        out_ref[k] = 0.5 * par_ref[k] + (tall + left + right) * (0.5 / 9.0)
        spill = jnp.where(lane == k, jnp.where(side, near_left, near_right) * (0.5 / 9.0), spill)
    for k in range(2, 8):
        out_ref[k] = par_ref[k]
    if not far_refs:
        out_ref[8] = spill
    light = sent_ref[2 * rows : 2 * rows + 2, 0:LIGHTS] + near_ref[2 * rows : 2 * rows + 2, 0:LIGHTS]
    gains = gain_ref[...]
    gain_out_ref[...] = gains + (light[0:1] - gains * light[1:2]) / (light[1:2] + 1.0)


def smem():
    return pl.BlockSpec(memory_space=pltpu.SMEM)


def vmem():
    return pl.BlockSpec(memory_space=pltpu.VMEM)


def params_of():
    return pltpu.CompilerParams(vmem_limit_bytes=VMEM_BYTES)


def normal_call(par, vis, gains, tables):
    _, rows, cols = par.shape
    parts = cols // LANES
    small = [tables[n] for n in ("near", "cams", "lobe", "mixed", "tall")]
    return pl.pallas_call(
        normal_kernel,
        name="normal_factor",
        out_shape=jax.ShapeDtypeStruct((44, rows, cols), f32),
        in_specs=[vmem()] * 8,
        out_specs=vmem(),
        scratch_shapes=[
            pltpu.VMEM((parts, 48 * rows, LANES), f32),
            pltpu.VMEM((parts, 96 * rows, LANES), f32),
            pltpu.VMEM((64, 2 * CAMS * LIGHTS), bf16),
            pltpu.VMEM((LIGHTS, LANES), f32),
            pltpu.VMEM((8 * CAMS, LANES), f32),
            pltpu.VMEM((32, LANES), f32),
            pltpu.VMEM((rows, 4, 8 * LIGHTS, cols), bf16),
        ],
        compiler_params=params_of(),
    )(par, vis, gains, *small)


def sample_call(tile, own, got, gains, tables, pars, vises, mend):
    parts = len(pars)
    samples, rows, _ = own.shape
    cols = pars[0].shape[2]
    held = 2 * samples

    def full(x):
        zeros = (0,) * len(x.shape)
        return pl.BlockSpec(x.shape, lambda s, tile: zeros)

    def chip(s, tile):
        return lax.rem(tile_of(tile) // 2 + (parts - s), parts)

    outs = [jax.ShapeDtypeStruct((9, rows, cols), f32) for _ in range(parts)]
    if mend:
        outs.append(jax.ShapeDtypeStruct((8, rows, cols), f32))
    small = [gains] + [tables[n] for n in ("here", "shade", "plain", "near_tall", "slab")]
    return pl.pallas_call(
        functools.partial(sample_kernel, parts=parts, mend=mend),
        name="sample_sums",
        out_shape=outs,
        grid_spec=pltpu.PrefetchScalarGridSpec(
            num_scalar_prefetch=1,
            grid=(parts,),
            in_specs=[
                pl.BlockSpec((samples, rows, cols), lambda s, tile: (0, 0, 2 * chip(s, tile) + lax.rem(tile[0], 2))),
                pl.BlockSpec((samples, rows, cols), lambda s, tile: (0, 0, chip(s, tile))),
            ]
            + [full(x) for x in small]
            + [full(x) for x in pars]
            + [full(x) for x in vises],
            out_specs=[full(x) for x in outs],
            scratch_shapes=[
                pltpu.VMEM((8, rows, cols), f32),
                pltpu.VMEM((rows, cols), jnp.int32),
                pltpu.VMEM((cols // LANES, held * rows, LANES), f32),
                pltpu.VMEM((cols // LANES, 72 * rows, LANES), f32),
                pltpu.VMEM((cols // LANES, 32 * rows, LANES), f32),
                pltpu.VMEM((2 * LIGHTS, LANES), f32),
                pltpu.VMEM((LIGHTS, LANES), f32),
                pltpu.VMEM((2 * tables["plain"].shape[0], held), bf16),
                pltpu.VMEM((rows, held, cols), bf16),
            ],
        ),
        compiler_params=params_of(),
    )(tile, own, got, *small, *pars, *vises)


def pack_kernel(tile_ref, seen_ref, par_ref, vis_ref, send_ref, first_ref, sems):
    parts = sems.shape[0]
    width = send_ref.shape[2] // parts
    copies = []
    for z in range(parts):
        start = pl.multiple_of((2 * z + 1 - lax.rem(tile_ref[0], 2)) * width, LANES)
        copies.append(
            pltpu.make_async_copy(
                seen_ref.at[:, :, pl.ds(start, width)],
                send_ref.at[:, :, z * width : (z + 1) * width],
                sems.at[z],
            )
        )
        copies[z].start()
    first_ref[0:8] = par_ref[...]
    first_ref[8] = vis_ref[...].astype(f32)
    for copy in copies:
        copy.wait()


def pack_call(tile, observed, params, visible, parts):
    far = pl.BlockSpec(memory_space=pltpu.MemorySpace.HBM)
    samples, rows, width = observed.shape
    return pl.pallas_call(
        pack_kernel,
        name="pack",
        out_shape=[
            jax.ShapeDtypeStruct((samples, rows, width // 2), observed.dtype),
            jax.ShapeDtypeStruct((9,) + params.shape[1:], f32),
        ],
        in_specs=[smem(), far, vmem(), vmem()],
        out_specs=[far, vmem()],
        scratch_shapes=[pltpu.SemaphoreType.DMA((parts,))],
        compiler_params=params_of(),
    )(tile, observed, params, visible)


def plain_call(kernel, name, shapes, scratch, tile, *args):
    return pl.pallas_call(
        kernel,
        name=name,
        out_shape=[jax.ShapeDtypeStruct(shape, f32) for shape in shapes],
        in_specs=[smem()] + [vmem()] * len(args),
        out_specs=[vmem()] * len(shapes),
        scratch_shapes=[pltpu.VMEM(shape, f32) for shape in scratch],
        compiler_params=params_of(),
    )(tile, *args)


def pairs(count, start):
    out = []
    for i in range(start, count - 1, 2):
        out += [(i, i + 1), (i + 1, i)]
    return out


def settle(tile, low, params, moved, gains, closed):
    _, rows, cols = params.shape
    grps, tiles = lax.axis_size("grp"), lax.axis_size("tile")
    strip = (8, cols)
    params, sent = plain_call(solve_kernel, "solve", [params.shape, strip], [], tile, low, params, *moved)
    first = lax.ppermute(sent, "grp", pairs(grps, 0))
    if grps == 4:
        (relay,) = plain_call(relay_kernel, "relay", [strip], [], tile, sent, first)
        edge = lax.ppermute(relay, "grp", [(i, i ^ 2) for i in range(grps)])
        lights = [relay, edge]
    else:
        second = lax.ppermute(sent, "grp", pairs(grps, 1))
        odd = lax.axis_index("grp") % 2 == 1
        edge = jnp.where(odd, second, jnp.roll(second, -2, axis=0))
        light = sent + first
        bit = 2
        while bit < grps:
            light = light + lax.ppermute(light, "grp", [(i, i ^ bit) for i in range(grps)])
            bit *= 2
        lights = [light]
    patch = (2 * rows + 8, LANES)
    tall, sent = plain_call(
        functools.partial(rows_kernel, last=grps - 1), "rows", [(2, rows, cols), patch], [(24, cols)],
        tile, params, first, edge, *lights,
    )
    ends = [lax.ppermute(sent, "tile", pairs(tiles, 1))] if closed else []
    near = lax.ppermute(sent, "tile", pairs(tiles, 0))
    slabs = 8 if closed else 9
    return plain_call(
        smooth_kernel, "smooth", [(slabs, rows, cols), gains.shape], [], tile, params, tall, gains, sent, near, *ends
    )


def exact(a, b, sides):
    return lax.dot_general(
        a, b, (sides, ((), ())), precision=lax.Precision.HIGHEST, preferred_element_type=f32
    )


def iota(shape, axis):
    return lax.broadcasted_iota(jnp.int32, shape, axis)


def pick(test):
    return jnp.where(test, 1.0, 0.0).astype(f32)


def setup_kernel(
    tile_ref, light_ref, view_ref,
    near_ref, cams_ref, lobe_ref, mixed_ref,
    here_ref, shade_ref, plain_ref, tall_ref, near_tall_ref, slab_ref, light_scr, view_scr,
):
    samples = lobe_ref.shape[0]
    held = here_ref.shape[0]
    cams = held // LIGHTS
    first = (tile_of(tile_ref) // 2) * cams

    def unit(raw_ref, scr):
        scr[...] = jnp.zeros(scr.shape, f32)
        scr[0:3, :] = raw_ref[...]
        scr[2:3, :] = scr[2:3, :] + lift_z
        lifted = scr[...]
        return lifted / jnp.sqrt(jnp.sum(lifted * lifted, axis=0, keepdims=True))

    lights = unit(light_ref, light_scr)
    views = unit(view_ref, view_scr)
    near = jnp.where(iota(lights.shape, 0) == 3, 1.0, lights)
    near_ref[...] = near
    cams_ref[...] = views

    def across(count, start, period):
        at_light = pick(iota((LIGHTS, count), 1) % LIGHTS == iota((LIGHTS, count), 0))
        at_view = pick(iota((CAMS, count), 1) // LIGHTS % period + start == iota((CAMS, count), 0))
        wide = exact(near, at_light, ((1,), (0,)))
        view = exact(views, at_view, ((1,), (0,)))
        row = iota((8, count), 0)
        raw = jnp.where(row < 3, wide + view, 0.0)
        half = raw / jnp.sqrt(jnp.sum(raw * raw, axis=0, keepdims=True))
        echo = jnp.sum(wide * view, axis=0, keepdims=True)
        return wide, half, echo

    def down(count, start):
        at_light = pick(iota((count, LIGHTS), 0) % LIGHTS == iota((count, LIGHTS), 1))
        at_view = pick(iota((count, CAMS), 0) // LIGHTS + start == iota((count, CAMS), 1))
        tall = exact(at_light, near, ((1,), (1,)))
        view = exact(at_view, views, ((1,), (1,)))
        lane = iota((count, 8), 1)
        raw = jnp.where(lane < 3, tall + view, 0.0)
        half = raw / jnp.sqrt(jnp.sum(raw * raw, axis=1, keepdims=True))
        half = jnp.where(lane == 3, 1.0, half)
        echo = jnp.sum(tall * view, axis=1, keepdims=True)
        return half, jnp.where(lane == 4, echo, tall)

    def spread(values, width, depth, order):
        lane = iota((8, depth), 1)
        out = None
        for which in range(max(order) + 1):
            head = values.astype(bf16)
            values = values - head.astype(f32)
            group = None
            for g, k in enumerate(order):
                if k == which:
                    hit = lane // width == g
                    group = hit if group is None else jnp.logical_or(group, hit)
            place = pick(jnp.logical_and(group, lane % width == iota((8, depth), 0)))
            place = jnp.where(iota((8, depth), 0) < width, place, 0.0).astype(bf16)
            got = dot(head, place)
            out = got if out is None else out + got
        return out

    wide, half, echo = across(samples, 0, CAMS)
    high = [jnp.ones((1, samples), f32)] + [half[k : k + 1] for k in range(3)]
    low = [wide[k : k + 1] for k in range(3)] + [echo]
    which = iota((1, samples), 1) // LIGHTS % 4
    for i in range(4):
        for j in range(4):
            mixed_ref[4 * i + j : 4 * i + j + 1, :] = high[i] * low[j]
            mixed_ref[16 + 4 * i + j : 17 + 4 * i + j, :] = jnp.where(which == i, high[j], 0.0)
    depth = lobe_ref.shape[1]
    half, _ = down(samples, 0)
    for k in range(3):
        tall_ref[k] = jnp.broadcast_to(half[:, k : k + 1], (samples, LANES))
    hot = pick(iota((samples, depth), 0) // LIGHTS + 24 == iota((samples, depth), 1))
    lobe_ref[...] = (spread(half, 4, depth, (0, 0, 1, 0, 1, 2)) + hot).astype(bf16)

    half, tall = down(held, first)
    for k in range(3):
        near_tall_ref[k] = jnp.broadcast_to(half[:, k : k + 1], (held, LANES))
    cam = iota((held, 32), 0) // LIGHTS
    lane = iota((held, 32), 1)
    hot = pick(cam + 24 == lane)
    here_ref[...] = (spread(half, 4, 32, (0, 0, 1, 0, 1, 2)) + hot).astype(bf16)
    hot = pick(cam + 15 == lane) + pick(cam + (15 + cams) == lane)
    shade_ref[...] = (spread(tall, 5, 32, (0, 0, 1)) + hot).astype(bf16)

    wide, _, _ = across(held, first, cams)
    plain_ref[...] = jnp.zeros(plain_ref.shape, f32)
    which = iota((1, held), 1) // LIGHTS
    for c in range(cams):
        plain_ref[4 * c : 4 * c + 1, :] = pick(which == c)
        for k in range(3):
            plain_ref[4 * c + 1 + k : 4 * c + 2 + k, :] = jnp.where(which == c, wide[k : k + 1], 0.0)
        mine = jnp.sum(jnp.where(iota(views.shape, 1) == first + c, views, 0.0), axis=1, keepdims=True)
        slab_ref[8 * c : 8 * c + 8, :] = jnp.broadcast_to(mine, (8, LANES))


TABLES = ("near", "cams", "lobe", "mixed", "here", "shade", "plain", "tall", "near_tall", "slab")


def setup_call(tile, light_directions, view_dirs, held):
    samples = CAMS * LIGHTS
    cams = held // LIGHTS
    count = max(8, 4 * cams)
    shapes = [
        ((8, LIGHTS), f32), ((8, CAMS), f32), ((samples, 48), bf16), ((32, samples), f32),
        ((held, 32), bf16), ((held, 32), bf16), ((count, held), f32),
        ((3, samples, LANES), f32), ((3, held, LANES), f32), ((8 * cams, LANES), f32),
    ]
    outs = pl.pallas_call(
        setup_kernel,
        name="tables",
        out_shape=[jax.ShapeDtypeStruct(a, b) for a, b in shapes],
        in_specs=[smem(), vmem(), vmem()],
        out_specs=[vmem()] * len(shapes),
        scratch_shapes=[pltpu.VMEM((8, LIGHTS), f32), pltpu.VMEM((8, CAMS), f32)],
        compiler_params=params_of(),
    )(tile, light_directions, view_dirs)
    return dict(zip(TABLES, outs))


def shifted(x, by, nz):
    return lax.ppermute(x, "tile", [(2 * z + c, 2 * ((z + by) % nz) + c) for z in range(nz) for c in range(2)])


def on_device(observed, visible, params_start, light_directions, view_dirs, gains_start):
    samples = observed.shape[0]
    tiles = lax.axis_size("tile")
    nz = tiles // 2
    tile = lax.axis_index("tile")
    held = 2 * samples

    here = (tile + PLACE * lax.axis_index("grp")).astype(jnp.int32).reshape(1)
    send, first = pack_call(here, observed, params_start, visible, nz)
    got = lax.ppermute(send, "tile", [(i, i ^ 1) for i in range(tiles)])
    blocks = [first] + [shifted(first, s, nz) for s in range(1, nz)]
    vises = blocks
    tables = setup_call(here, light_directions, view_dirs, held)

    params = params_start
    gains = gains_start.reshape(1, LIGHTS)
    for iteration in range(ITERS):
        rights = sample_call(here, observed, got, gains, tables, blocks, vises, iteration > 0)
        if iteration > 0:
            *rights, params = rights
        low = normal_call(params, visible, gains, tables)
        moved = [rights[0]] + [shifted(rights[s], -s, nz) for s in range(1, nz)]
        closed = iteration + 1 == ITERS
        params, gains = settle(here, low, params, moved, gains, closed)
        if not closed:
            blocks = [params] + [shifted(params, s, nz) for s in range(1, nz)]
    return params, gains.reshape(LIGHTS)


def solution(mesh):
    return jax.shard_map(
        on_device,
        mesh=mesh,
        in_specs=(P("tile", "grp", None), P("grp", "tile"), P(None, "grp", "tile"), P(), P(), P()),
        out_specs=(P(None, "grp", "tile"), P()),
        check_vma=False,
    )
```

```python
import functools

import jax
import jax.numpy as jnp
from jax import lax
from jax.experimental import pallas as pl
from jax.experimental.pallas import tpu as pltpu
from jax.sharding import PartitionSpec as P

CAMS = 16
LIGHTS = 32
ITERS = 2

damping = 4.0
lift_z = 1.6
hidden = 1024.0
f32 = jnp.float32
bf16 = jnp.bfloat16
LANES = 128
VMEM_BYTES = 16 * 1024 * 1024
LINEAR = (2, 3, 5, 6, 7)
ENTRIES = [(i, j) for i in range(8) for j in range(i, 8)]


PLACE = 4096


def tile_of(ref):
    return lax.rem(ref[0], PLACE)


def row_is_odd(ref):
    return lax.rem(ref[0] // PLACE, 2) == 1


def column_is_odd(ref):
    return lax.rem(ref[0], 2) == 1


def split_value(x, count):
    pieces = []
    for _ in range(count - 1):
        head = x.astype(bf16).astype(f32)
        pieces.append(head)
        x = x - head
    pieces.append(x)
    return pieces


def split_pair(x):
    head = x.astype(bf16)
    return head, (x - head.astype(f32)).astype(bf16)


def dot(a, b):
    return jnp.dot(a, b, preferred_element_type=f32)


def total(terms):
    terms = list(terms)
    out = terms[0]
    for t in terms[1:]:
        out = out + t
    return out


def inner(a, b):
    return total(x * y for x, y in zip(a, b))


def texel_forms(p):
    tu, tv, diffuse, spec, raw, ambient, rim, retro = p
    q = 1.0 / jnp.sqrt(1.0 + tu * tu + tv * tv)
    nx, ny, nz = tu * q, tv * q, q
    side = -(nx * ny) * q
    by_u = ((1.0 - nx * nx) * q, side, -(nz * nx) * q)
    by_v = (side, (1.0 - ny * ny) * q, -(nz * ny) * q)
    sigma = 1.0 / (1.0 + jnp.exp(-raw))
    sharp = 1.0 + 20.0 * sigma
    slope = 20.0 * sigma * (1.0 - sigma)
    return (nx, ny, nz), by_u, by_v, sharp, slope


def seen(mask, c):
    return jnp.bitwise_and(jnp.right_shift(mask, c), 1).astype(f32)


def put_slab(ref, k, value):
    rows, cols = value.shape
    for h in range(cols // LANES):
        ref[h, k * rows : (k + 1) * rows, :] = value[:, h * LANES : (h + 1) * LANES]


def get_slab(ref, k, rows):
    return jnp.concatenate([ref[h, k * rows : (k + 1) * rows, :] for h in range(ref.shape[0])], axis=1)


def get_rows(ref, start, count, stride):
    return jnp.concatenate([ref[h, pl.ds(start, count, stride=stride), :] for h in range(ref.shape[0])], axis=1)


def put_rows(ref, start, stride, value):
    count, cols = value.shape
    for h in range(cols // LANES):
        ref[h, pl.ds(start, count, stride=stride), :] = value[:, h * LANES : (h + 1) * LANES]


def gain_columns(gains):
    same = pick(iota((LIGHTS, LIGHTS), 0) == iota((LIGHTS, LIGHTS), 1))
    tall = exact(same, jnp.broadcast_to(gains, (8, LIGHTS)), ((1,), (1,)))
    return jnp.broadcast_to(tall[:, 0:1], (LIGHTS, LANES))


def eights(x):
    return total(x[i : i + 8] for i in range(0, x.shape[0], 8))


def put_lobe_rows(slab, normal, sharp):
    base = [sharp * normal[0], sharp * normal[1], sharp * normal[2], -sharp]
    parts = [split_value(x, 3) for x in base]
    row = 0
    for which in (0, 1, 0, 2, 1, 0):
        for part in parts:
            slab(row, part[which])
            row += 1
    return row


def normal_kernel(
    par_ref, vis_ref, gain_ref, near_ref, cams_ref, lobe_ref, mixed_ref, tall_ref, out_ref,
    rows_ref, sums_ref, mixed_scr, gain_scr, cam_scr, gram_scr, lobe_scr,
):
    rows, cols = par_ref.shape[1], par_ref.shape[2]
    depth = lobe_ref.shape[1]
    chunk = 4 * LIGHTS
    chunks = CAMS // 4

    near, views = near_ref[...], cams_ref[...]
    gain2 = gain_ref[...] * gain_ref[...]
    grams = [jnp.sum(near * near[i : i + 1] * gain2, axis=1, keepdims=True) for i in range(4)]
    for i in range(4):
        gram_scr[8 * i : 8 * i + 8, :] = jnp.broadcast_to(grams[i], (8, LANES))
    spread = [total(grams[i][k : k + 1] * views[k : k + 1] for k in range(3)) for i in range(4)]
    echo_sq = total(spread[k] * views[k : k + 1] for k in range(3))
    row = iota(views.shape, 0)
    full = jnp.where(row == 3, echo_sq, jnp.where(row == 4, spread[3], views))
    for c in range(CAMS):
        cam_scr[8 * c : 8 * c + 8, :] = jnp.broadcast_to(full[:, c : c + 1], (8, LANES))

    gain_scr[...] = gain_columns(gain2)
    across = CAMS * LIGHTS
    at_light = pick(iota((LIGHTS, across), 1) % LIGHTS == iota((LIGHTS, across), 0))
    gain2 = exact(jnp.broadcast_to(gain2, (8, LIGHTS)), at_light, ((1,), (0,)))[0:1]
    for src, dst in ((mixed_ref, mixed_scr),):
        head, tail = split_pair(src[...] * gain2)
        count = src.shape[0]
        for ch in range(chunks):
            part = slice(ch * chunk, (ch + 1) * chunk)
            first = slice(2 * ch * chunk, (2 * ch + 1) * chunk)
            second = slice((2 * ch + 1) * chunk, (2 * ch + 2) * chunk)
            dst[0:count, first] = head[:, part]
            dst[0:count, second] = head[:, part]
            dst[count : 2 * count, first] = tail[:, part]
            dst[count : 2 * count, second] = jnp.zeros((count, chunk), bf16)

    def slab(k, value):
        put_slab(rows_ref, k, value)

    p = [par_ref[i] for i in range(8)]
    normal, _, _, sharp, _ = texel_forms(p)
    used = put_lobe_rows(slab, normal, sharp)
    mask = vis_ref[...]
    for c in range(CAMS):
        slab(used + c, (seen(mask, c) - 1.0) * hidden)
    for k in range(used + CAMS, depth):
        slab(k, jnp.zeros((rows, cols), f32))

    quads = [(i, j) for i in range(4) for j in range(i, 4)]

    def one_row(r):
        texel = get_rows(rows_ref, r, depth, rows).astype(bf16)
        mixed = jnp.zeros((16, cols), f32)
        bent = {(h, ij): None for h in range(cols // LANES) for ij in quads}
        for ch in range(chunks):
            for c in range(4):
                part = slice(ch * chunk + c * LIGHTS, ch * chunk + (c + 1) * LIGHTS)
                lobe = jnp.exp(dot(lobe_ref[part, :], texel))
                head, tail = split_pair(lobe)
                lobe_scr[r, ch, c * LIGHTS : (c + 1) * LIGHTS, :] = head
                lobe_scr[r, ch, chunk + c * LIGHTS : chunk + (c + 1) * LIGHTS, :] = tail
                tall = [None] + [tall_ref[k, part, :] for k in range(3)]
                for h in range(cols // LANES):
                    lobe_h = lobe[:, h * LANES : (h + 1) * LANES]
                    single = [lobe_h * lobe_h * gain_scr[...]]
                    single += [single[0] * tall[k] for k in (1, 2, 3)]
                    for i, j in quads:
                        value = eights(single[j] if i == 0 else single[i] * tall[j])
                        old = bent[h, (i, j)]
                        bent[h, (i, j)] = value if old is None else old + value
            at = slice(2 * ch * chunk, (2 * ch + 2) * chunk)
            both = dot(mixed_scr[:, at], lobe_scr[r, ch])
            got = both[0:32] + both[32:64]
            mixed = mixed + got[0:16]
            put_rows(sums_ref, (32 + 16 * ch) * rows + r, rows, got[16:32])
        put_rows(sums_ref, r, rows, mixed)
        for h in range(cols // LANES):
            for k, ij in enumerate(quads):
                line = (16 + k) * rows + r
                sums_ref[h, line : line + 1, :] = jnp.sum(bent[h, ij], axis=0, keepdims=True)

    for r in range(rows):
        one_row(r)

    def one_part(h, carry):
        at = pl.ds(pl.multiple_of(h * LANES, LANES), LANES)

        def cam(c, i):
            return cam_scr[8 * c + i : 8 * c + i + 1, :]

        def sums(k):
            return sums_ref[h, k * rows : (k + 1) * rows, :]

        p = [par_ref[i, :, at] for i in range(8)]
        mask = vis_ref[:, at]
        normal, by_u, by_v, sharp, slope = texel_forms(p)
        diffuse, spec, rim = p[2], p[3], p[6]
        zero = jnp.zeros((rows, LANES), f32)
        gam = {i: zero for i in (0, 1, 5, 6)}
        own = {(i, j): zero for i in (0, 1, 5, 6) for j in (0, 1, 5, 6) if i <= j and j != 5 and i != 5}
        lit = {i: zero for i in (0, 1, 5, 6)}
        grid = {(i, k): zero for i in (0, 1, 5, 6) for k in range(4)}
        echo_sq = zero
        view_sum = [zero, zero, zero]
        for c in range(CAMS):
            w = seen(mask, c)
            v = [cam(c, i) for i in range(3)]
            back = 1.0 - inner(v, normal)
            turn = (-2.0 * rim) * back
            shape = {0: turn * inner(v, by_u), 1: turn * inner(v, by_v), 6: back * back}
            weighted = {i: w * shape[i] for i in shape}
            weighted[5] = w
            for i in gam:
                gam[i] = gam[i] + weighted[i]
                lit[i] = lit[i] + weighted[i] * cam(c, 4)
            for i, j in own:
                own[i, j] = own[i, j] + weighted[i] * shape[j]
            echo_sq = echo_sq + w * cam(c, 3)
            view_sum = [s + w * x for s, x in zip(view_sum, v)]
            for k in range(4):
                peak = sums(32 + 4 * c + k)
                for i in (0, 1, 6):
                    grid[i, k] = grid[i, k] + shape[i] * peak
                grid[5, k] = grid[5, k] + peak
        own[5, 5] = gam[5]
        for i in (0, 1):
            own[i, 5] = gam[i]
        own[5, 6] = gam[6]

        def gram(i, j):
            return gram_scr[8 * i + j : 8 * i + j + 1, :]

        entries = {ij: None for ij in ENTRIES}

        def add(i, j, value):
            ij = (min(i, j), max(i, j))
            entries[ij] = value if entries[ij] is None else entries[ij] + value

        def cross(i, j, value):
            add(i, j, value + value if i == j else value)

        flat = {0: [diffuse * x for x in by_u], 1: [diffuse * x for x in by_v], 2: list(normal)}
        edge = spec * sharp
        tilt = spec * slope
        glow = {
            0: {1 + k: edge * by_u[k] for k in range(3)},
            1: {1 + k: edge * by_v[k] for k in range(3)},
            3: {0: None},
            4: {0: -tilt, 1: tilt * normal[0], 2: tilt * normal[1], 3: tilt * normal[2]},
        }

        def combine(coefs, values):
            return total(values[k] if x is None else x * values[k] for k, x in coefs.items())

        count = gam[5]
        spread = {i: [total(gram(r, k) * flat[i][k] for k in range(3)) for r in range(3)] for i in flat}
        reach = {i: total(gram(3, k) * flat[i][k] for k in range(3)) for i in flat}
        view_spread = [total(gram(r, k) * view_sum[k] for k in range(3)) for r in range(3)]
        for i in flat:
            for j in flat:
                if i <= j:
                    add(i, j, count * inner(flat[j], spread[i]))
            for j in gam:
                cross(i, j, reach[i] * gam[j])
            cross(i, 7, inner(flat[i], view_spread))
        for i, j in own:
            add(i, j, gram(3, 3) * own[i, j])
        for i in lit:
            cross(i, 7, lit[i])
        add(7, 7, echo_sq)
        for j in glow:
            for i in flat:
                cross(i, j, total(flat[i][x] * combine(glow[j], {k: sums(4 * k + x) for k in glow[j]}) for x in range(3)))
            for i in gam:
                cross(i, j, combine(glow[j], {k: grid[i, k] for k in glow[j]}))
            cross(j, 7, combine(glow[j], {k: sums(4 * k + 3) for k in glow[j]}))
        packed = {}
        where = 0
        for i in range(4):
            for j in range(i, 4):
                packed[i, j] = packed[j, i] = where
                where += 1
        for i in glow:
            for j in glow:
                if i <= j:
                    half = {k: combine(glow[j], {x: sums(16 + packed[k, x]) for x in glow[j]}) for k in glow[i]}
                    add(i, j, combine(glow[i], half))

        def entry(i, j):
            return entries[min(i, j), max(i, j)]

        for i in range(8):
            out_ref[36 + i, :, at] = total(entry(i, j) * p[j] for j in LINEAR)
        lower = {}
        for j in range(8):
            accum = entries[j, j] + damping
            for k in range(j):
                accum = accum - lower[j, k] * lower[j, k]
            inverse = lax.rsqrt(accum)
            lower[j, j] = inverse
            for i in range(j + 1, 8):
                accum = entries[j, i]
                for k in range(j):
                    accum = accum - lower[i, k] * lower[j, k]
                lower[i, j] = accum * inverse
        for where, (i, j) in enumerate(ENTRIES):
            out_ref[where, :, at] = lower[j, i]
        return carry

    lax.fori_loop(0, cols // LANES, one_part, 0)


def sample_kernel(
    tile_ref, own_ref, got_ref, gain_ref, lobe_ref, shade_ref, plain_ref, tall_ref, slab_ref, *refs, parts, mend
):
    par_refs, vis_refs = refs[:parts], refs[parts : 2 * parts]
    out_refs = refs[2 * parts : 3 * parts]
    extra = 1 if mend else 0
    own_out_refs = refs[3 * parts : 3 * parts + extra]
    par_scr, vis_scr, obs_scr, rows_ref, sums_ref, light_scr, gain_scr, plain_scr, flat_scr = refs[3 * parts + extra :]
    step = pl.program_id(0)
    samples, rows, cols = own_ref.shape
    held = 2 * samples
    cams = held // LIGHTS
    for s in range(parts):

        @pl.when(step == s)
        def _():
            par_scr[...] = par_refs[s][0:8]
            if mend:
                side = column_is_odd(tile_ref)
                chip = lax.rem(tile_of(tile_ref) // 2 + (parts - s), parts)
                inside = jnp.where(side, chip, parts - 1 - chip) < parts - 1
                lane = iota((rows, cols), 1)
                hit = jnp.logical_and(lane == jnp.where(side, cols - 1, 0), inside)
                lower, upper = par_refs[(s + 1) % parts], par_refs[(s - 1) % parts]
                for k in range(2):
                    end = jnp.where(side, upper[8, :, k : k + 1], lower[8, :, k : k + 1])
                    par_scr[k] = par_refs[s][k] + jnp.where(hit, end, 0.0)
                if s == 0:
                    own_out_refs[0][...] = par_scr[...]
            vis_scr[...] = vis_refs[s][8].astype(jnp.int32)

    core = tile_of(tile_ref) % 2
    mine = pl.multiple_of(core * (samples * rows), rows)
    theirs = pl.multiple_of((1 - core) * (samples * rows), rows)
    for h in range(cols // LANES):
        lanes = slice(h * LANES, (h + 1) * LANES)
        for src, at in ((own_ref, mine), (got_ref, theirs)):
            obs_scr[h, pl.ds(at, samples * rows), :] = src[:, :, lanes].astype(f32).reshape(samples * rows, LANES)

    def slab(k, value):
        put_slab(rows_ref, k, value)

    p = [par_scr[i] for i in range(8)]
    mask = vis_scr[...]
    normal, by_u, by_v, sharp, slope = texel_forms(p)
    base = (tile_of(tile_ref) // 2) * cams

    def cam(c, i):
        return slab_ref[8 * c + i : 8 * c + i + 1, :][:, 0:1]

    used = put_lobe_rows(slab, normal, sharp)
    weights = [seen(mask, base + c) for c in range(cams)]
    for c in range(cams):
        slab(used + c, (weights[c] - 1.0) * hidden)
        slab(65 + c, weights[c])
    for k in range(used + cams, 32):
        slab(k, jnp.zeros((rows, cols), f32))
    shade = [p[2] * normal[0], p[2] * normal[1], p[2] * normal[2], p[5], p[7]]
    pieces = [split_value(x, 2) for x in shade]
    at = 32
    for which in (0, 1, 0):
        for piece in pieces:
            slab(at, piece[which])
            at += 1
    for c in range(cams):
        back = 1.0 - inner([cam(c, i) for i in range(3)], normal)
        head, tail = split_value(p[6] * (back * back), 2)
        slab(at + c, head)
        slab(at + cams + c, tail)
    for k in range(at + 2 * cams, 64):
        slab(k, jnp.zeros((rows, cols), f32))
    slab(64, p[3])

    @pl.when(step == 0)
    def _():
        at_light = pick(iota((LIGHTS, held), 1) % LIGHTS == iota((LIGHTS, held), 0))
        gains = exact(jnp.broadcast_to(gain_ref[...], (8, LIGHTS)), at_light, ((1,), (0,)))[0:1]
        plain_scr[...] = jnp.concatenate(split_value(plain_ref[...] * gains, 2), axis=0).astype(bf16)
        gain_scr[...] = gain_columns(gain_ref[...])

    count = plain_ref.shape[0]

    def fold(x):
        return total(x[:, k * LANES : (k + 1) * LANES] for k in range(cols // LANES))

    def one_row(r, lift, energy):
        texel = get_rows(rows_ref, r, 32, rows).astype(bf16)
        tint = get_rows(rows_ref, 32 * rows + r, 32, rows).astype(bf16)
        misc = get_rows(rows_ref, 64 * rows + r, 8, rows)
        peak = {}
        for c in range(cams):
            part = slice(c * LIGHTS, (c + 1) * LIGHTS)
            lobe = jnp.exp(dot(lobe_ref[part, :], texel))
            full = dot(shade_ref[part, :], tint) + misc[0:1] * lobe
            obs = get_rows(obs_scr, c * LIGHTS * rows + r, LIGHTS, rows)
            kept = full * misc[1 + c : 2 + c]
            lift = lift + fold(kept * obs)
            energy = energy + fold(kept * full)
            flat_scr[r, part, :] = obs.astype(bf16)
            lit = obs * lobe
            for h in range(cols // LANES):
                base = lit[:, h * LANES : (h + 1) * LANES] * gain_scr[...]
                for k in range(4):
                    value = eights(base if k == 0 else base * tall_ref[k - 1, part, :])
                    peak[h, k] = value if c == 0 else peak[h, k] + value
        both = dot(plain_scr[...], flat_scr[r])
        put_rows(sums_ref, r, rows, both[0:count] + both[count : 2 * count])
        for h, k in peak:
            line = (count + k) * rows + r
            sums_ref[h, line : line + 1, :] = jnp.sum(peak[h, k], axis=0, keepdims=True)
        return lift, energy

    lift = energy = jnp.zeros((LIGHTS, LANES), f32)
    for r in range(rows):
        lift, energy = one_row(r, lift, energy)

    @pl.when(step == 0)
    def _():
        light_scr[0:LIGHTS, :] = lift
        light_scr[LIGHTS : 2 * LIGHTS, :] = energy

    @pl.when(step != 0)
    def _():
        light_scr[0:LIGHTS, :] = light_scr[0:LIGHTS, :] + lift
        light_scr[LIGHTS : 2 * LIGHTS, :] = light_scr[LIGHTS : 2 * LIGHTS, :] + energy

    @pl.when(step == parts - 1)
    def _():
        out_refs[parts - 1][8] = jnp.zeros((rows, cols), f32)
        for k in range(2):
            part = light_scr[k * LIGHTS : (k + 1) * LIGHTS, :]
            line = exact(jnp.ones((8, LANES), f32), part, ((1,), (1,)))[0:1]
            for ref in out_refs:
                ref[8, k : k + 1, 0:LIGHTS] = line

    def sums(k):
        return get_slab(sums_ref, k, rows)

    flat = [None, None, None]
    lone, rim_sum, echo_sum, turn_u, turn_v = None, None, None, None, None

    def grow(old, new):
        return new if old is None else old + new

    for c in range(cams):
        v = [cam(c, i) for i in range(3)]
        w = weights[c]
        one = w * sums(4 * c)
        lit = [w * sums(4 * c + 1 + x) for x in range(3)]
        back = 1.0 - inner(v, normal)
        bent = back * one
        lone = grow(lone, one)
        rim_sum = grow(rim_sum, back * bent)
        turn_u = grow(turn_u, bent * inner(v, by_u))
        turn_v = grow(turn_v, bent * inner(v, by_v))
        echo_sum = grow(echo_sum, inner(v, lit))
        flat = [grow(f, x) for f, x in zip(flat, lit)]
    spot = sums(count)
    spots = [sums(count + 1 + x) for x in range(3)]
    edge = p[3] * sharp
    twice = -2.0 * p[6]
    right = [
        p[2] * inner(by_u, flat) + edge * inner(by_u, spots) + twice * turn_u,
        p[2] * inner(by_v, flat) + edge * inner(by_v, spots) + twice * turn_v,
        inner(normal, flat),
        spot,
        p[3] * slope * (inner(normal, spots) - spot),
        lone,
        rim_sum,
        echo_sum,
    ]
    for s in range(parts):

        @pl.when(step == s)
        def _():
            for i in range(8):
                out_refs[s][i] = right[i]
            if s < parts - 1:
                out_refs[s][8] = jnp.zeros((rows, cols), f32)


def ring_total(terms):
    while len(terms) > 1:
        half = len(terms) // 2
        terms = [terms[k] + terms[k + half] for k in range(half)]
    return terms[0]


def solve_kernel(tile_ref, low_ref, par_ref, *refs):
    right_refs, (out_ref, sent_ref) = refs[:-2], refs[-2:]
    lower = {}
    for where, (i, j) in enumerate(ENTRIES):
        lower[j, i] = low_ref[where]
    right = [total(ref[i] for ref in right_refs) - low_ref[36 + i] for i in range(8)]
    forward = []
    for i in range(8):
        accum = right[i]
        for k in range(i):
            accum = accum - lower[i, k] * forward[k]
        forward.append(accum * lower[i, i])
    answer = [None] * 8
    for i in range(7, -1, -1):
        accum = forward[i]
        for k in range(i + 1, 8):
            accum = accum - lower[k, i] * answer[k]
        answer[i] = accum * lower[i, i]
    rows = par_ref.shape[1]
    sent_ref[...] = jnp.zeros(sent_ref.shape, f32)
    for i in range(8):
        fresh = par_ref[i] + answer[i]
        out_ref[i] = fresh
        if i < 2:
            sent_ref[i : i + 1, :] = fresh[0:1]
            sent_ref[2 + i : 3 + i, :] = fresh[rows - 1 : rows]
    sent_ref[4:6, 0:LANES] = ring_total([ref[8, 0:2, 0:LANES] for ref in right_refs])


def relay_kernel(tile_ref, sent_ref, first_ref, out_ref):
    odd = row_is_odd(tile_ref)
    out_ref[...] = sent_ref[...] + first_ref[...]
    out_ref[0:2, :] = jnp.where(odd, first_ref[0:2, :], first_ref[2:4, :])


def rows_kernel(tile_ref, par_ref, first_ref, edge_ref, *refs, last):
    light_refs, (tall_ref, near_ref, scr) = refs[:-3], refs[-3:]
    rows, cols = par_ref.shape[1:]
    place = tile_ref[0] // PLACE
    odd = row_is_odd(tile_ref)
    outer = jnp.where(jnp.logical_or(place == 0, place == last), 0.0, 1.0)
    near_ref[...] = jnp.zeros(near_ref.shape, f32)
    lane = iota((rows, LANES), 1)
    for k in range(2):
        other = outer * edge_ref[k : k + 1, :]
        scr[7:8, :] = jnp.where(odd, first_ref[2 + k : 3 + k, :], other)
        scr[8 : 8 + rows, :] = par_ref[k]
        scr[8 + rows : 9 + rows, :] = jnp.where(odd, other, first_ref[k : k + 1, :])
        tall = scr[7 : 7 + rows, :] + scr[8 : 8 + rows, :] + scr[9 : 9 + rows, :]
        tall_ref[k] = tall
        ends = jnp.where(lane == 0, tall[:, 0:1], jnp.where(lane == 1, tall[:, cols - 1 : cols], 0.0))
        near_ref[k * rows : (k + 1) * rows, :] = ends
    near_ref[2 * rows : 2 * rows + 2, :] = total(ref[4:6, 0:LANES] for ref in light_refs)


def smooth_kernel(tile_ref, par_ref, tall_ref, gain_ref, sent_ref, near_ref, *refs):
    far_refs, (out_ref, gain_out_ref) = refs[:-2], refs[-2:]
    rows, cols = par_ref.shape[1:]
    side = column_is_odd(tile_ref)
    lane = iota((rows, cols), 1)
    spill = jnp.zeros((rows, cols), f32)
    for k in range(2):
        at = slice(k * rows, (k + 1) * rows)
        tall = tall_ref[k]
        near_left, near_right = near_ref[at, 0:1], near_ref[at, 1:2]
        far_left = far_right = jnp.zeros((rows, 1), f32)
        if far_refs:
            far_left, far_right = far_refs[0][at, 0:1], far_refs[0][at, 1:2]
        before = jnp.where(side, near_right, far_right)
        after = jnp.where(side, far_left, near_left)
        left = jnp.where(lane == 0, before, pltpu.roll(tall, 1, 1))
        right = jnp.where(lane == cols - 1, after, pltpu.roll(tall, cols - 1, 1))
        out_ref[k] = 0.5 * par_ref[k] + (tall + left + right) * (0.5 / 9.0)
        spill = jnp.where(lane == k, jnp.where(side, near_left, near_right) * (0.5 / 9.0), spill)
    for k in range(2, 8):
        out_ref[k] = par_ref[k]
    if not far_refs:
        out_ref[8] = spill
    light = sent_ref[2 * rows : 2 * rows + 2, 0:LIGHTS] + near_ref[2 * rows : 2 * rows + 2, 0:LIGHTS]
    gains = gain_ref[...]
    gain_out_ref[...] = gains + (light[0:1] - gains * light[1:2]) / (light[1:2] + 1.0)


def smem():
    return pl.BlockSpec(memory_space=pltpu.SMEM)


def vmem():
    return pl.BlockSpec(memory_space=pltpu.VMEM)


def params_of():
    return pltpu.CompilerParams(vmem_limit_bytes=VMEM_BYTES)


def normal_call(par, vis, gains, tables):
    _, rows, cols = par.shape
    parts = cols // LANES
    small = [tables[n] for n in ("near", "cams", "lobe", "mixed", "tall")]
    return pl.pallas_call(
        normal_kernel,
        name="normal_factor",
        out_shape=jax.ShapeDtypeStruct((44, rows, cols), f32),
        in_specs=[vmem()] * 8,
        out_specs=vmem(),
        scratch_shapes=[
            pltpu.VMEM((parts, 48 * rows, LANES), f32),
            pltpu.VMEM((parts, 96 * rows, LANES), f32),
            pltpu.VMEM((64, 2 * CAMS * LIGHTS), bf16),
            pltpu.VMEM((LIGHTS, LANES), f32),
            pltpu.VMEM((8 * CAMS, LANES), f32),
            pltpu.VMEM((32, LANES), f32),
            pltpu.VMEM((rows, 4, 8 * LIGHTS, cols), bf16),
        ],
        compiler_params=params_of(),
    )(par, vis, gains, *small)


def sample_call(tile, own, got, gains, tables, pars, vises, mend):
    parts = len(pars)
    samples, rows, _ = own.shape
    cols = pars[0].shape[2]
    held = 2 * samples

    def full(x):
        zeros = (0,) * len(x.shape)
        return pl.BlockSpec(x.shape, lambda s, tile: zeros)

    def chip(s, tile):
        return lax.rem(tile_of(tile) // 2 + (parts - s), parts)

    outs = [jax.ShapeDtypeStruct((9, rows, cols), f32) for _ in range(parts)]
    if mend:
        outs.append(jax.ShapeDtypeStruct((8, rows, cols), f32))
    small = [gains] + [tables[n] for n in ("here", "shade", "plain", "near_tall", "slab")]
    return pl.pallas_call(
        functools.partial(sample_kernel, parts=parts, mend=mend),
        name="sample_sums",
        out_shape=outs,
        grid_spec=pltpu.PrefetchScalarGridSpec(
            num_scalar_prefetch=1,
            grid=(parts,),
            in_specs=[
                pl.BlockSpec((samples, rows, cols), lambda s, tile: (0, 0, 2 * chip(s, tile) + lax.rem(tile[0], 2))),
                pl.BlockSpec((samples, rows, cols), lambda s, tile: (0, 0, chip(s, tile))),
            ]
            + [full(x) for x in small]
            + [full(x) for x in pars]
            + [full(x) for x in vises],
            out_specs=[full(x) for x in outs],
            scratch_shapes=[
                pltpu.VMEM((8, rows, cols), f32),
                pltpu.VMEM((rows, cols), jnp.int32),
                pltpu.VMEM((cols // LANES, held * rows, LANES), f32),
                pltpu.VMEM((cols // LANES, 72 * rows, LANES), f32),
                pltpu.VMEM((cols // LANES, 32 * rows, LANES), f32),
                pltpu.VMEM((2 * LIGHTS, LANES), f32),
                pltpu.VMEM((LIGHTS, LANES), f32),
                pltpu.VMEM((2 * tables["plain"].shape[0], held), bf16),
                pltpu.VMEM((rows, held, cols), bf16),
            ],
        ),
        compiler_params=params_of(),
    )(tile, own, got, *small, *pars, *vises)


def pack_kernel(tile_ref, seen_ref, par_ref, vis_ref, send_ref, first_ref, vis_scr, sems):
    parts = sems.shape[0] - 2
    width = send_ref.shape[2] // parts
    copies = [
        pltpu.make_async_copy(vis_ref, vis_scr, sems.at[parts]),
        pltpu.make_async_copy(par_ref, first_ref.at[0:8], sems.at[parts + 1]),
    ]
    copies[0].start()
    copies[1].start()
    for z in range(parts):
        start = pl.multiple_of((2 * z + 1 - lax.rem(tile_ref[0], 2)) * width, LANES)
        copies.append(
            pltpu.make_async_copy(
                seen_ref.at[:, :, pl.ds(start, width)],
                send_ref.at[:, :, z * width : (z + 1) * width],
                sems.at[z],
            )
        )
        copies[z + 2].start()
    copies[0].wait()
    first_ref[8] = vis_scr[...].astype(f32)
    for copy in copies[1:]:
        copy.wait()


def pack_call(tile, observed, params, visible, parts):
    far = pl.BlockSpec(memory_space=pltpu.MemorySpace.HBM)
    samples, rows, width = observed.shape
    return pl.pallas_call(
        pack_kernel,
        name="pack",
        out_shape=[
            jax.ShapeDtypeStruct((samples, rows, width // 2), observed.dtype),
            jax.ShapeDtypeStruct((9,) + params.shape[1:], f32),
        ],
        in_specs=[smem(), far, far, far],
        out_specs=[far, vmem()],
        scratch_shapes=[pltpu.VMEM(visible.shape, jnp.int32), pltpu.SemaphoreType.DMA((parts + 2,))],
        compiler_params=params_of(),
    )(tile, *[pltpu.with_memory_space_constraint(x, pltpu.MemorySpace.HBM) for x in (observed, params, visible)])


def plain_call(kernel, name, shapes, scratch, tile, *args):
    return pl.pallas_call(
        kernel,
        name=name,
        out_shape=[jax.ShapeDtypeStruct(shape, f32) for shape in shapes],
        in_specs=[smem()] + [vmem()] * len(args),
        out_specs=[vmem()] * len(shapes),
        scratch_shapes=[pltpu.VMEM(shape, f32) for shape in scratch],
        compiler_params=params_of(),
    )(tile, *args)


def pairs(count, start):
    out = []
    for i in range(start, count - 1, 2):
        out += [(i, i + 1), (i + 1, i)]
    return out


def settle(tile, low, params, moved, gains, closed):
    _, rows, cols = params.shape
    grps, tiles = lax.axis_size("grp"), lax.axis_size("tile")
    strip = (8, cols)
    params, sent = plain_call(solve_kernel, "solve", [params.shape, strip], [], tile, low, params, *moved)
    first = lax.ppermute(sent, "grp", pairs(grps, 0))
    if grps == 4:
        (relay,) = plain_call(relay_kernel, "relay", [strip], [], tile, sent, first)
        edge = lax.ppermute(relay, "grp", [(i, i ^ 2) for i in range(grps)])
        lights = [relay, edge]
    else:
        second = lax.ppermute(sent, "grp", pairs(grps, 1))
        odd = lax.axis_index("grp") % 2 == 1
        edge = jnp.where(odd, second, jnp.roll(second, -2, axis=0))
        light = sent + first
        bit = 2
        while bit < grps:
            light = light + lax.ppermute(light, "grp", [(i, i ^ bit) for i in range(grps)])
            bit *= 2
        lights = [light]
    patch = (2 * rows + 8, LANES)
    tall, sent = plain_call(
        functools.partial(rows_kernel, last=grps - 1), "rows", [(2, rows, cols), patch], [(24, cols)],
        tile, params, first, edge, *lights,
    )
    ends = [lax.ppermute(sent, "tile", pairs(tiles, 1))] if closed else []
    near = lax.ppermute(sent, "tile", pairs(tiles, 0))
    slabs = 8 if closed else 9
    return plain_call(
        smooth_kernel, "smooth", [(slabs, rows, cols), gains.shape], [], tile, params, tall, gains, sent, near, *ends
    )


def exact(a, b, sides):
    return lax.dot_general(
        a, b, (sides, ((), ())), precision=lax.Precision.HIGHEST, preferred_element_type=f32
    )


def iota(shape, axis):
    return lax.broadcasted_iota(jnp.int32, shape, axis)


def pick(test):
    return jnp.where(test, 1.0, 0.0).astype(f32)


def setup_kernel(
    tile_ref, light_ref, view_ref,
    near_ref, cams_ref, lobe_ref, mixed_ref,
    here_ref, shade_ref, plain_ref, tall_ref, near_tall_ref, slab_ref, light_scr, view_scr,
):
    samples = lobe_ref.shape[0]
    held = here_ref.shape[0]
    cams = held // LIGHTS
    first = (tile_of(tile_ref) // 2) * cams

    def unit(raw_ref, scr):
        scr[...] = jnp.zeros(scr.shape, f32)
        scr[0:3, :] = raw_ref[...]
        scr[2:3, :] = scr[2:3, :] + lift_z
        lifted = scr[...]
        return lifted / jnp.sqrt(jnp.sum(lifted * lifted, axis=0, keepdims=True))

    lights = unit(light_ref, light_scr)
    views = unit(view_ref, view_scr)
    near = jnp.where(iota(lights.shape, 0) == 3, 1.0, lights)
    near_ref[...] = near
    cams_ref[...] = views

    def across(count, start, period):
        at_light = pick(iota((LIGHTS, count), 1) % LIGHTS == iota((LIGHTS, count), 0))
        at_view = pick(iota((CAMS, count), 1) // LIGHTS % period + start == iota((CAMS, count), 0))
        wide = exact(near, at_light, ((1,), (0,)))
        view = exact(views, at_view, ((1,), (0,)))
        row = iota((8, count), 0)
        raw = jnp.where(row < 3, wide + view, 0.0)
        half = raw / jnp.sqrt(jnp.sum(raw * raw, axis=0, keepdims=True))
        echo = jnp.sum(wide * view, axis=0, keepdims=True)
        return wide, half, echo

    def down(count, start):
        at_light = pick(iota((count, LIGHTS), 0) % LIGHTS == iota((count, LIGHTS), 1))
        at_view = pick(iota((count, CAMS), 0) // LIGHTS + start == iota((count, CAMS), 1))
        tall = exact(at_light, near, ((1,), (1,)))
        view = exact(at_view, views, ((1,), (1,)))
        lane = iota((count, 8), 1)
        raw = jnp.where(lane < 3, tall + view, 0.0)
        half = raw / jnp.sqrt(jnp.sum(raw * raw, axis=1, keepdims=True))
        half = jnp.where(lane == 3, 1.0, half)
        echo = jnp.sum(tall * view, axis=1, keepdims=True)
        return half, jnp.where(lane == 4, echo, tall)

    def spread(values, width, depth, order):
        lane = iota((8, depth), 1)
        out = None
        for which in range(max(order) + 1):
            head = values.astype(bf16)
            values = values - head.astype(f32)
            group = None
            for g, k in enumerate(order):
                if k == which:
                    hit = lane // width == g
                    group = hit if group is None else jnp.logical_or(group, hit)
            place = pick(jnp.logical_and(group, lane % width == iota((8, depth), 0)))
            place = jnp.where(iota((8, depth), 0) < width, place, 0.0).astype(bf16)
            got = dot(head, place)
            out = got if out is None else out + got
        return out

    wide, half, echo = across(samples, 0, CAMS)
    high = [jnp.ones((1, samples), f32)] + [half[k : k + 1] for k in range(3)]
    low = [wide[k : k + 1] for k in range(3)] + [echo]
    which = iota((1, samples), 1) // LIGHTS % 4
    for i in range(4):
        for j in range(4):
            mixed_ref[4 * i + j : 4 * i + j + 1, :] = high[i] * low[j]
            mixed_ref[16 + 4 * i + j : 17 + 4 * i + j, :] = jnp.where(which == i, high[j], 0.0)
    depth = lobe_ref.shape[1]
    half, _ = down(samples, 0)
    for k in range(3):
        tall_ref[k] = jnp.broadcast_to(half[:, k : k + 1], (samples, LANES))
    hot = pick(iota((samples, depth), 0) // LIGHTS + 24 == iota((samples, depth), 1))
    lobe_ref[...] = (spread(half, 4, depth, (0, 0, 1, 0, 1, 2)) + hot).astype(bf16)

    half, tall = down(held, first)
    for k in range(3):
        near_tall_ref[k] = jnp.broadcast_to(half[:, k : k + 1], (held, LANES))
    cam = iota((held, 32), 0) // LIGHTS
    lane = iota((held, 32), 1)
    hot = pick(cam + 24 == lane)
    here_ref[...] = (spread(half, 4, 32, (0, 0, 1, 0, 1, 2)) + hot).astype(bf16)
    hot = pick(cam + 15 == lane) + pick(cam + (15 + cams) == lane)
    shade_ref[...] = (spread(tall, 5, 32, (0, 0, 1)) + hot).astype(bf16)

    wide, _, _ = across(held, first, cams)
    plain_ref[...] = jnp.zeros(plain_ref.shape, f32)
    which = iota((1, held), 1) // LIGHTS
    for c in range(cams):
        plain_ref[4 * c : 4 * c + 1, :] = pick(which == c)
        for k in range(3):
            plain_ref[4 * c + 1 + k : 4 * c + 2 + k, :] = jnp.where(which == c, wide[k : k + 1], 0.0)
        mine = jnp.sum(jnp.where(iota(views.shape, 1) == first + c, views, 0.0), axis=1, keepdims=True)
        slab_ref[8 * c : 8 * c + 8, :] = jnp.broadcast_to(mine, (8, LANES))


TABLES = ("near", "cams", "lobe", "mixed", "here", "shade", "plain", "tall", "near_tall", "slab")


def setup_call(tile, light_directions, view_dirs, held):
    samples = CAMS * LIGHTS
    cams = held // LIGHTS
    count = max(8, 4 * cams)
    shapes = [
        ((8, LIGHTS), f32), ((8, CAMS), f32), ((samples, 48), bf16), ((32, samples), f32),
        ((held, 32), bf16), ((held, 32), bf16), ((count, held), f32),
        ((3, samples, LANES), f32), ((3, held, LANES), f32), ((8 * cams, LANES), f32),
    ]
    outs = pl.pallas_call(
        setup_kernel,
        name="tables",
        out_shape=[jax.ShapeDtypeStruct(a, b) for a, b in shapes],
        in_specs=[smem(), vmem(), vmem()],
        out_specs=[vmem()] * len(shapes),
        scratch_shapes=[pltpu.VMEM((8, LIGHTS), f32), pltpu.VMEM((8, CAMS), f32)],
        compiler_params=params_of(),
    )(tile, light_directions, view_dirs)
    return dict(zip(TABLES, outs))


def shifted(x, by, nz):
    return lax.ppermute(x, "tile", [(2 * z + c, 2 * ((z + by) % nz) + c) for z in range(nz) for c in range(2)])


def on_device(observed, visible, params_start, light_directions, view_dirs, gains_start):
    samples = observed.shape[0]
    tiles = lax.axis_size("tile")
    nz = tiles // 2
    tile = lax.axis_index("tile")
    held = 2 * samples

    here = (tile + PLACE * lax.axis_index("grp")).astype(jnp.int32).reshape(1)
    send, first = pack_call(here, observed, params_start, visible, nz)
    got = lax.ppermute(send, "tile", [(i, i ^ 1) for i in range(tiles)])
    blocks = [first] + [shifted(first, s, nz) for s in range(1, nz)]
    vises = blocks
    tables = setup_call(here, light_directions, view_dirs, held)

    params = params_start
    gains = gains_start.reshape(1, LIGHTS)
    for iteration in range(ITERS):
        rights = sample_call(here, observed, got, gains, tables, blocks, vises, iteration > 0)
        if iteration > 0:
            *rights, params = rights
        low = normal_call(params, visible, gains, tables)
        moved = [rights[0]] + [shifted(rights[s], -s, nz) for s in range(1, nz)]
        closed = iteration + 1 == ITERS
        params, gains = settle(here, low, params, moved, gains, closed)
        if not closed:
            blocks = [params] + [shifted(params, s, nz) for s in range(1, nz)]
    return params, gains.reshape(LIGHTS)


def solution(mesh):
    return jax.shard_map(
        on_device,
        mesh=mesh,
        in_specs=(P("tile", "grp", None), P("grp", "tile"), P(None, "grp", "tile"), P(), P(), P()),
        out_specs=(P(None, "grp", "tile"), P()),
        check_vma=False,
    )
```

```python
import functools

import jax
import jax.numpy as jnp
from jax import lax
from jax.experimental import pallas as pl
from jax.experimental.pallas import tpu as pltpu
from jax.sharding import PartitionSpec as P

CAMS = 16
LIGHTS = 32
ITERS = 2

damping = 4.0
lift_z = 1.6
hidden = 1024.0
f32 = jnp.float32
bf16 = jnp.bfloat16
LANES = 128
VMEM_BYTES = 16 * 1024 * 1024
LINEAR = (2, 3, 5, 6, 7)
ENTRIES = [(i, j) for i in range(8) for j in range(i, 8)]


PLACE = 4096


def tile_of(ref):
    return lax.rem(ref[0], PLACE)


def row_is_odd(ref):
    return lax.rem(ref[0] // PLACE, 2) == 1


def column_is_odd(ref):
    return lax.rem(ref[0], 2) == 1


def split_value(x, count):
    pieces = []
    for _ in range(count - 1):
        head = x.astype(bf16).astype(f32)
        pieces.append(head)
        x = x - head
    pieces.append(x)
    return pieces


def split_pair(x):
    head = x.astype(bf16)
    return head, (x - head.astype(f32)).astype(bf16)


def dot(a, b):
    return jnp.dot(a, b, preferred_element_type=f32)


def total(terms):
    terms = list(terms)
    out = terms[0]
    for t in terms[1:]:
        out = out + t
    return out


def inner(a, b):
    return total(x * y for x, y in zip(a, b))


def texel_forms(p):
    tu, tv, diffuse, spec, raw, ambient, rim, retro = p
    q = 1.0 / jnp.sqrt(1.0 + tu * tu + tv * tv)
    nx, ny, nz = tu * q, tv * q, q
    side = -(nx * ny) * q
    by_u = ((1.0 - nx * nx) * q, side, -(nz * nx) * q)
    by_v = (side, (1.0 - ny * ny) * q, -(nz * ny) * q)
    sigma = 1.0 / (1.0 + jnp.exp(-raw))
    sharp = 1.0 + 20.0 * sigma
    slope = 20.0 * sigma * (1.0 - sigma)
    return (nx, ny, nz), by_u, by_v, sharp, slope


def seen(mask, c):
    return jnp.bitwise_and(jnp.right_shift(mask, c), 1).astype(f32)


def put_slab(ref, k, value):
    rows, cols = value.shape
    for h in range(cols // LANES):
        ref[h, k * rows : (k + 1) * rows, :] = value[:, h * LANES : (h + 1) * LANES]


def get_slab(ref, k, rows):
    return jnp.concatenate([ref[h, k * rows : (k + 1) * rows, :] for h in range(ref.shape[0])], axis=1)


def get_rows(ref, start, count, stride):
    return jnp.concatenate([ref[h, pl.ds(start, count, stride=stride), :] for h in range(ref.shape[0])], axis=1)


def put_rows(ref, start, stride, value):
    count, cols = value.shape
    for h in range(cols // LANES):
        ref[h, pl.ds(start, count, stride=stride), :] = value[:, h * LANES : (h + 1) * LANES]


def gain_columns(gains):
    same = pick(iota((LIGHTS, LIGHTS), 0) == iota((LIGHTS, LIGHTS), 1))
    tall = exact(same, jnp.broadcast_to(gains, (8, LIGHTS)), ((1,), (1,)))
    return jnp.broadcast_to(tall[:, 0:1], (LIGHTS, LANES))


def eights(x):
    return total(x[i : i + 8] for i in range(0, x.shape[0], 8))


def put_lobe_rows(slab, normal, sharp):
    base = [sharp * normal[0], sharp * normal[1], sharp * normal[2], -sharp]
    parts = [split_value(x, 3) for x in base]
    row = 0
    for which in (0, 1, 0, 2, 1, 0):
        for part in parts:
            slab(row, part[which])
            row += 1
    return row


def normal_kernel(
    par_ref, vis_ref, gain_ref, near_ref, cams_ref, lobe_ref, mixed_ref, tall_ref, out_ref,
    rows_ref, sums_ref, mixed_scr, gain_scr, cam_scr, gram_scr, lobe_scr,
):
    rows, cols = par_ref.shape[1], par_ref.shape[2]
    depth = lobe_ref.shape[1]
    chunk = 4 * LIGHTS
    chunks = CAMS // 4

    near, views = near_ref[...], cams_ref[...]
    gain2 = gain_ref[...] * gain_ref[...]
    grams = [jnp.sum(near * near[i : i + 1] * gain2, axis=1, keepdims=True) for i in range(4)]
    for i in range(4):
        gram_scr[8 * i : 8 * i + 8, :] = jnp.broadcast_to(grams[i], (8, LANES))
    spread = [total(grams[i][k : k + 1] * views[k : k + 1] for k in range(3)) for i in range(4)]
    echo_sq = total(spread[k] * views[k : k + 1] for k in range(3))
    row = iota(views.shape, 0)
    full = jnp.where(row == 3, echo_sq, jnp.where(row == 4, spread[3], views))
    for c in range(CAMS):
        cam_scr[8 * c : 8 * c + 8, :] = jnp.broadcast_to(full[:, c : c + 1], (8, LANES))

    gain_scr[...] = gain_columns(gain2)
    across = CAMS * LIGHTS
    at_light = pick(iota((LIGHTS, across), 1) % LIGHTS == iota((LIGHTS, across), 0))
    gain2 = exact(jnp.broadcast_to(gain2, (8, LIGHTS)), at_light, ((1,), (0,)))[0:1]
    for src, dst in ((mixed_ref, mixed_scr),):
        head, tail = split_pair(src[...] * gain2)
        count = src.shape[0]
        for ch in range(chunks):
            part = slice(ch * chunk, (ch + 1) * chunk)
            first = slice(2 * ch * chunk, (2 * ch + 1) * chunk)
            second = slice((2 * ch + 1) * chunk, (2 * ch + 2) * chunk)
            dst[0:count, first] = head[:, part]
            dst[0:count, second] = head[:, part]
            dst[count : 2 * count, first] = tail[:, part]
            dst[count : 2 * count, second] = jnp.zeros((count, chunk), bf16)

    def slab(k, value):
        put_slab(rows_ref, k, value)

    p = [par_ref[i] for i in range(8)]
    normal, _, _, sharp, _ = texel_forms(p)
    used = put_lobe_rows(slab, normal, sharp)
    mask = vis_ref[...]
    for c in range(CAMS):
        slab(used + c, (seen(mask, c) - 1.0) * hidden)
    for k in range(used + CAMS, depth):
        slab(k, jnp.zeros((rows, cols), f32))

    quads = [(i, j) for i in range(4) for j in range(i, 4)]

    def one_row(r):
        texel = get_rows(rows_ref, r, depth, rows).astype(bf16)
        mixed = jnp.zeros((16, cols), f32)
        bent = {(h, ij): None for h in range(cols // LANES) for ij in quads}
        for ch in range(chunks):
            for c in range(4):
                part = slice(ch * chunk + c * LIGHTS, ch * chunk + (c + 1) * LIGHTS)
                lobe = jnp.exp(dot(lobe_ref[part, :], texel))
                head, tail = split_pair(lobe)
                lobe_scr[r, ch, c * LIGHTS : (c + 1) * LIGHTS, :] = head
                lobe_scr[r, ch, chunk + c * LIGHTS : chunk + (c + 1) * LIGHTS, :] = tail
                tall = [None] + [tall_ref[k, part, :] for k in range(3)]
                for h in range(cols // LANES):
                    lobe_h = lobe[:, h * LANES : (h + 1) * LANES]
                    single = [lobe_h * lobe_h * gain_scr[...]]
                    single += [single[0] * tall[k] for k in (1, 2, 3)]
                    for i, j in quads:
                        value = eights(single[j] if i == 0 else single[i] * tall[j])
                        old = bent[h, (i, j)]
                        bent[h, (i, j)] = value if old is None else old + value
            at = slice(2 * ch * chunk, (2 * ch + 2) * chunk)
            both = dot(mixed_scr[:, at], lobe_scr[r, ch])
            got = both[0:32] + both[32:64]
            mixed = mixed + got[0:16]
            put_rows(sums_ref, (32 + 16 * ch) * rows + r, rows, got[16:32])
        put_rows(sums_ref, r, rows, mixed)
        for h in range(cols // LANES):
            for k, ij in enumerate(quads):
                line = (16 + k) * rows + r
                sums_ref[h, line : line + 1, :] = jnp.sum(bent[h, ij], axis=0, keepdims=True)

    for r in range(rows):
        one_row(r)

    def one_part(h, carry):
        at = pl.ds(pl.multiple_of(h * LANES, LANES), LANES)

        def cam(c, i):
            return cam_scr[8 * c + i : 8 * c + i + 1, :]

        def sums(k):
            return sums_ref[h, k * rows : (k + 1) * rows, :]

        p = [par_ref[i, :, at] for i in range(8)]
        mask = vis_ref[:, at]
        normal, by_u, by_v, sharp, slope = texel_forms(p)
        diffuse, spec, rim = p[2], p[3], p[6]
        zero = jnp.zeros((rows, LANES), f32)
        gam = {i: zero for i in (0, 1, 5, 6)}
        own = {(i, j): zero for i in (0, 1, 5, 6) for j in (0, 1, 5, 6) if i <= j and j != 5 and i != 5}
        lit = {i: zero for i in (0, 1, 5, 6)}
        grid = {(i, k): zero for i in (0, 1, 5, 6) for k in range(4)}
        echo_sq = zero
        view_sum = [zero, zero, zero]
        for c in range(CAMS):
            w = seen(mask, c)
            v = [cam(c, i) for i in range(3)]
            back = 1.0 - inner(v, normal)
            turn = (-2.0 * rim) * back
            shape = {0: turn * inner(v, by_u), 1: turn * inner(v, by_v), 6: back * back}
            weighted = {i: w * shape[i] for i in shape}
            weighted[5] = w
            for i in gam:
                gam[i] = gam[i] + weighted[i]
                lit[i] = lit[i] + weighted[i] * cam(c, 4)
            for i, j in own:
                own[i, j] = own[i, j] + weighted[i] * shape[j]
            echo_sq = echo_sq + w * cam(c, 3)
            view_sum = [s + w * x for s, x in zip(view_sum, v)]
            for k in range(4):
                peak = sums(32 + 4 * c + k)
                for i in (0, 1, 6):
                    grid[i, k] = grid[i, k] + shape[i] * peak
                grid[5, k] = grid[5, k] + peak
        own[5, 5] = gam[5]
        for i in (0, 1):
            own[i, 5] = gam[i]
        own[5, 6] = gam[6]

        def gram(i, j):
            return gram_scr[8 * i + j : 8 * i + j + 1, :]

        entries = {ij: None for ij in ENTRIES}

        def add(i, j, value):
            ij = (min(i, j), max(i, j))
            entries[ij] = value if entries[ij] is None else entries[ij] + value

        def cross(i, j, value):
            add(i, j, value + value if i == j else value)

        flat = {0: [diffuse * x for x in by_u], 1: [diffuse * x for x in by_v], 2: list(normal)}
        edge = spec * sharp
        tilt = spec * slope
        glow = {
            0: {1 + k: edge * by_u[k] for k in range(3)},
            1: {1 + k: edge * by_v[k] for k in range(3)},
            3: {0: None},
            4: {0: -tilt, 1: tilt * normal[0], 2: tilt * normal[1], 3: tilt * normal[2]},
        }

        def combine(coefs, values):
            return total(values[k] if x is None else x * values[k] for k, x in coefs.items())

        count = gam[5]
        spread = {i: [total(gram(r, k) * flat[i][k] for k in range(3)) for r in range(3)] for i in flat}
        reach = {i: total(gram(3, k) * flat[i][k] for k in range(3)) for i in flat}
        view_spread = [total(gram(r, k) * view_sum[k] for k in range(3)) for r in range(3)]
        for i in flat:
            for j in flat:
                if i <= j:
                    add(i, j, count * inner(flat[j], spread[i]))
            for j in gam:
                cross(i, j, reach[i] * gam[j])
            cross(i, 7, inner(flat[i], view_spread))
        for i, j in own:
            add(i, j, gram(3, 3) * own[i, j])
        for i in lit:
            cross(i, 7, lit[i])
        add(7, 7, echo_sq)
        for j in glow:
            for i in flat:
                cross(i, j, total(flat[i][x] * combine(glow[j], {k: sums(4 * k + x) for k in glow[j]}) for x in range(3)))
            for i in gam:
                cross(i, j, combine(glow[j], {k: grid[i, k] for k in glow[j]}))
            cross(j, 7, combine(glow[j], {k: sums(4 * k + 3) for k in glow[j]}))
        packed = {}
        where = 0
        for i in range(4):
            for j in range(i, 4):
                packed[i, j] = packed[j, i] = where
                where += 1
        for i in glow:
            for j in glow:
                if i <= j:
                    half = {k: combine(glow[j], {x: sums(16 + packed[k, x]) for x in glow[j]}) for k in glow[i]}
                    add(i, j, combine(glow[i], half))

        def entry(i, j):
            return entries[min(i, j), max(i, j)]

        for i in range(8):
            out_ref[36 + i, :, at] = total(entry(i, j) * p[j] for j in LINEAR)
        lower = {}
        for j in range(8):
            accum = entries[j, j] + damping
            for k in range(j):
                accum = accum - lower[j, k] * lower[j, k]
            inverse = lax.rsqrt(accum)
            lower[j, j] = inverse
            for i in range(j + 1, 8):
                accum = entries[j, i]
                for k in range(j):
                    accum = accum - lower[i, k] * lower[j, k]
                lower[i, j] = accum * inverse
        for where, (i, j) in enumerate(ENTRIES):
            out_ref[where, :, at] = lower[j, i]
        return carry

    lax.fori_loop(0, cols // LANES, one_part, 0)


def sample_kernel(
    tile_ref, own_ref, got_ref, gain_ref, lobe_ref, shade_ref, plain_ref, tall_ref, slab_ref, *refs, parts, mend
):
    par_refs, vis_refs = by_shift(refs[:parts]), by_shift(refs[parts : 2 * parts])
    out_refs = refs[2 * parts : 3 * parts]
    extra = 1 if mend else 0
    own_out_refs = refs[3 * parts : 3 * parts + extra]
    par_scr, vis_scr, obs_scr, rows_ref, sums_ref, light_scr, gain_scr, plain_scr, flat_scr = refs[3 * parts + extra :]
    step = pl.program_id(0)
    samples, rows, cols = own_ref.shape
    held = 2 * samples
    cams = held // LIGHTS
    for s in range(parts):

        @pl.when(step == s)
        def _():
            par_scr[...] = par_refs[s][0:8]
            if mend:
                side = column_is_odd(tile_ref)
                chip = lax.rem(tile_of(tile_ref) // 2 + (parts - s), parts)
                inside = jnp.where(side, chip, parts - 1 - chip) < parts - 1
                lane = iota((rows, cols), 1)
                hit = jnp.logical_and(lane == jnp.where(side, cols - 1, 0), inside)
                lower, upper = par_refs[(s + 1) % parts], par_refs[(s - 1) % parts]
                for k in range(2):
                    end = jnp.where(side, upper[8, :, k : k + 1], lower[8, :, k : k + 1])
                    par_scr[k] = par_refs[s][k] + jnp.where(hit, end, 0.0)
                if s == 0:
                    own_out_refs[0][...] = par_scr[...]
            vis_scr[...] = vis_refs[s][8].astype(jnp.int32)

    core = tile_of(tile_ref) % 2
    mine = pl.multiple_of(core * (samples * rows), rows)
    theirs = pl.multiple_of((1 - core) * (samples * rows), rows)
    for h in range(cols // LANES):
        lanes = slice(h * LANES, (h + 1) * LANES)
        for src, at in ((own_ref, mine), (got_ref, theirs)):
            obs_scr[h, pl.ds(at, samples * rows), :] = src[:, :, lanes].astype(f32).reshape(samples * rows, LANES)

    def slab(k, value):
        put_slab(rows_ref, k, value)

    p = [par_scr[i] for i in range(8)]
    mask = vis_scr[...]
    normal, by_u, by_v, sharp, slope = texel_forms(p)
    base = (tile_of(tile_ref) // 2) * cams

    def cam(c, i):
        return slab_ref[8 * c + i : 8 * c + i + 1, :][:, 0:1]

    used = put_lobe_rows(slab, normal, sharp)
    weights = [seen(mask, base + c) for c in range(cams)]
    for c in range(cams):
        slab(used + c, (weights[c] - 1.0) * hidden)
        slab(65 + c, weights[c])
    for k in range(used + cams, 32):
        slab(k, jnp.zeros((rows, cols), f32))
    shade = [p[2] * normal[0], p[2] * normal[1], p[2] * normal[2], p[5], p[7]]
    pieces = [split_value(x, 2) for x in shade]
    at = 32
    for which in (0, 1, 0):
        for piece in pieces:
            slab(at, piece[which])
            at += 1
    for c in range(cams):
        back = 1.0 - inner([cam(c, i) for i in range(3)], normal)
        head, tail = split_value(p[6] * (back * back), 2)
        slab(at + c, head)
        slab(at + cams + c, tail)
    for k in range(at + 2 * cams, 64):
        slab(k, jnp.zeros((rows, cols), f32))
    slab(64, p[3])

    @pl.when(step == 0)
    def _():
        at_light = pick(iota((LIGHTS, held), 1) % LIGHTS == iota((LIGHTS, held), 0))
        gains = exact(jnp.broadcast_to(gain_ref[...], (8, LIGHTS)), at_light, ((1,), (0,)))[0:1]
        plain_scr[...] = jnp.concatenate(split_value(plain_ref[...] * gains, 2), axis=0).astype(bf16)
        gain_scr[...] = gain_columns(gain_ref[...])

    count = plain_ref.shape[0]

    def fold(x):
        return total(x[:, k * LANES : (k + 1) * LANES] for k in range(cols // LANES))

    def one_row(r, lift, energy):
        texel = get_rows(rows_ref, r, 32, rows).astype(bf16)
        tint = get_rows(rows_ref, 32 * rows + r, 32, rows).astype(bf16)
        misc = get_rows(rows_ref, 64 * rows + r, 8, rows)
        peak = {}
        for c in range(cams):
            part = slice(c * LIGHTS, (c + 1) * LIGHTS)
            lobe = jnp.exp(dot(lobe_ref[part, :], texel))
            full = dot(shade_ref[part, :], tint) + misc[0:1] * lobe
            obs = get_rows(obs_scr, c * LIGHTS * rows + r, LIGHTS, rows)
            kept = full * misc[1 + c : 2 + c]
            lift = lift + fold(kept * obs)
            energy = energy + fold(kept * full)
            flat_scr[r, part, :] = obs.astype(bf16)
            lit = obs * lobe
            for h in range(cols // LANES):
                base = lit[:, h * LANES : (h + 1) * LANES] * gain_scr[...]
                for k in range(4):
                    value = eights(base if k == 0 else base * tall_ref[k - 1, part, :])
                    peak[h, k] = value if c == 0 else peak[h, k] + value
        both = dot(plain_scr[...], flat_scr[r])
        put_rows(sums_ref, r, rows, both[0:count] + both[count : 2 * count])
        for h, k in peak:
            line = (count + k) * rows + r
            sums_ref[h, line : line + 1, :] = jnp.sum(peak[h, k], axis=0, keepdims=True)
        return lift, energy

    lift = energy = jnp.zeros((LIGHTS, LANES), f32)
    for r in range(rows):
        lift, energy = one_row(r, lift, energy)

    @pl.when(step == 0)
    def _():
        light_scr[0:LIGHTS, :] = lift
        light_scr[LIGHTS : 2 * LIGHTS, :] = energy

    @pl.when(step != 0)
    def _():
        light_scr[0:LIGHTS, :] = light_scr[0:LIGHTS, :] + lift
        light_scr[LIGHTS : 2 * LIGHTS, :] = light_scr[LIGHTS : 2 * LIGHTS, :] + energy

    @pl.when(step == parts - 1)
    def _():
        out_refs[parts - 1][8] = jnp.zeros((rows, cols), f32)
        for k in range(2):
            part = light_scr[k * LIGHTS : (k + 1) * LIGHTS, :]
            line = exact(jnp.ones((8, LANES), f32), part, ((1,), (1,)))[0:1]
            for ref in out_refs:
                ref[8, k : k + 1, 0:LIGHTS] = line

    def sums(k):
        return get_slab(sums_ref, k, rows)

    flat = [None, None, None]
    lone, rim_sum, echo_sum, turn_u, turn_v = None, None, None, None, None

    def grow(old, new):
        return new if old is None else old + new

    for c in range(cams):
        v = [cam(c, i) for i in range(3)]
        w = weights[c]
        one = w * sums(4 * c)
        lit = [w * sums(4 * c + 1 + x) for x in range(3)]
        back = 1.0 - inner(v, normal)
        bent = back * one
        lone = grow(lone, one)
        rim_sum = grow(rim_sum, back * bent)
        turn_u = grow(turn_u, bent * inner(v, by_u))
        turn_v = grow(turn_v, bent * inner(v, by_v))
        echo_sum = grow(echo_sum, inner(v, lit))
        flat = [grow(f, x) for f, x in zip(flat, lit)]
    spot = sums(count)
    spots = [sums(count + 1 + x) for x in range(3)]
    edge = p[3] * sharp
    twice = -2.0 * p[6]
    right = [
        p[2] * inner(by_u, flat) + edge * inner(by_u, spots) + twice * turn_u,
        p[2] * inner(by_v, flat) + edge * inner(by_v, spots) + twice * turn_v,
        inner(normal, flat),
        spot,
        p[3] * slope * (inner(normal, spots) - spot),
        lone,
        rim_sum,
        echo_sum,
    ]
    for s in range(parts):

        @pl.when(step == s)
        def _():
            for i in range(8):
                out_refs[s][i] = right[i]
            if s < parts - 1:
                out_refs[s][8] = jnp.zeros((rows, cols), f32)


def ring_total(terms):
    while len(terms) > 1:
        half = len(terms) // 2
        terms = [terms[k] + terms[k + half] for k in range(half)]
    return terms[0]


def solve_kernel(tile_ref, low_ref, par_ref, *refs):
    right_refs, (out_ref, sent_ref) = refs[:-2], refs[-2:]
    lower = {}
    for where, (i, j) in enumerate(ENTRIES):
        lower[j, i] = low_ref[where]
    right = [total(ref[i] for ref in right_refs) - low_ref[36 + i] for i in range(8)]
    forward = []
    for i in range(8):
        accum = right[i]
        for k in range(i):
            accum = accum - lower[i, k] * forward[k]
        forward.append(accum * lower[i, i])
    answer = [None] * 8
    for i in range(7, -1, -1):
        accum = forward[i]
        for k in range(i + 1, 8):
            accum = accum - lower[k, i] * answer[k]
        answer[i] = accum * lower[i, i]
    rows = par_ref.shape[1]
    sent_ref[...] = jnp.zeros(sent_ref.shape, f32)
    for i in range(8):
        fresh = par_ref[i] + answer[i]
        out_ref[i] = fresh
        if i < 2:
            sent_ref[i : i + 1, :] = fresh[0:1]
            sent_ref[2 + i : 3 + i, :] = fresh[rows - 1 : rows]
    sent_ref[4:6, 0:LANES] = ring_total([ref[8, 0:2, 0:LANES] for ref in right_refs])


def relay_kernel(tile_ref, sent_ref, first_ref, out_ref):
    odd = row_is_odd(tile_ref)
    out_ref[...] = sent_ref[...] + first_ref[...]
    out_ref[0:2, :] = jnp.where(odd, first_ref[0:2, :], first_ref[2:4, :])


def rows_kernel(tile_ref, par_ref, first_ref, edge_ref, *refs, last):
    light_refs, (tall_ref, near_ref, scr) = refs[:-3], refs[-3:]
    rows, cols = par_ref.shape[1:]
    place = tile_ref[0] // PLACE
    odd = row_is_odd(tile_ref)
    outer = jnp.where(jnp.logical_or(place == 0, place == last), 0.0, 1.0)
    near_ref[...] = jnp.zeros(near_ref.shape, f32)
    lane = iota((rows, LANES), 1)
    for k in range(2):
        other = outer * edge_ref[k : k + 1, :]
        scr[7:8, :] = jnp.where(odd, first_ref[2 + k : 3 + k, :], other)
        scr[8 : 8 + rows, :] = par_ref[k]
        scr[8 + rows : 9 + rows, :] = jnp.where(odd, other, first_ref[k : k + 1, :])
        tall = scr[7 : 7 + rows, :] + scr[8 : 8 + rows, :] + scr[9 : 9 + rows, :]
        tall_ref[k] = tall
        ends = jnp.where(lane == 0, tall[:, 0:1], jnp.where(lane == 1, tall[:, cols - 1 : cols], 0.0))
        near_ref[k * rows : (k + 1) * rows, :] = ends
    near_ref[2 * rows : 2 * rows + 2, :] = total(ref[4:6, 0:LANES] for ref in light_refs)


def smooth_kernel(tile_ref, par_ref, tall_ref, gain_ref, sent_ref, near_ref, *refs):
    far_refs, (out_ref, gain_out_ref) = refs[:-2], refs[-2:]
    rows, cols = par_ref.shape[1:]
    side = column_is_odd(tile_ref)
    lane = iota((rows, cols), 1)
    spill = jnp.zeros((rows, cols), f32)
    for k in range(2):
        at = slice(k * rows, (k + 1) * rows)
        tall = tall_ref[k]
        near_left, near_right = near_ref[at, 0:1], near_ref[at, 1:2]
        far_left = far_right = jnp.zeros((rows, 1), f32)
        if far_refs:
            far_left, far_right = far_refs[0][at, 0:1], far_refs[0][at, 1:2]
        before = jnp.where(side, near_right, far_right)
        after = jnp.where(side, far_left, near_left)
        left = jnp.where(lane == 0, before, pltpu.roll(tall, 1, 1))
        right = jnp.where(lane == cols - 1, after, pltpu.roll(tall, cols - 1, 1))
        out_ref[k] = 0.5 * par_ref[k] + (tall + left + right) * (0.5 / 9.0)
        spill = jnp.where(lane == k, jnp.where(side, near_left, near_right) * (0.5 / 9.0), spill)
    for k in range(2, 8):
        out_ref[k] = par_ref[k]
    if not far_refs:
        out_ref[8] = spill
    light = sent_ref[2 * rows : 2 * rows + 2, 0:LIGHTS] + near_ref[2 * rows : 2 * rows + 2, 0:LIGHTS]
    gains = gain_ref[...]
    gain_out_ref[...] = gains + (light[0:1] - gains * light[1:2]) / (light[1:2] + 1.0)


def smem():
    return pl.BlockSpec(memory_space=pltpu.SMEM)


def vmem():
    return pl.BlockSpec(memory_space=pltpu.VMEM)


def params_of():
    return pltpu.CompilerParams(vmem_limit_bytes=VMEM_BYTES)


def normal_call(par, vis, gains, tables):
    _, rows, cols = par.shape
    parts = cols // LANES
    small = [tables[n] for n in ("near", "cams", "lobe", "mixed", "tall")]
    return pl.pallas_call(
        normal_kernel,
        name="normal_factor",
        out_shape=jax.ShapeDtypeStruct((44, rows, cols), f32),
        in_specs=[vmem()] * 8,
        out_specs=vmem(),
        scratch_shapes=[
            pltpu.VMEM((parts, 48 * rows, LANES), f32),
            pltpu.VMEM((parts, 96 * rows, LANES), f32),
            pltpu.VMEM((64, 2 * CAMS * LIGHTS), bf16),
            pltpu.VMEM((LIGHTS, LANES), f32),
            pltpu.VMEM((8 * CAMS, LANES), f32),
            pltpu.VMEM((32, LANES), f32),
            pltpu.VMEM((rows, 4, 8 * LIGHTS, cols), bf16),
        ],
        compiler_params=params_of(),
    )(par, vis, gains, *small)


def sample_call(tile, own, got, gains, tables, pars, vises, mend):
    parts = len(pars)
    samples, rows, _ = own.shape
    cols = pars[0].shape[2]
    held = 2 * samples

    def full(x):
        zeros = (0,) * len(x.shape)
        return pl.BlockSpec(x.shape, lambda s, tile: zeros)

    def chip(s, tile):
        return lax.rem(tile_of(tile) // 2 + (parts - s), parts)

    outs = [jax.ShapeDtypeStruct((9, rows, cols), f32) for _ in range(parts)]
    if mend:
        outs.append(jax.ShapeDtypeStruct((8, rows, cols), f32))
    small = [gains] + [tables[n] for n in ("here", "shade", "plain", "near_tall", "slab")]
    return pl.pallas_call(
        functools.partial(sample_kernel, parts=parts, mend=mend),
        name="sample_sums",
        out_shape=outs,
        grid_spec=pltpu.PrefetchScalarGridSpec(
            num_scalar_prefetch=1,
            grid=(parts,),
            in_specs=[
                pl.BlockSpec((samples, rows, cols), lambda s, tile: (0, 0, 2 * chip(s, tile) + lax.rem(tile[0], 2))),
                pl.BlockSpec((samples, rows, cols), lambda s, tile: (0, 0, chip(s, tile))),
            ]
            + [full(x) for x in small]
            + [full(x) for x in pars]
            + [full(x) for x in vises],
            out_specs=[full(x) for x in outs],
            scratch_shapes=[
                pltpu.VMEM((8, rows, cols), f32),
                pltpu.VMEM((rows, cols), jnp.int32),
                pltpu.VMEM((cols // LANES, held * rows, LANES), f32),
                pltpu.VMEM((cols // LANES, 72 * rows, LANES), f32),
                pltpu.VMEM((cols // LANES, 32 * rows, LANES), f32),
                pltpu.VMEM((2 * LIGHTS, LANES), f32),
                pltpu.VMEM((LIGHTS, LANES), f32),
                pltpu.VMEM((2 * tables["plain"].shape[0], held), bf16),
                pltpu.VMEM((rows, held, cols), bf16),
            ],
        ),
        compiler_params=params_of(),
    )(tile, own, got, *small, *in_order(pars), *in_order(vises))


def pack_kernel(tile_ref, seen_ref, par_ref, vis_ref, send_ref, first_ref, vis_scr, sems):
    parts = sems.shape[0] - 2
    width = send_ref.shape[2] // parts
    copies = [
        pltpu.make_async_copy(vis_ref, vis_scr, sems.at[parts]),
        pltpu.make_async_copy(par_ref, first_ref.at[0:8], sems.at[parts + 1]),
    ]
    copies[0].start()
    copies[1].start()
    for z in range(parts):
        start = pl.multiple_of((2 * z + 1 - lax.rem(tile_ref[0], 2)) * width, LANES)
        copies.append(
            pltpu.make_async_copy(
                seen_ref.at[:, :, pl.ds(start, width)],
                send_ref.at[:, :, z * width : (z + 1) * width],
                sems.at[z],
            )
        )
        copies[z + 2].start()
    copies[0].wait()
    first_ref[8] = vis_scr[...].astype(f32)
    for copy in copies[1:]:
        copy.wait()


def pack_call(tile, observed, params, visible, parts):
    far = pl.BlockSpec(memory_space=pltpu.MemorySpace.HBM)
    samples, rows, width = observed.shape
    return pl.pallas_call(
        pack_kernel,
        name="pack",
        out_shape=[
            jax.ShapeDtypeStruct((samples, rows, width // 2), observed.dtype),
            jax.ShapeDtypeStruct((9,) + params.shape[1:], f32),
        ],
        in_specs=[smem(), far, far, far],
        out_specs=[far, vmem()],
        scratch_shapes=[pltpu.VMEM(visible.shape, jnp.int32), pltpu.SemaphoreType.DMA((parts + 2,))],
        compiler_params=params_of(),
    )(tile, *[pltpu.with_memory_space_constraint(x, pltpu.MemorySpace.HBM) for x in (observed, params, visible)])


def plain_call(kernel, name, shapes, scratch, tile, *args):
    return pl.pallas_call(
        kernel,
        name=name,
        out_shape=[jax.ShapeDtypeStruct(shape, f32) for shape in shapes],
        in_specs=[smem()] + [vmem()] * len(args),
        out_specs=[vmem()] * len(shapes),
        scratch_shapes=[pltpu.VMEM(shape, f32) for shape in scratch],
        compiler_params=params_of(),
    )(tile, *args)


def pairs(count, start):
    out = []
    for i in range(start, count - 1, 2):
        out += [(i, i + 1), (i + 1, i)]
    return out


def settle(tile, low, params, moved, gains, closed):
    _, rows, cols = params.shape
    grps, tiles = lax.axis_size("grp"), lax.axis_size("tile")
    strip = (8, cols)
    params, sent = plain_call(solve_kernel, "solve", [params.shape, strip], [], tile, low, params, *moved)
    first = lax.ppermute(sent, "grp", pairs(grps, 0))
    if grps == 4:
        (relay,) = plain_call(relay_kernel, "relay", [strip], [], tile, sent, first)
        edge = lax.ppermute(relay, "grp", [(i, i ^ 2) for i in range(grps)])
        lights = [relay, edge]
    else:
        second = lax.ppermute(sent, "grp", pairs(grps, 1))
        odd = lax.axis_index("grp") % 2 == 1
        edge = jnp.where(odd, second, jnp.roll(second, -2, axis=0))
        light = sent + first
        bit = 2
        while bit < grps:
            light = light + lax.ppermute(light, "grp", [(i, i ^ bit) for i in range(grps)])
            bit *= 2
        lights = [light]
    patch = (2 * rows + 8, LANES)
    tall, sent = plain_call(
        functools.partial(rows_kernel, last=grps - 1), "rows", [(2, rows, cols), patch], [(24, cols)],
        tile, params, first, edge, *lights,
    )
    ends = [lax.ppermute(sent, "tile", pairs(tiles, 1))] if closed else []
    near = lax.ppermute(sent, "tile", pairs(tiles, 0))
    slabs = 8 if closed else 9
    return plain_call(
        smooth_kernel, "smooth", [(slabs, rows, cols), gains.shape], [], tile, params, tall, gains, sent, near, *ends
    )


def exact(a, b, sides):
    return lax.dot_general(
        a, b, (sides, ((), ())), precision=lax.Precision.HIGHEST, preferred_element_type=f32
    )


def iota(shape, axis):
    return lax.broadcasted_iota(jnp.int32, shape, axis)


def pick(test):
    return jnp.where(test, 1.0, 0.0).astype(f32)


def setup_kernel(
    tile_ref, light_ref, view_ref,
    near_ref, cams_ref, lobe_ref, mixed_ref,
    here_ref, shade_ref, plain_ref, tall_ref, near_tall_ref, slab_ref, light_scr, view_scr,
):
    samples = lobe_ref.shape[0]
    held = here_ref.shape[0]
    cams = held // LIGHTS
    first = (tile_of(tile_ref) // 2) * cams

    def unit(raw_ref, scr):
        scr[...] = jnp.zeros(scr.shape, f32)
        scr[0:3, :] = raw_ref[...]
        scr[2:3, :] = scr[2:3, :] + lift_z
        lifted = scr[...]
        return lifted / jnp.sqrt(jnp.sum(lifted * lifted, axis=0, keepdims=True))

    lights = unit(light_ref, light_scr)
    views = unit(view_ref, view_scr)
    near = jnp.where(iota(lights.shape, 0) == 3, 1.0, lights)
    near_ref[...] = near
    cams_ref[...] = views

    def across(count, start, period):
        at_light = pick(iota((LIGHTS, count), 1) % LIGHTS == iota((LIGHTS, count), 0))
        at_view = pick(iota((CAMS, count), 1) // LIGHTS % period + start == iota((CAMS, count), 0))
        wide = exact(near, at_light, ((1,), (0,)))
        view = exact(views, at_view, ((1,), (0,)))
        row = iota((8, count), 0)
        raw = jnp.where(row < 3, wide + view, 0.0)
        half = raw / jnp.sqrt(jnp.sum(raw * raw, axis=0, keepdims=True))
        echo = jnp.sum(wide * view, axis=0, keepdims=True)
        return wide, half, echo

    def down(count, start):
        at_light = pick(iota((count, LIGHTS), 0) % LIGHTS == iota((count, LIGHTS), 1))
        at_view = pick(iota((count, CAMS), 0) // LIGHTS + start == iota((count, CAMS), 1))
        tall = exact(at_light, near, ((1,), (1,)))
        view = exact(at_view, views, ((1,), (1,)))
        lane = iota((count, 8), 1)
        raw = jnp.where(lane < 3, tall + view, 0.0)
        half = raw / jnp.sqrt(jnp.sum(raw * raw, axis=1, keepdims=True))
        half = jnp.where(lane == 3, 1.0, half)
        echo = jnp.sum(tall * view, axis=1, keepdims=True)
        return half, jnp.where(lane == 4, echo, tall)

    def spread(values, width, depth, order):
        lane = iota((8, depth), 1)
        out = None
        for which in range(max(order) + 1):
            head = values.astype(bf16)
            values = values - head.astype(f32)
            group = None
            for g, k in enumerate(order):
                if k == which:
                    hit = lane // width == g
                    group = hit if group is None else jnp.logical_or(group, hit)
            place = pick(jnp.logical_and(group, lane % width == iota((8, depth), 0)))
            place = jnp.where(iota((8, depth), 0) < width, place, 0.0).astype(bf16)
            got = dot(head, place)
            out = got if out is None else out + got
        return out

    wide, half, echo = across(samples, 0, CAMS)
    high = [jnp.ones((1, samples), f32)] + [half[k : k + 1] for k in range(3)]
    low = [wide[k : k + 1] for k in range(3)] + [echo]
    which = iota((1, samples), 1) // LIGHTS % 4
    for i in range(4):
        for j in range(4):
            mixed_ref[4 * i + j : 4 * i + j + 1, :] = high[i] * low[j]
            mixed_ref[16 + 4 * i + j : 17 + 4 * i + j, :] = jnp.where(which == i, high[j], 0.0)
    depth = lobe_ref.shape[1]
    half, _ = down(samples, 0)
    for k in range(3):
        tall_ref[k] = jnp.broadcast_to(half[:, k : k + 1], (samples, LANES))
    hot = pick(iota((samples, depth), 0) // LIGHTS + 24 == iota((samples, depth), 1))
    lobe_ref[...] = (spread(half, 4, depth, (0, 0, 1, 0, 1, 2)) + hot).astype(bf16)

    half, tall = down(held, first)
    for k in range(3):
        near_tall_ref[k] = jnp.broadcast_to(half[:, k : k + 1], (held, LANES))
    cam = iota((held, 32), 0) // LIGHTS
    lane = iota((held, 32), 1)
    hot = pick(cam + 24 == lane)
    here_ref[...] = (spread(half, 4, 32, (0, 0, 1, 0, 1, 2)) + hot).astype(bf16)
    hot = pick(cam + 15 == lane) + pick(cam + (15 + cams) == lane)
    shade_ref[...] = (spread(tall, 5, 32, (0, 0, 1)) + hot).astype(bf16)

    wide, _, _ = across(held, first, cams)
    plain_ref[...] = jnp.zeros(plain_ref.shape, f32)
    which = iota((1, held), 1) // LIGHTS
    for c in range(cams):
        plain_ref[4 * c : 4 * c + 1, :] = pick(which == c)
        for k in range(3):
            plain_ref[4 * c + 1 + k : 4 * c + 2 + k, :] = jnp.where(which == c, wide[k : k + 1], 0.0)
        mine = jnp.sum(jnp.where(iota(views.shape, 1) == first + c, views, 0.0), axis=1, keepdims=True)
        slab_ref[8 * c : 8 * c + 8, :] = jnp.broadcast_to(mine, (8, LANES))


TABLES = ("near", "cams", "lobe", "mixed", "here", "shade", "plain", "tall", "near_tall", "slab")


def setup_call(tile, light_directions, view_dirs, held):
    samples = CAMS * LIGHTS
    cams = held // LIGHTS
    count = max(8, 4 * cams)
    shapes = [
        ((8, LIGHTS), f32), ((8, CAMS), f32), ((samples, 48), bf16), ((32, samples), f32),
        ((held, 32), bf16), ((held, 32), bf16), ((count, held), f32),
        ((3, samples, LANES), f32), ((3, held, LANES), f32), ((8 * cams, LANES), f32),
    ]
    outs = pl.pallas_call(
        setup_kernel,
        name="tables",
        out_shape=[jax.ShapeDtypeStruct(a, b) for a, b in shapes],
        in_specs=[smem(), vmem(), vmem()],
        out_specs=[vmem()] * len(shapes),
        scratch_shapes=[pltpu.VMEM((8, LIGHTS), f32), pltpu.VMEM((8, CAMS), f32)],
        compiler_params=params_of(),
    )(tile, light_directions, view_dirs)
    return dict(zip(TABLES, outs))


def passing_order(parts):
    return ([1] + list(range(parts - 1, 1, -1)) if parts > 1 else []) + [0]


def in_order(items):
    return [items[i] for i in passing_order(len(items))]


def by_shift(items):
    order = passing_order(len(items))
    return [items[order.index(i)] for i in range(len(items))]


def shifted(x, by, nz):
    return lax.ppermute(x, "tile", [(2 * z + c, 2 * ((z + by) % nz) + c) for z in range(nz) for c in range(2)])


def on_device(observed, visible, params_start, light_directions, view_dirs, gains_start):
    samples = observed.shape[0]
    tiles = lax.axis_size("tile")
    nz = tiles // 2
    tile = lax.axis_index("tile")
    held = 2 * samples

    here = (tile + PLACE * lax.axis_index("grp")).astype(jnp.int32).reshape(1)
    send, first = pack_call(here, observed, params_start, visible, nz)
    got = lax.ppermute(send, "tile", [(i, i ^ 1) for i in range(tiles)])
    blocks = [first] + [shifted(first, s, nz) for s in range(1, nz)]
    vises = blocks
    tables = setup_call(here, light_directions, view_dirs, held)

    params = params_start
    gains = gains_start.reshape(1, LIGHTS)
    for iteration in range(ITERS):
        rights = sample_call(here, observed, got, gains, tables, blocks, vises, iteration > 0)
        if iteration > 0:
            *rights, params = rights
        low = normal_call(params, visible, gains, tables)
        moved = [rights[0]] + [shifted(rights[s], -s, nz) for s in range(1, nz)]
        closed = iteration + 1 == ITERS
        params, gains = settle(here, low, params, moved, gains, closed)
        if not closed:
            blocks = [params] + [shifted(params, s, nz) for s in range(1, nz)]
    return params, gains.reshape(LIGHTS)


def solution(mesh):
    return jax.shard_map(
        on_device,
        mesh=mesh,
        in_specs=(P("tile", "grp", None), P("grp", "tile"), P(None, "grp", "tile"), P(), P(), P()),
        out_specs=(P(None, "grp", "tile"), P()),
        check_vma=False,
    )
```

```python
import functools

import jax
import jax.numpy as jnp
from jax import lax
from jax.experimental import pallas as pl
from jax.experimental.pallas import tpu as pltpu
from jax.sharding import PartitionSpec as P

CAMS = 16
LIGHTS = 32
ITERS = 2

damping = 4.0
lift_z = 1.6
hidden = 1024.0
f32 = jnp.float32
bf16 = jnp.bfloat16
LANES = 128
VMEM_BYTES = 16 * 1024 * 1024
LINEAR = (2, 3, 5, 6, 7)
ENTRIES = [(i, j) for i in range(8) for j in range(i, 8)]


PLACE = 4096


def tile_of(ref):
    return lax.rem(ref[0], PLACE)


def row_is_odd(ref):
    return lax.rem(ref[0] // PLACE, 2) == 1


def column_is_odd(ref):
    return lax.rem(ref[0], 2) == 1


def split_value(x, count):
    pieces = []
    for _ in range(count - 1):
        head = x.astype(bf16).astype(f32)
        pieces.append(head)
        x = x - head
    pieces.append(x)
    return pieces


def split_pair(x):
    head = x.astype(bf16)
    return head, (x - head.astype(f32)).astype(bf16)


def dot(a, b):
    return jnp.dot(a, b, preferred_element_type=f32)


def total(terms):
    terms = list(terms)
    out = terms[0]
    for t in terms[1:]:
        out = out + t
    return out


def inner(a, b):
    return total(x * y for x, y in zip(a, b))


def texel_forms(p):
    tu, tv, diffuse, spec, raw, ambient, rim, retro = p
    q = 1.0 / jnp.sqrt(1.0 + tu * tu + tv * tv)
    nx, ny, nz = tu * q, tv * q, q
    side = -(nx * ny) * q
    by_u = ((1.0 - nx * nx) * q, side, -(nz * nx) * q)
    by_v = (side, (1.0 - ny * ny) * q, -(nz * ny) * q)
    sigma = 1.0 / (1.0 + jnp.exp(-raw))
    sharp = 1.0 + 20.0 * sigma
    slope = 20.0 * sigma * (1.0 - sigma)
    return (nx, ny, nz), by_u, by_v, sharp, slope


def seen(mask, c):
    return jnp.bitwise_and(jnp.right_shift(mask, c), 1).astype(f32)


def put_slab(ref, k, value):
    rows, cols = value.shape
    for h in range(cols // LANES):
        ref[h, k * rows : (k + 1) * rows, :] = value[:, h * LANES : (h + 1) * LANES]


def get_slab(ref, k, rows):
    return jnp.concatenate([ref[h, k * rows : (k + 1) * rows, :] for h in range(ref.shape[0])], axis=1)


def get_rows(ref, start, count, stride):
    return jnp.concatenate([ref[h, pl.ds(start, count, stride=stride), :] for h in range(ref.shape[0])], axis=1)


def put_rows(ref, start, stride, value):
    count, cols = value.shape
    for h in range(cols // LANES):
        ref[h, pl.ds(start, count, stride=stride), :] = value[:, h * LANES : (h + 1) * LANES]


def gain_columns(gains):
    same = pick(iota((LIGHTS, LIGHTS), 0) == iota((LIGHTS, LIGHTS), 1))
    tall = exact(same, jnp.broadcast_to(gains, (8, LIGHTS)), ((1,), (1,)))
    return jnp.broadcast_to(tall[:, 0:1], (LIGHTS, LANES))


def eights(x):
    return total(x[i : i + 8] for i in range(0, x.shape[0], 8))


def put_lobe_rows(slab, normal, sharp):
    base = [sharp * normal[0], sharp * normal[1], sharp * normal[2], -sharp]
    parts = [split_value(x, 3) for x in base]
    row = 0
    for which in (0, 1, 0, 2, 1, 0):
        for part in parts:
            slab(row, part[which])
            row += 1
    return row


def normal_kernel(
    par_ref, vis_ref, gain_ref, near_ref, cams_ref, lobe_ref, mixed_ref, tall_ref, out_ref,
    rows_ref, sums_ref, mixed_scr, gain_scr, cam_scr, gram_scr, lobe_scr,
):
    rows, cols = par_ref.shape[1], par_ref.shape[2]
    depth = lobe_ref.shape[1]
    chunk = 4 * LIGHTS
    chunks = CAMS // 4

    near, views = near_ref[...], cams_ref[...]
    gain2 = gain_ref[...] * gain_ref[...]
    grams = [jnp.sum(near * near[i : i + 1] * gain2, axis=1, keepdims=True) for i in range(4)]
    for i in range(4):
        gram_scr[8 * i : 8 * i + 8, :] = jnp.broadcast_to(grams[i], (8, LANES))
    spread = [total(grams[i][k : k + 1] * views[k : k + 1] for k in range(3)) for i in range(4)]
    echo_sq = total(spread[k] * views[k : k + 1] for k in range(3))
    row = iota(views.shape, 0)
    full = jnp.where(row == 3, echo_sq, jnp.where(row == 4, spread[3], views))
    for c in range(CAMS):
        cam_scr[8 * c : 8 * c + 8, :] = jnp.broadcast_to(full[:, c : c + 1], (8, LANES))

    gain_scr[...] = gain_columns(gain2)
    across = CAMS * LIGHTS
    at_light = pick(iota((LIGHTS, across), 1) % LIGHTS == iota((LIGHTS, across), 0))
    gain2 = exact(jnp.broadcast_to(gain2, (8, LIGHTS)), at_light, ((1,), (0,)))[0:1]
    for src, dst in ((mixed_ref, mixed_scr),):
        head, tail = split_pair(src[...] * gain2)
        count = src.shape[0]
        for ch in range(chunks):
            part = slice(ch * chunk, (ch + 1) * chunk)
            first = slice(2 * ch * chunk, (2 * ch + 1) * chunk)
            second = slice((2 * ch + 1) * chunk, (2 * ch + 2) * chunk)
            dst[0:count, first] = head[:, part]
            dst[0:count, second] = head[:, part]
            dst[count : 2 * count, first] = tail[:, part]
            dst[count : 2 * count, second] = jnp.zeros((count, chunk), bf16)

    def slab(k, value):
        put_slab(rows_ref, k, value)

    p = [par_ref[i] for i in range(8)]
    normal, _, _, sharp, _ = texel_forms(p)
    used = put_lobe_rows(slab, normal, sharp)
    mask = vis_ref[...]
    for c in range(CAMS):
        slab(used + c, (seen(mask, c) - 1.0) * hidden)
    for k in range(used + CAMS, depth):
        slab(k, jnp.zeros((rows, cols), f32))

    quads = [(i, j) for i in range(4) for j in range(i, 4)]

    def one_row(r):
        texel = get_rows(rows_ref, r, depth, rows).astype(bf16)
        mixed = jnp.zeros((16, cols), f32)
        bent = {(h, ij): None for h in range(cols // LANES) for ij in quads}
        for ch in range(chunks):
            for c in range(4):
                part = slice(ch * chunk + c * LIGHTS, ch * chunk + (c + 1) * LIGHTS)
                lobe = jnp.exp(dot(lobe_ref[part, :], texel))
                head, tail = split_pair(lobe)
                lobe_scr[r, ch, c * LIGHTS : (c + 1) * LIGHTS, :] = head
                lobe_scr[r, ch, chunk + c * LIGHTS : chunk + (c + 1) * LIGHTS, :] = tail
                tall = [None] + [tall_ref[k, part, :] for k in range(3)]
                for h in range(cols // LANES):
                    lobe_h = lobe[:, h * LANES : (h + 1) * LANES]
                    single = [lobe_h * lobe_h * gain_scr[...]]
                    single += [single[0] * tall[k] for k in (1, 2, 3)]
                    for i, j in quads:
                        value = eights(single[j] if i == 0 else single[i] * tall[j])
                        old = bent[h, (i, j)]
                        bent[h, (i, j)] = value if old is None else old + value
            at = slice(2 * ch * chunk, (2 * ch + 2) * chunk)
            both = dot(mixed_scr[:, at], lobe_scr[r, ch])
            got = both[0:32] + both[32:64]
            mixed = mixed + got[0:16]
            put_rows(sums_ref, (32 + 16 * ch) * rows + r, rows, got[16:32])
        put_rows(sums_ref, r, rows, mixed)
        for h in range(cols // LANES):
            for k, ij in enumerate(quads):
                line = (16 + k) * rows + r
                sums_ref[h, line : line + 1, :] = jnp.sum(bent[h, ij], axis=0, keepdims=True)

    for r in range(rows):
        one_row(r)

    def one_part(h, carry):
        at = pl.ds(pl.multiple_of(h * LANES, LANES), LANES)

        def cam(c, i):
            return cam_scr[8 * c + i : 8 * c + i + 1, :]

        def sums(k):
            return sums_ref[h, k * rows : (k + 1) * rows, :]

        p = [par_ref[i, :, at] for i in range(8)]
        mask = vis_ref[:, at]
        normal, by_u, by_v, sharp, slope = texel_forms(p)
        diffuse, spec, rim = p[2], p[3], p[6]
        zero = jnp.zeros((rows, LANES), f32)
        gam = {i: zero for i in (0, 1, 5, 6)}
        own = {(i, j): zero for i in (0, 1, 5, 6) for j in (0, 1, 5, 6) if i <= j and j != 5 and i != 5}
        lit = {i: zero for i in (0, 1, 5, 6)}
        grid = {(i, k): zero for i in (0, 1, 5, 6) for k in range(4)}
        echo_sq = zero
        view_sum = [zero, zero, zero]
        for c in range(CAMS):
            w = seen(mask, c)
            v = [cam(c, i) for i in range(3)]
            back = 1.0 - inner(v, normal)
            turn = (-2.0 * rim) * back
            shape = {0: turn * inner(v, by_u), 1: turn * inner(v, by_v), 6: back * back}
            weighted = {i: w * shape[i] for i in shape}
            weighted[5] = w
            for i in gam:
                gam[i] = gam[i] + weighted[i]
                lit[i] = lit[i] + weighted[i] * cam(c, 4)
            for i, j in own:
                own[i, j] = own[i, j] + weighted[i] * shape[j]
            echo_sq = echo_sq + w * cam(c, 3)
            view_sum = [s + w * x for s, x in zip(view_sum, v)]
            for k in range(4):
                peak = sums(32 + 4 * c + k)
                for i in (0, 1, 6):
                    grid[i, k] = grid[i, k] + shape[i] * peak
                grid[5, k] = grid[5, k] + peak
        own[5, 5] = gam[5]
        for i in (0, 1):
            own[i, 5] = gam[i]
        own[5, 6] = gam[6]

        def gram(i, j):
            return gram_scr[8 * i + j : 8 * i + j + 1, :]

        entries = {ij: None for ij in ENTRIES}

        def add(i, j, value):
            ij = (min(i, j), max(i, j))
            entries[ij] = value if entries[ij] is None else entries[ij] + value

        def cross(i, j, value):
            add(i, j, value + value if i == j else value)

        flat = {0: [diffuse * x for x in by_u], 1: [diffuse * x for x in by_v], 2: list(normal)}
        edge = spec * sharp
        tilt = spec * slope
        glow = {
            0: {1 + k: edge * by_u[k] for k in range(3)},
            1: {1 + k: edge * by_v[k] for k in range(3)},
            3: {0: None},
            4: {0: -tilt, 1: tilt * normal[0], 2: tilt * normal[1], 3: tilt * normal[2]},
        }

        def combine(coefs, values):
            return total(values[k] if x is None else x * values[k] for k, x in coefs.items())

        count = gam[5]
        spread = {i: [total(gram(r, k) * flat[i][k] for k in range(3)) for r in range(3)] for i in flat}
        reach = {i: total(gram(3, k) * flat[i][k] for k in range(3)) for i in flat}
        view_spread = [total(gram(r, k) * view_sum[k] for k in range(3)) for r in range(3)]
        for i in flat:
            for j in flat:
                if i <= j:
                    add(i, j, count * inner(flat[j], spread[i]))
            for j in gam:
                cross(i, j, reach[i] * gam[j])
            cross(i, 7, inner(flat[i], view_spread))
        for i, j in own:
            add(i, j, gram(3, 3) * own[i, j])
        for i in lit:
            cross(i, 7, lit[i])
        add(7, 7, echo_sq)
        for j in glow:
            for i in flat:
                cross(i, j, total(flat[i][x] * combine(glow[j], {k: sums(4 * k + x) for k in glow[j]}) for x in range(3)))
            for i in gam:
                cross(i, j, combine(glow[j], {k: grid[i, k] for k in glow[j]}))
            cross(j, 7, combine(glow[j], {k: sums(4 * k + 3) for k in glow[j]}))
        packed = {}
        where = 0
        for i in range(4):
            for j in range(i, 4):
                packed[i, j] = packed[j, i] = where
                where += 1
        for i in glow:
            for j in glow:
                if i <= j:
                    half = {k: combine(glow[j], {x: sums(16 + packed[k, x]) for x in glow[j]}) for k in glow[i]}
                    add(i, j, combine(glow[i], half))

        def entry(i, j):
            return entries[min(i, j), max(i, j)]

        for i in range(8):
            out_ref[36 + i, :, at] = total(entry(i, j) * p[j] for j in LINEAR)
        lower = {}
        for j in range(8):
            accum = entries[j, j] + damping
            for k in range(j):
                accum = accum - lower[j, k] * lower[j, k]
            inverse = lax.rsqrt(accum)
            lower[j, j] = inverse
            for i in range(j + 1, 8):
                accum = entries[j, i]
                for k in range(j):
                    accum = accum - lower[i, k] * lower[j, k]
                lower[i, j] = accum * inverse
        for where, (i, j) in enumerate(ENTRIES):
            out_ref[where, :, at] = lower[j, i]
        return carry

    lax.fori_loop(0, cols // LANES, one_part, 0, unroll=2)


def sample_kernel(
    tile_ref, own_ref, got_ref, gain_ref, lobe_ref, shade_ref, plain_ref, tall_ref, slab_ref, *refs, parts, mend
):
    par_refs, vis_refs = by_shift(refs[:parts]), by_shift(refs[parts : 2 * parts])
    out_refs = refs[2 * parts : 3 * parts]
    extra = 1 if mend else 0
    own_out_refs = refs[3 * parts : 3 * parts + extra]
    par_scr, vis_scr, obs_scr, rows_ref, sums_ref, light_scr, gain_scr, plain_scr, flat_scr = refs[3 * parts + extra :]
    step = pl.program_id(0)
    samples, rows, cols = own_ref.shape
    held = 2 * samples
    cams = held // LIGHTS
    for s in range(parts):

        @pl.when(step == s)
        def _():
            if not mend:
                par_scr[...] = par_refs[s][0:8]
            else:
                wide = cols // LANES
                for i in range(8 * wide):
                    h = i % wide
                    par_scr[i // wide, :, h * LANES : (h + 1) * LANES] = par_refs[s][i]
                side = column_is_odd(tile_ref)
                chip = lax.rem(tile_of(tile_ref) // 2 + (parts - s), parts)
                inside = jnp.where(side, chip, parts - 1 - chip) < parts - 1
                lane = iota((rows, cols), 1)
                hit = jnp.logical_and(lane == jnp.where(side, cols - 1, 0), inside)
                lower, upper = par_refs[(s + 1) % parts], par_refs[(s - 1) % parts]
                for k in range(2):
                    end = jnp.where(side, upper[8 * wide, :, k : k + 1], lower[8 * wide, :, k : k + 1])
                    par_scr[k] = par_scr[k] + jnp.where(hit, end, 0.0)
                if s == 0:
                    own_out_refs[0][...] = par_scr[...]
            vis_scr[...] = vis_refs[s][8].astype(jnp.int32)

    core = tile_of(tile_ref) % 2
    mine = pl.multiple_of(core * (samples * rows), rows)
    theirs = pl.multiple_of((1 - core) * (samples * rows), rows)
    for h in range(cols // LANES):
        lanes = slice(h * LANES, (h + 1) * LANES)
        for src, at in ((own_ref, mine), (got_ref, theirs)):
            obs_scr[h, pl.ds(at, samples * rows), :] = src[:, :, lanes].astype(f32).reshape(samples * rows, LANES)

    def slab(k, value):
        put_slab(rows_ref, k, value)

    p = [par_scr[i] for i in range(8)]
    mask = vis_scr[...]
    normal, by_u, by_v, sharp, slope = texel_forms(p)
    base = (tile_of(tile_ref) // 2) * cams

    def cam(c, i):
        return slab_ref[8 * c + i : 8 * c + i + 1, :][:, 0:1]

    used = put_lobe_rows(slab, normal, sharp)
    weights = [seen(mask, base + c) for c in range(cams)]
    for c in range(cams):
        slab(used + c, (weights[c] - 1.0) * hidden)
        slab(65 + c, weights[c])
    for k in range(used + cams, 32):
        slab(k, jnp.zeros((rows, cols), f32))
    shade = [p[2] * normal[0], p[2] * normal[1], p[2] * normal[2], p[5], p[7]]
    pieces = [split_value(x, 2) for x in shade]
    at = 32
    for which in (0, 1, 0):
        for piece in pieces:
            slab(at, piece[which])
            at += 1
    for c in range(cams):
        back = 1.0 - inner([cam(c, i) for i in range(3)], normal)
        head, tail = split_value(p[6] * (back * back), 2)
        slab(at + c, head)
        slab(at + cams + c, tail)
    for k in range(at + 2 * cams, 64):
        slab(k, jnp.zeros((rows, cols), f32))
    slab(64, p[3])

    @pl.when(step == 0)
    def _():
        at_light = pick(iota((LIGHTS, held), 1) % LIGHTS == iota((LIGHTS, held), 0))
        gains = exact(jnp.broadcast_to(gain_ref[...], (8, LIGHTS)), at_light, ((1,), (0,)))[0:1]
        plain_scr[...] = jnp.concatenate(split_value(plain_ref[...] * gains, 2), axis=0).astype(bf16)
        gain_scr[...] = gain_columns(gain_ref[...])

    count = plain_ref.shape[0]

    def fold(x):
        return total(x[:, k * LANES : (k + 1) * LANES] for k in range(cols // LANES))

    def one_row(r, lift, energy):
        texel = get_rows(rows_ref, r, 32, rows).astype(bf16)
        tint = get_rows(rows_ref, 32 * rows + r, 32, rows).astype(bf16)
        misc = get_rows(rows_ref, 64 * rows + r, 8, rows)
        peak = {}
        for c in range(cams):
            part = slice(c * LIGHTS, (c + 1) * LIGHTS)
            lobe = jnp.exp(dot(lobe_ref[part, :], texel))
            full = dot(shade_ref[part, :], tint) + misc[0:1] * lobe
            obs = get_rows(obs_scr, c * LIGHTS * rows + r, LIGHTS, rows)
            kept = full * misc[1 + c : 2 + c]
            lift = lift + fold(kept * obs)
            energy = energy + fold(kept * full)
            flat_scr[r, part, :] = obs.astype(bf16)
            lit = obs * lobe
            for h in range(cols // LANES):
                base = lit[:, h * LANES : (h + 1) * LANES] * gain_scr[...]
                for k in range(4):
                    value = eights(base if k == 0 else base * tall_ref[k - 1, part, :])
                    peak[h, k] = value if c == 0 else peak[h, k] + value
        both = dot(plain_scr[...], flat_scr[r])
        put_rows(sums_ref, r, rows, both[0:count] + both[count : 2 * count])
        for h, k in peak:
            line = (count + k) * rows + r
            sums_ref[h, line : line + 1, :] = jnp.sum(peak[h, k], axis=0, keepdims=True)
        return lift, energy

    lift = energy = jnp.zeros((LIGHTS, LANES), f32)
    for r in range(rows):
        lift, energy = one_row(r, lift, energy)

    @pl.when(step == 0)
    def _():
        light_scr[0:LIGHTS, :] = lift
        light_scr[LIGHTS : 2 * LIGHTS, :] = energy

    @pl.when(step != 0)
    def _():
        light_scr[0:LIGHTS, :] = light_scr[0:LIGHTS, :] + lift
        light_scr[LIGHTS : 2 * LIGHTS, :] = light_scr[LIGHTS : 2 * LIGHTS, :] + energy

    @pl.when(step == parts - 1)
    def _():
        out_refs[parts - 1][8] = jnp.zeros((rows, cols), f32)
        for k in range(2):
            part = light_scr[k * LIGHTS : (k + 1) * LIGHTS, :]
            line = exact(jnp.ones((8, LANES), f32), part, ((1,), (1,)))[0:1]
            for ref in out_refs:
                ref[8, k : k + 1, 0:LIGHTS] = line

    def sums(k):
        return get_slab(sums_ref, k, rows)

    flat = [None, None, None]
    lone, rim_sum, echo_sum, turn_u, turn_v = None, None, None, None, None

    def grow(old, new):
        return new if old is None else old + new

    for c in range(cams):
        v = [cam(c, i) for i in range(3)]
        w = weights[c]
        one = w * sums(4 * c)
        lit = [w * sums(4 * c + 1 + x) for x in range(3)]
        back = 1.0 - inner(v, normal)
        bent = back * one
        lone = grow(lone, one)
        rim_sum = grow(rim_sum, back * bent)
        turn_u = grow(turn_u, bent * inner(v, by_u))
        turn_v = grow(turn_v, bent * inner(v, by_v))
        echo_sum = grow(echo_sum, inner(v, lit))
        flat = [grow(f, x) for f, x in zip(flat, lit)]
    spot = sums(count)
    spots = [sums(count + 1 + x) for x in range(3)]
    edge = p[3] * sharp
    twice = -2.0 * p[6]
    right = [
        p[2] * inner(by_u, flat) + edge * inner(by_u, spots) + twice * turn_u,
        p[2] * inner(by_v, flat) + edge * inner(by_v, spots) + twice * turn_v,
        inner(normal, flat),
        spot,
        p[3] * slope * (inner(normal, spots) - spot),
        lone,
        rim_sum,
        echo_sum,
    ]
    for s in range(parts):

        @pl.when(step == s)
        def _():
            for i in range(8):
                out_refs[s][i] = right[i]
            if s < parts - 1:
                out_refs[s][8] = jnp.zeros((rows, cols), f32)


def ring_total(terms):
    while len(terms) > 1:
        half = len(terms) // 2
        terms = [terms[k] + terms[k + half] for k in range(half)]
    return terms[0]


def solve_kernel(tile_ref, low_ref, par_ref, *refs):
    right_refs, (out_ref, sent_ref) = refs[:-2], refs[-2:]
    lower = {}
    for where, (i, j) in enumerate(ENTRIES):
        lower[j, i] = low_ref[where]
    right = [total(ref[i] for ref in right_refs) - low_ref[36 + i] for i in range(8)]
    forward = []
    for i in range(8):
        accum = right[i]
        for k in range(i):
            accum = accum - lower[i, k] * forward[k]
        forward.append(accum * lower[i, i])
    answer = [None] * 8
    for i in range(7, -1, -1):
        accum = forward[i]
        for k in range(i + 1, 8):
            accum = accum - lower[k, i] * answer[k]
        answer[i] = accum * lower[i, i]
    rows = par_ref.shape[1]
    sent_ref[...] = jnp.zeros(sent_ref.shape, f32)
    for i in range(8):
        fresh = par_ref[i] + answer[i]
        out_ref[i] = fresh
        if i < 2:
            sent_ref[i : i + 1, :] = fresh[0:1]
            sent_ref[2 + i : 3 + i, :] = fresh[rows - 1 : rows]
    sent_ref[4:6, 0:LANES] = ring_total([ref[8, 0:2, 0:LANES] for ref in right_refs])


def relay_kernel(tile_ref, sent_ref, first_ref, out_ref):
    odd = row_is_odd(tile_ref)
    out_ref[...] = sent_ref[...] + first_ref[...]
    out_ref[0:2, :] = jnp.where(odd, first_ref[0:2, :], first_ref[2:4, :])


def rows_kernel(tile_ref, par_ref, first_ref, edge_ref, *refs, last):
    light_refs, (tall_ref, near_ref, scr) = refs[:-3], refs[-3:]
    rows, cols = par_ref.shape[1:]
    place = tile_ref[0] // PLACE
    odd = row_is_odd(tile_ref)
    outer = jnp.where(jnp.logical_or(place == 0, place == last), 0.0, 1.0)
    near_ref[...] = jnp.zeros(near_ref.shape, f32)
    lane = iota((rows, LANES), 1)
    for k in range(2):
        other = outer * edge_ref[k : k + 1, :]
        scr[7:8, :] = jnp.where(odd, first_ref[2 + k : 3 + k, :], other)
        scr[8 : 8 + rows, :] = par_ref[k]
        scr[8 + rows : 9 + rows, :] = jnp.where(odd, other, first_ref[k : k + 1, :])
        tall = scr[7 : 7 + rows, :] + scr[8 : 8 + rows, :] + scr[9 : 9 + rows, :]
        tall_ref[k] = tall
        ends = jnp.where(lane == 0, tall[:, 0:1], jnp.where(lane == 1, tall[:, cols - 1 : cols], 0.0))
        near_ref[k * rows : (k + 1) * rows, :] = ends
    near_ref[2 * rows : 2 * rows + 2, :] = total(ref[4:6, 0:LANES] for ref in light_refs)


def smooth_kernel(tile_ref, par_ref, tall_ref, gain_ref, sent_ref, near_ref, *refs):
    far_refs, (out_ref, gain_out_ref) = refs[:-2], refs[-2:]
    rows, cols = par_ref.shape[1:]
    side = column_is_odd(tile_ref)
    lane = iota((rows, cols), 1)
    spill = jnp.zeros((rows, cols), f32)

    def give(k, value):
        if far_refs:
            out_ref[k] = value
        else:
            for h in range(cols // LANES):
                out_ref[k * (cols // LANES) + h] = value[:, h * LANES : (h + 1) * LANES]

    for k in range(2):
        at = slice(k * rows, (k + 1) * rows)
        tall = tall_ref[k]
        near_left, near_right = near_ref[at, 0:1], near_ref[at, 1:2]
        far_left = far_right = jnp.zeros((rows, 1), f32)
        if far_refs:
            far_left, far_right = far_refs[0][at, 0:1], far_refs[0][at, 1:2]
        before = jnp.where(side, near_right, far_right)
        after = jnp.where(side, far_left, near_left)
        left = jnp.where(lane == 0, before, pltpu.roll(tall, 1, 1))
        right = jnp.where(lane == cols - 1, after, pltpu.roll(tall, cols - 1, 1))
        give(k, 0.5 * par_ref[k] + (tall + left + right) * (0.5 / 9.0))
        spill = jnp.where(lane == k, jnp.where(side, near_left, near_right) * (0.5 / 9.0), spill)
    for k in range(2, 8):
        give(k, par_ref[k])
    if not far_refs:
        out_ref[8 * (cols // LANES)] = spill[:, 0:LANES]
    light = sent_ref[2 * rows : 2 * rows + 2, 0:LIGHTS] + near_ref[2 * rows : 2 * rows + 2, 0:LIGHTS]
    gains = gain_ref[...]
    gain_out_ref[...] = gains + (light[0:1] - gains * light[1:2]) / (light[1:2] + 1.0)


def smem():
    return pl.BlockSpec(memory_space=pltpu.SMEM)


def vmem():
    return pl.BlockSpec(memory_space=pltpu.VMEM)


def params_of():
    return pltpu.CompilerParams(vmem_limit_bytes=VMEM_BYTES)


def normal_call(par, vis, gains, tables):
    _, rows, cols = par.shape
    parts = cols // LANES
    small = [tables[n] for n in ("near", "cams", "lobe", "mixed", "tall")]
    return pl.pallas_call(
        normal_kernel,
        name="normal_factor",
        out_shape=jax.ShapeDtypeStruct((44, rows, cols), f32),
        in_specs=[vmem()] * 8,
        out_specs=vmem(),
        scratch_shapes=[
            pltpu.VMEM((parts, 48 * rows, LANES), f32),
            pltpu.VMEM((parts, 96 * rows, LANES), f32),
            pltpu.VMEM((64, 2 * CAMS * LIGHTS), bf16),
            pltpu.VMEM((LIGHTS, LANES), f32),
            pltpu.VMEM((8 * CAMS, LANES), f32),
            pltpu.VMEM((32, LANES), f32),
            pltpu.VMEM((rows, 4, 8 * LIGHTS, cols), bf16),
        ],
        compiler_params=params_of(),
    )(par, vis, gains, *small)


def sample_call(tile, own, got, gains, tables, pars, vises, mend):
    parts = len(pars)
    samples, rows, _ = own.shape
    cols = vises[0].shape[2]
    held = 2 * samples

    def full(x):
        zeros = (0,) * len(x.shape)
        return pl.BlockSpec(x.shape, lambda s, tile: zeros)

    def chip(s, tile):
        return lax.rem(tile_of(tile) // 2 + (parts - s), parts)

    outs = [jax.ShapeDtypeStruct((9, rows, cols), f32) for _ in range(parts)]
    if mend:
        outs.append(jax.ShapeDtypeStruct((8, rows, cols), f32))
    small = [gains] + [tables[n] for n in ("here", "shade", "plain", "near_tall", "slab")]
    return pl.pallas_call(
        functools.partial(sample_kernel, parts=parts, mend=mend),
        name="sample_sums",
        out_shape=outs,
        grid_spec=pltpu.PrefetchScalarGridSpec(
            num_scalar_prefetch=1,
            grid=(parts,),
            in_specs=[
                pl.BlockSpec((samples, rows, cols), lambda s, tile: (0, 0, 2 * chip(s, tile) + lax.rem(tile[0], 2))),
                pl.BlockSpec((samples, rows, cols), lambda s, tile: (0, 0, chip(s, tile))),
            ]
            + [full(x) for x in small]
            + [full(x) for x in pars]
            + [full(x) for x in vises],
            out_specs=[full(x) for x in outs],
            scratch_shapes=[
                pltpu.VMEM((8, rows, cols), f32),
                pltpu.VMEM((rows, cols), jnp.int32),
                pltpu.VMEM((cols // LANES, held * rows, LANES), f32),
                pltpu.VMEM((cols // LANES, 72 * rows, LANES), f32),
                pltpu.VMEM((cols // LANES, 32 * rows, LANES), f32),
                pltpu.VMEM((2 * LIGHTS, LANES), f32),
                pltpu.VMEM((LIGHTS, LANES), f32),
                pltpu.VMEM((2 * tables["plain"].shape[0], held), bf16),
                pltpu.VMEM((rows, held, cols), bf16),
            ],
        ),
        compiler_params=params_of(),
    )(tile, own, got, *small, *in_order(pars), *in_order(vises))


def pack_kernel(tile_ref, seen_ref, par_ref, vis_ref, send_ref, first_ref, vis_scr, sems):
    parts = sems.shape[0] - 2
    width = send_ref.shape[2] // parts
    copies = [
        pltpu.make_async_copy(vis_ref, vis_scr, sems.at[parts]),
        pltpu.make_async_copy(par_ref, first_ref.at[0:8], sems.at[parts + 1]),
    ]
    copies[0].start()
    copies[1].start()
    for z in range(parts):
        start = pl.multiple_of((2 * z + 1 - lax.rem(tile_ref[0], 2)) * width, LANES)
        copies.append(
            pltpu.make_async_copy(
                seen_ref.at[:, :, pl.ds(start, width)],
                send_ref.at[:, :, z * width : (z + 1) * width],
                sems.at[z],
            )
        )
        copies[z + 2].start()
    copies[0].wait()
    first_ref[8] = vis_scr[...].astype(f32)
    for copy in copies[1:]:
        copy.wait()


def pack_call(tile, observed, params, visible, parts):
    far = pl.BlockSpec(memory_space=pltpu.MemorySpace.HBM)
    samples, rows, width = observed.shape
    return pl.pallas_call(
        pack_kernel,
        name="pack",
        out_shape=[
            jax.ShapeDtypeStruct((samples, rows, width // 2), observed.dtype),
            jax.ShapeDtypeStruct((9,) + params.shape[1:], f32),
        ],
        in_specs=[smem(), far, far, far],
        out_specs=[far, vmem()],
        scratch_shapes=[pltpu.VMEM(visible.shape, jnp.int32), pltpu.SemaphoreType.DMA((parts + 2,))],
        compiler_params=params_of(),
    )(tile, *[pltpu.with_memory_space_constraint(x, pltpu.MemorySpace.HBM) for x in (observed, params, visible)])


def plain_call(kernel, name, shapes, scratch, tile, *args):
    return pl.pallas_call(
        kernel,
        name=name,
        out_shape=[jax.ShapeDtypeStruct(shape, f32) for shape in shapes],
        in_specs=[smem()] + [vmem()] * len(args),
        out_specs=[vmem()] * len(shapes),
        scratch_shapes=[pltpu.VMEM(shape, f32) for shape in scratch],
        compiler_params=params_of(),
    )(tile, *args)


def pairs(count, start):
    out = []
    for i in range(start, count - 1, 2):
        out += [(i, i + 1), (i + 1, i)]
    return out


def settle(tile, low, params, moved, gains, closed):
    _, rows, cols = params.shape
    grps, tiles = lax.axis_size("grp"), lax.axis_size("tile")
    strip = (8, cols)
    params, sent = plain_call(solve_kernel, "solve", [params.shape, strip], [], tile, low, params, *moved)
    first = lax.ppermute(sent, "grp", pairs(grps, 0))
    if grps == 4:
        (relay,) = plain_call(relay_kernel, "relay", [strip], [], tile, sent, first)
        edge = lax.ppermute(relay, "grp", [(i, i ^ 2) for i in range(grps)])
        lights = [relay, edge]
    else:
        second = lax.ppermute(sent, "grp", pairs(grps, 1))
        odd = lax.axis_index("grp") % 2 == 1
        edge = jnp.where(odd, second, jnp.roll(second, -2, axis=0))
        light = sent + first
        bit = 2
        while bit < grps:
            light = light + lax.ppermute(light, "grp", [(i, i ^ bit) for i in range(grps)])
            bit *= 2
        lights = [light]
    patch = (2 * rows + 8, LANES)
    tall, sent = plain_call(
        functools.partial(rows_kernel, last=grps - 1), "rows", [(2, rows, cols), patch], [(24, cols)],
        tile, params, first, edge, *lights,
    )
    ends = [lax.ppermute(sent, "tile", pairs(tiles, 1))] if closed else []
    near = lax.ppermute(sent, "tile", pairs(tiles, 0))
    shape = params.shape if closed else (8 * (cols // LANES) + 1, rows, LANES)
    return plain_call(
        smooth_kernel, "smooth", [shape, gains.shape], [], tile, params, tall, gains, sent, near, *ends
    )


def exact(a, b, sides):
    return lax.dot_general(
        a, b, (sides, ((), ())), precision=lax.Precision.HIGHEST, preferred_element_type=f32
    )


def iota(shape, axis):
    return lax.broadcasted_iota(jnp.int32, shape, axis)


def pick(test):
    return jnp.where(test, 1.0, 0.0).astype(f32)


def setup_kernel(
    tile_ref, light_ref, view_ref,
    near_ref, cams_ref, lobe_ref, mixed_ref,
    here_ref, shade_ref, plain_ref, tall_ref, near_tall_ref, slab_ref, light_scr, view_scr,
):
    samples = lobe_ref.shape[0]
    held = here_ref.shape[0]
    cams = held // LIGHTS
    first = (tile_of(tile_ref) // 2) * cams

    def unit(raw_ref, scr):
        scr[...] = jnp.zeros(scr.shape, f32)
        scr[0:3, :] = raw_ref[...]
        scr[2:3, :] = scr[2:3, :] + lift_z
        lifted = scr[...]
        return lifted / jnp.sqrt(jnp.sum(lifted * lifted, axis=0, keepdims=True))

    lights = unit(light_ref, light_scr)
    views = unit(view_ref, view_scr)
    near = jnp.where(iota(lights.shape, 0) == 3, 1.0, lights)
    near_ref[...] = near
    cams_ref[...] = views

    def across(count, start, period):
        at_light = pick(iota((LIGHTS, count), 1) % LIGHTS == iota((LIGHTS, count), 0))
        at_view = pick(iota((CAMS, count), 1) // LIGHTS % period + start == iota((CAMS, count), 0))
        wide = exact(near, at_light, ((1,), (0,)))
        view = exact(views, at_view, ((1,), (0,)))
        row = iota((8, count), 0)
        raw = jnp.where(row < 3, wide + view, 0.0)
        half = raw / jnp.sqrt(jnp.sum(raw * raw, axis=0, keepdims=True))
        echo = jnp.sum(wide * view, axis=0, keepdims=True)
        return wide, half, echo

    def down(count, start):
        at_light = pick(iota((count, LIGHTS), 0) % LIGHTS == iota((count, LIGHTS), 1))
        at_view = pick(iota((count, CAMS), 0) // LIGHTS + start == iota((count, CAMS), 1))
        tall = exact(at_light, near, ((1,), (1,)))
        view = exact(at_view, views, ((1,), (1,)))
        lane = iota((count, 8), 1)
        raw = jnp.where(lane < 3, tall + view, 0.0)
        half = raw / jnp.sqrt(jnp.sum(raw * raw, axis=1, keepdims=True))
        half = jnp.where(lane == 3, 1.0, half)
        echo = jnp.sum(tall * view, axis=1, keepdims=True)
        return half, jnp.where(lane == 4, echo, tall)

    def spread(values, width, depth, order):
        lane = iota((8, depth), 1)
        out = None
        for which in range(max(order) + 1):
            head = values.astype(bf16)
            values = values - head.astype(f32)
            group = None
            for g, k in enumerate(order):
                if k == which:
                    hit = lane // width == g
                    group = hit if group is None else jnp.logical_or(group, hit)
            place = pick(jnp.logical_and(group, lane % width == iota((8, depth), 0)))
            place = jnp.where(iota((8, depth), 0) < width, place, 0.0).astype(bf16)
            got = dot(head, place)
            out = got if out is None else out + got
        return out

    wide, half, echo = across(samples, 0, CAMS)
    high = [jnp.ones((1, samples), f32)] + [half[k : k + 1] for k in range(3)]
    low = [wide[k : k + 1] for k in range(3)] + [echo]
    which = iota((1, samples), 1) // LIGHTS % 4
    for i in range(4):
        for j in range(4):
            mixed_ref[4 * i + j : 4 * i + j + 1, :] = high[i] * low[j]
            mixed_ref[16 + 4 * i + j : 17 + 4 * i + j, :] = jnp.where(which == i, high[j], 0.0)
    depth = lobe_ref.shape[1]
    half, _ = down(samples, 0)
    for k in range(3):
        tall_ref[k] = jnp.broadcast_to(half[:, k : k + 1], (samples, LANES))
    hot = pick(iota((samples, depth), 0) // LIGHTS + 24 == iota((samples, depth), 1))
    lobe_ref[...] = (spread(half, 4, depth, (0, 0, 1, 0, 1, 2)) + hot).astype(bf16)

    half, tall = down(held, first)
    for k in range(3):
        near_tall_ref[k] = jnp.broadcast_to(half[:, k : k + 1], (held, LANES))
    cam = iota((held, 32), 0) // LIGHTS
    lane = iota((held, 32), 1)
    hot = pick(cam + 24 == lane)
    here_ref[...] = (spread(half, 4, 32, (0, 0, 1, 0, 1, 2)) + hot).astype(bf16)
    hot = pick(cam + 15 == lane) + pick(cam + (15 + cams) == lane)
    shade_ref[...] = (spread(tall, 5, 32, (0, 0, 1)) + hot).astype(bf16)

    wide, _, _ = across(held, first, cams)
    plain_ref[...] = jnp.zeros(plain_ref.shape, f32)
    which = iota((1, held), 1) // LIGHTS
    for c in range(cams):
        plain_ref[4 * c : 4 * c + 1, :] = pick(which == c)
        for k in range(3):
            plain_ref[4 * c + 1 + k : 4 * c + 2 + k, :] = jnp.where(which == c, wide[k : k + 1], 0.0)
        mine = jnp.sum(jnp.where(iota(views.shape, 1) == first + c, views, 0.0), axis=1, keepdims=True)
        slab_ref[8 * c : 8 * c + 8, :] = jnp.broadcast_to(mine, (8, LANES))


TABLES = ("near", "cams", "lobe", "mixed", "here", "shade", "plain", "tall", "near_tall", "slab")


def setup_call(tile, light_directions, view_dirs, held):
    samples = CAMS * LIGHTS
    cams = held // LIGHTS
    count = max(8, 4 * cams)
    shapes = [
        ((8, LIGHTS), f32), ((8, CAMS), f32), ((samples, 48), bf16), ((32, samples), f32),
        ((held, 32), bf16), ((held, 32), bf16), ((count, held), f32),
        ((3, samples, LANES), f32), ((3, held, LANES), f32), ((8 * cams, LANES), f32),
    ]
    outs = pl.pallas_call(
        setup_kernel,
        name="tables",
        out_shape=[jax.ShapeDtypeStruct(a, b) for a, b in shapes],
        in_specs=[smem(), vmem(), vmem()],
        out_specs=[vmem()] * len(shapes),
        scratch_shapes=[pltpu.VMEM((8, LIGHTS), f32), pltpu.VMEM((8, CAMS), f32)],
        compiler_params=params_of(),
    )(tile, light_directions, view_dirs)
    return dict(zip(TABLES, outs))


def passing_order(parts):
    return ([1] + list(range(parts - 1, 1, -1)) if parts > 1 else []) + [0]


def in_order(items):
    return [items[i] for i in passing_order(len(items))]


def by_shift(items):
    order = passing_order(len(items))
    return [items[order.index(i)] for i in range(len(items))]


def shifted(x, by, nz):
    return lax.ppermute(x, "tile", [(2 * z + c, 2 * ((z + by) % nz) + c) for z in range(nz) for c in range(2)])


def on_device(observed, visible, params_start, light_directions, view_dirs, gains_start):
    samples = observed.shape[0]
    tiles = lax.axis_size("tile")
    nz = tiles // 2
    tile = lax.axis_index("tile")
    held = 2 * samples

    here = (tile + PLACE * lax.axis_index("grp")).astype(jnp.int32).reshape(1)
    send, first = pack_call(here, observed, params_start, visible, nz)
    got = lax.ppermute(send, "tile", [(i, i ^ 1) for i in range(tiles)])
    blocks = [first] + [shifted(first, s, nz) for s in range(1, nz)]
    vises = blocks
    tables = setup_call(here, light_directions, view_dirs, held)

    params = params_start
    gains = gains_start.reshape(1, LIGHTS)
    for iteration in range(ITERS):
        rights = sample_call(here, observed, got, gains, tables, blocks, vises, iteration > 0)
        if iteration > 0:
            *rights, params = rights
        low = normal_call(params, visible, gains, tables)
        moved = [rights[0]] + [shifted(rights[s], -s, nz) for s in range(1, nz)]
        closed = iteration + 1 == ITERS
        params, gains = settle(here, low, params, moved, gains, closed)
        if not closed:
            blocks = [params] + [shifted(params, s, nz) for s in range(1, nz)]
    return params, gains.reshape(LIGHTS)


def solution(mesh):
    return jax.shard_map(
        on_device,
        mesh=mesh,
        in_specs=(P("tile", "grp", None), P("grp", "tile"), P(None, "grp", "tile"), P(), P(), P()),
        out_specs=(P(None, "grp", "tile"), P()),
        check_vma=False,
    )
```
